256 devices in a mesh: head: 16 (over y, x_lo, core), ctx: 16 (over x_hi, z).
Axes of the slice: x: 4 (x_hi: 2, x_lo: 2; x = x_hi * 2 + x_lo), y: 4, z: 8, core: 2. Of those that a mesh axis runs over, the one named last changes fastest.
Arguments:
- queries: bfloat16 [65536, 2048], P(('ctx', 'head')), may hold values from -6 to 6
- keys: bfloat16 [65536, 2048], P(('ctx', 'head')), may hold values from -6 to 6
- values: bfloat16 [65536, 2048], P(('ctx', 'head')), may hold values from -24 to 24
- picks: int32 [128, 2], replicated, may hold values from 0 to 127, as said below
Outputs:
- attended: bfloat16 [65536, 2048], P(('ctx', 'head'))
The draws below stay inside these ranges and needn't reach their ends.
Inputs may be any that keep to these rules, and one draw needn't show every extreme that they name: `picks`: rows 8 * c to 8 * c + 7 are the query blocks held by index c of ctx, and blocks 8 * o to 8 * o + 7 are held by index o. Among the 16 entries of one such group of rows, at most 2 name blocks held by any one index of ctx; one index o, the same for every group, is named exactly 2 times by every group.
All inputs are finite; a program needn't handle non-finite values.
Results may differ from the reference program's by a relative error of at most 0.0039.
Values may be sent and summed in bfloat16 or wider, within the bound.
A program may use at most 128 MiB of HBM per device.

```python
import jax
import jax.numpy as jnp
from jax import lax

HEADS = 16
HD = 128
BLOCK = 512
RSEL = 2
D = 2048
SEQ = 65536
NBLK = 128
LOCB = 8
CAP = 2


def draw_queries(key, part):
    base = jnp.clip(1.5 * jax.random.normal(jax.random.fold_in(key, 1), (SEQ, D)), -6.0, 6.0)
    return base.astype(jnp.bfloat16)


def draw_keys(key, part):
    base = jnp.clip(jax.random.normal(jax.random.fold_in(key, 2), (SEQ, D)), -6.0, 6.0)
    return base.astype(jnp.bfloat16)


def draw_picks(key, part):
    groups = NBLK // LOCB
    slots = LOCB * RSEL
    key_hot = jax.random.fold_in(key, 11)
    key_perm = jax.random.fold_in(key, 12)
    key_local = jax.random.fold_in(key, 13)
    hot = jax.random.randint(key_hot, (), 0, groups)
    entries = jnp.arange(groups * CAP, dtype=jnp.int32)
    owner_of = entries // CAP

    def one_group(group_key):
        rank = jax.random.permutation(jax.random.fold_in(group_key, 1), groups * CAP).astype(jnp.int32)
        score = jnp.where(owner_of == hot, entries - groups * CAP, rank)
        order = jnp.argsort(score, stable=True)
        chosen = owner_of[order][:slots]
        shuffle = jax.random.permutation(jax.random.fold_in(group_key, 2), slots)
        return chosen[shuffle]
    owners = jax.vmap(one_group)(jax.random.split(key_perm, groups))
    local = jax.random.randint(key_local, (groups, slots), 0, LOCB)
    return (owners * LOCB + local).reshape(NBLK, RSEL).astype(jnp.int32)


def block_levels(stream_key, dims, cuts, least, high):
    factor_of, own = 1.0, jax.random.fold_in(stream_key, 6)
    for position, shards_of in cuts:
        draws = jnp.exp(jax.random.uniform(jax.random.fold_in(own, position), (shards_of,), jnp.float32, least / len(cuts), high / len(cuts)))
        factor_of = factor_of * jnp.repeat(draws, dims[position] // shards_of).reshape([-1 if axis == position else 1 for axis in range(len(dims))])
    return factor_of


def normal_values(key, dims, width, reach, shards=(), kind=jnp.bfloat16):
    array = jax.random.normal(key, dims, jnp.float32) * width
    if len(shards) > 0:
        array = block_levels(key, dims, shards, -0.22, 0.18) * array
    return jnp.clip(array, min=-reach, max=reach).astype(kind)


def setup_inputs(seed: int = 0) -> dict:
    key_of = jax.random.split(jax.random.key(seed), 5)
    queries = draw_queries(jax.random.fold_in(key_of[4], 71), 0)
    keys = draw_keys(jax.random.fold_in(key_of[4], 71), 0)
    values = normal_values(key_of[2], (SEQ, D), 4.0, 24.0, ((0, 256),))
    picks = draw_picks(jax.random.fold_in(key_of[4], 71), 0)
    return {"queries": queries, "keys": keys, "values": values, "picks": picks}


def block_pair(query_block, key_block, value_block, score_scale):
    scores = jnp.einsum("qhd,khd->hqk", query_block.astype(jnp.float32), key_block.astype(jnp.float32)) * score_scale
    row_max = jnp.max(scores, axis=-1)
    exponent = jnp.exp(scores - row_max[..., None])
    row_sum = jnp.sum(exponent, axis=-1)
    weights = lax.optimization_barrier(exponent.astype(jnp.bfloat16))
    partial_out = jnp.einsum("hqk,khd->qhd", weights.astype(jnp.float32), value_block.astype(jnp.float32))
    return partial_out, row_max, row_sum


def reference(queries, keys, values, picks):
    score_scale = 1.0 / (HD ** 0.5)
    query_blocks = queries.reshape(NBLK, BLOCK, HEADS, HD)
    key_blocks = keys.reshape(NBLK, BLOCK, HEADS, HD)
    value_blocks = values.reshape(NBLK, BLOCK, HEADS, HD)

    def one_block(index):
        listed = lax.dynamic_index_in_dim(picks, index, 0, keepdims=False).astype(jnp.int32)
        block_ids = jnp.concatenate([index[None].astype(jnp.int32), listed])
        key_group = key_blocks[block_ids]
        value_group = value_blocks[block_ids]
        query_block = lax.dynamic_index_in_dim(query_blocks, index, 0, keepdims=False)

        def slot_pair(key_one, value_one):
            return block_pair(query_block, key_one, value_one, score_scale)

        outs_all, maxes_all, sums_all = jax.vmap(slot_pair)(key_group, value_group)
        overall = jnp.max(maxes_all, axis=0)
        factors = jnp.exp(maxes_all - overall[None])
        numer = jnp.sum(outs_all * jnp.transpose(factors, (0, 2, 1))[..., None], axis=0)
        denom = jnp.sum(sums_all * factors, axis=0)
        return (numer / jnp.transpose(denom, (1, 0))[..., None]).astype(jnp.bfloat16)

    result = lax.map(one_block, jnp.arange(NBLK, dtype=jnp.int32))
    return result.reshape(SEQ, HEADS * HD)
```

```python
import functools
import math

import jax
import jax.numpy as jnp
from jax import lax
from jax.experimental import pallas as pl
from jax.experimental.pallas import tpu as pltpu
from jax.sharding import PartitionSpec as P

HEADS = 16
HD = 128
BLOCK = 512
RSEL = 2


def route_tables(picks, local_blocks, ctx_count):
    slots = local_blocks * RSEL
    owners = (picks // local_blocks).reshape(ctx_count, slots)
    within = (picks % local_blocks).reshape(ctx_count, slots)
    owner_ids = jnp.arange(ctx_count, dtype=jnp.int32)
    one_hot = (owners[:, :, None] == owner_ids[None, None, :]).astype(jnp.int32)
    running = jnp.cumsum(one_hot, axis=1)
    position = jnp.sum(one_hot * running, axis=-1) - 1
    return (owners, within, position)


def slot_attention(q, k, v, scale):
    scores = lax.dot_general(
        q, k, (((1,), (1,)), ((), ())), preferred_element_type=jnp.float32
    ) * scale
    row_max = jnp.max(scores, axis=1, keepdims=True)
    exponent = jnp.exp(scores - row_max)
    row_sum = jnp.sum(exponent, axis=1, keepdims=True)
    partial = jnp.dot(
        exponent.astype(jnp.bfloat16), v, preferred_element_type=jnp.float32
    )
    return row_max, row_sum, partial


def attend_kernel(idx_ref, q_ref, kv_ref, far0_ref, far1_ref, o_ref, *, heads_here, scale):
    for h in range(heads_here):
        cols = slice(h * HD, (h + 1) * HD)
        q = q_ref[0, :, cols]
        parts = [
            slot_attention(q, kv_ref[0, 0, :, cols], kv_ref[1, 0, :, cols], scale),
            slot_attention(q, far0_ref[0, 0, :, cols], far0_ref[1, 0, :, cols], scale),
            slot_attention(q, far1_ref[0, 0, :, cols], far1_ref[1, 0, :, cols], scale),
        ]
        top = jnp.maximum(jnp.maximum(parts[0][0], parts[1][0]), parts[2][0])
        numer = None
        denom = None
        for row_max, row_sum, partial in parts:
            factor = jnp.exp(row_max - top)
            numer = partial * factor if numer is None else numer + partial * factor
            denom = row_sum * factor if denom is None else denom + row_sum * factor
        o_ref[0, :, cols] = (numer / denom).astype(o_ref.dtype)


def attend(far_index, q_blocks, kv_blocks, far_kv, scale):
    local_blocks, _, width = q_blocks.shape
    heads_here = width // HD
    kernel = functools.partial(attend_kernel, heads_here=heads_here, scale=scale)
    grid_spec = pltpu.PrefetchScalarGridSpec(
        num_scalar_prefetch=1,
        grid=(local_blocks,),
        in_specs=[
            pl.BlockSpec((1, BLOCK, width), lambda i, idx: (i, 0, 0)),
            pl.BlockSpec((2, 1, BLOCK, width), lambda i, idx: (0, i, 0, 0)),
            pl.BlockSpec((2, 1, BLOCK, width), lambda i, idx: (0, idx[i * RSEL], 0, 0)),
            pl.BlockSpec((2, 1, BLOCK, width), lambda i, idx: (0, idx[i * RSEL + 1], 0, 0)),
        ],
        out_specs=pl.BlockSpec((1, BLOCK, width), lambda i, idx: (i, 0, 0)),
    )
    flops = local_blocks * heads_here * 3 * 4 * BLOCK * BLOCK * HD
    return pl.pallas_call(
        kernel,
        out_shape=jax.ShapeDtypeStruct((local_blocks, BLOCK, width), jnp.bfloat16),
        grid_spec=grid_spec,
        cost_estimate=pl.CostEstimate(
            flops=flops,
            transcendentals=local_blocks * heads_here * 3 * BLOCK * BLOCK,
            bytes_accessed=local_blocks * BLOCK * width * 2 * 8,
        ),
    )(far_index, q_blocks, kv_blocks, far_kv, far_kv)


def local(queries, keys, values, picks):
    head_count = lax.axis_size("head")
    ctx_count = lax.axis_size("ctx")
    my_index = lax.axis_index("ctx")
    heads_here = HEADS // head_count
    width = heads_here * HD
    tok_rows = queries.shape[0]
    score_scale = 1.0 / math.sqrt(HD)
    kv_split = jnp.stack([keys, values]).reshape(2, tok_rows, HEADS, HD)
    kv_heads = lax.all_to_all(kv_split, "head", split_axis=2, concat_axis=1, tiled=True)
    q_heads = lax.all_to_all(
        queries.reshape(tok_rows, HEADS, HD), "head", split_axis=1, concat_axis=0, tiled=True
    )
    local_blocks = q_heads.shape[0] // BLOCK
    q_blocks = q_heads.reshape(local_blocks, BLOCK, width)
    kv_blocks = kv_heads.reshape(2, local_blocks, BLOCK, width)

    capacity = (local_blocks * RSEL + ctx_count - 1) // ctx_count + 1
    owners, within, position = route_tables(picks, local_blocks, ctx_count)
    mine_owner = lax.dynamic_index_in_dim(owners, my_index, 0, keepdims=False)
    mine_pos = lax.dynamic_index_in_dim(position, my_index, 0, keepdims=False)
    slot_ids = jnp.arange(capacity, dtype=jnp.int32)
    asked = (owners == my_index)[:, :, None] & (position[:, :, None] == slot_ids[None, None, :])
    wanted = jnp.sum(asked.astype(jnp.int32) * within[:, :, None], axis=1)
    far_index = (mine_owner * capacity + mine_pos).astype(jnp.int32)

    send_kv = kv_blocks[:, wanted.reshape(-1)].reshape(
        2, ctx_count, capacity, BLOCK, width
    )
    got_kv = lax.all_to_all(send_kv, "ctx", split_axis=1, concat_axis=1, tiled=True)
    far_kv = got_kv.reshape(2, ctx_count * capacity, BLOCK, width)

    result = attend(far_index, q_blocks, kv_blocks, far_kv, score_scale)
    result = result.reshape(local_blocks * BLOCK, heads_here, HD)
    restored = lax.all_to_all(result, "head", split_axis=0, concat_axis=1, tiled=True)
    return restored.reshape(tok_rows, HEADS * HD)


def solution(mesh):
    placed = (P(("ctx", "head"), None), P(("ctx", "head"), None), P(("ctx", "head"), None), P())
    return jax.shard_map(
        local, mesh=mesh, in_specs=placed, out_specs=P(("ctx", "head"), None), check_vma=False
    )
```

```python
import functools
import math

import jax
import jax.numpy as jnp
from jax import lax
from jax.experimental import pallas as pl
from jax.experimental.pallas import tpu as pltpu
from jax.sharding import PartitionSpec as P

MESH = pl.DeviceIdType.MESH

HEADS = 16
HD = 128
BLOCK = 512
RSEL = 2


def exchange_kernel(*refs, axis, axes, n, split_axis, concat_axis, count):
    srcs, dsts = refs[:count], refs[count:2 * count]
    send_sems, recv_sems = refs[2 * count], refs[2 * count + 1]
    me = lax.axis_index(axis)

    def device(peer):
        return tuple(peer if name == axis else lax.axis_index(name) for name in axes)

    barrier = pltpu.get_barrier_semaphore()
    for k in range(1, n):
        pl.semaphore_signal(barrier, inc=1, device_id=device((me + k) % n), device_id_type=MESH)
    pl.semaphore_wait(barrier, n - 1)

    def view(ref, dim, index):
        size = ref.shape[dim] // n
        where = [slice(None)] * len(ref.shape)
        where[dim] = pl.ds(index * size, size)
        return ref.at[tuple(where)]

    copies = []
    for a in range(count):
        own = pltpu.make_async_copy(
            view(srcs[a], split_axis, me), view(dsts[a], concat_axis, me), send_sems.at[a, 0]
        )
        own.start()
        copies.append(own)
        for k in range(1, n):
            peer = (me + k) % n
            copy = pltpu.make_async_remote_copy(
                src_ref=view(srcs[a], split_axis, peer),
                dst_ref=view(dsts[a], concat_axis, me),
                send_sem=send_sems.at[a, k],
                recv_sem=recv_sems.at[a, k],
                device_id=device(peer),
                device_id_type=MESH,
            )
            copy.start()
            copies.append(copy)
    for copy in copies:
        copy.wait()


def exchange(arrays, axis, axes, split_axis, concat_axis, collective_id):
    n = lax.axis_size(axis)
    count = len(arrays)
    out_shapes = []
    for x in arrays:
        shape = list(x.shape)
        shape[split_axis] //= n
        shape[concat_axis] *= n
        out_shapes.append(jax.ShapeDtypeStruct(tuple(shape), x.dtype))
    kernel = functools.partial(
        exchange_kernel, axis=axis, axes=axes, n=n, split_axis=split_axis,
        concat_axis=concat_axis, count=count,
    )
    return pl.pallas_call(
        kernel,
        out_shape=tuple(out_shapes),
        in_specs=[pl.BlockSpec(memory_space=pl.ANY)] * count,
        out_specs=tuple(pl.BlockSpec(memory_space=pl.ANY) for _ in range(count)),
        scratch_shapes=[
            pltpu.SemaphoreType.DMA((count, n)),
            pltpu.SemaphoreType.DMA((count, n)),
        ],
        compiler_params=pltpu.CompilerParams(collective_id=collective_id, has_side_effects=True),
    )(*arrays)


def route_tables(picks, local_blocks, ctx_count):
    slots = local_blocks * RSEL
    owners = (picks // local_blocks).reshape(ctx_count, slots)
    within = (picks % local_blocks).reshape(ctx_count, slots)
    owner_ids = jnp.arange(ctx_count, dtype=jnp.int32)
    one_hot = (owners[:, :, None] == owner_ids[None, None, :]).astype(jnp.int32)
    running = jnp.cumsum(one_hot, axis=1)
    position = jnp.sum(one_hot * running, axis=-1) - 1
    return (owners, within, position)


def slot_attention(q, k, v, scale):
    scores = lax.dot_general(
        q, k, (((1,), (1,)), ((), ())), preferred_element_type=jnp.float32
    ) * scale
    row_max = jnp.max(scores, axis=1, keepdims=True)
    exponent = jnp.exp(scores - row_max)
    row_sum = jnp.sum(exponent, axis=1, keepdims=True)
    partial = jnp.dot(
        exponent.astype(jnp.bfloat16), v, preferred_element_type=jnp.float32
    )
    return row_max, row_sum, partial


def attend_kernel(
    idx_ref, q_ref, k_ref, v_ref, fk0_ref, fv0_ref, fk1_ref, fv1_ref, o_ref, *, heads_here, scale
):
    for h in range(heads_here):
        cols = slice(h * HD, (h + 1) * HD)
        q = q_ref[0, :, cols]
        parts = [
            slot_attention(q, k_ref[0, :, cols], v_ref[0, :, cols], scale),
            slot_attention(q, fk0_ref[0, :, cols], fv0_ref[0, :, cols], scale),
            slot_attention(q, fk1_ref[0, :, cols], fv1_ref[0, :, cols], scale),
        ]
        top = jnp.maximum(jnp.maximum(parts[0][0], parts[1][0]), parts[2][0])
        numer = None
        denom = None
        for row_max, row_sum, partial in parts:
            factor = jnp.exp(row_max - top)
            numer = partial * factor if numer is None else numer + partial * factor
            denom = row_sum * factor if denom is None else denom + row_sum * factor
        o_ref[0, :, cols] = (numer / denom).astype(o_ref.dtype)


def attend(far_index, q_blocks, k_blocks, v_blocks, far_k, far_v, scale):
    local_blocks, _, width = q_blocks.shape
    heads_here = width // HD
    kernel = functools.partial(attend_kernel, heads_here=heads_here, scale=scale)
    grid_spec = pltpu.PrefetchScalarGridSpec(
        num_scalar_prefetch=1,
        grid=(local_blocks,),
        in_specs=[
            pl.BlockSpec((1, BLOCK, width), lambda i, idx: (i, 0, 0)),
            pl.BlockSpec((1, BLOCK, width), lambda i, idx: (i, 0, 0)),
            pl.BlockSpec((1, BLOCK, width), lambda i, idx: (i, 0, 0)),
            pl.BlockSpec((1, BLOCK, width), lambda i, idx: (idx[i * RSEL], 0, 0)),
            pl.BlockSpec((1, BLOCK, width), lambda i, idx: (idx[i * RSEL], 0, 0)),
            pl.BlockSpec((1, BLOCK, width), lambda i, idx: (idx[i * RSEL + 1], 0, 0)),
            pl.BlockSpec((1, BLOCK, width), lambda i, idx: (idx[i * RSEL + 1], 0, 0)),
        ],
        out_specs=pl.BlockSpec((1, BLOCK, width), lambda i, idx: (i, 0, 0)),
    )
    flops = local_blocks * heads_here * 3 * 4 * BLOCK * BLOCK * HD
    return pl.pallas_call(
        kernel,
        out_shape=jax.ShapeDtypeStruct((local_blocks, BLOCK, width), jnp.bfloat16),
        grid_spec=grid_spec,
        cost_estimate=pl.CostEstimate(
            flops=flops,
            transcendentals=local_blocks * heads_here * 3 * BLOCK * BLOCK,
            bytes_accessed=local_blocks * BLOCK * width * 2 * 8,
        ),
    )(far_index, q_blocks, k_blocks, v_blocks, far_k, far_v, far_k, far_v)


def local(queries, keys, values, picks, axes):
    head_count = lax.axis_size("head")
    ctx_count = lax.axis_size("ctx")
    my_index = lax.axis_index("ctx")
    heads_here = HEADS // head_count
    width = heads_here * HD
    tok_rows = queries.shape[0]
    score_scale = 1.0 / math.sqrt(HD)
    q_heads, k_heads, v_heads = exchange(
        (queries, keys, values), "head", axes, split_axis=1, concat_axis=0, collective_id=0
    )
    local_blocks = q_heads.shape[0] // BLOCK
    q_blocks = q_heads.reshape(local_blocks, BLOCK, width)
    k_blocks = k_heads.reshape(local_blocks, BLOCK, width)
    v_blocks = v_heads.reshape(local_blocks, BLOCK, width)

    capacity = (local_blocks * RSEL + ctx_count - 1) // ctx_count + 1
    owners, within, position = route_tables(picks, local_blocks, ctx_count)
    mine_owner = lax.dynamic_index_in_dim(owners, my_index, 0, keepdims=False)
    mine_pos = lax.dynamic_index_in_dim(position, my_index, 0, keepdims=False)
    slot_ids = jnp.arange(capacity, dtype=jnp.int32)
    asked = (owners == my_index)[:, :, None] & (position[:, :, None] == slot_ids[None, None, :])
    wanted = jnp.sum(asked.astype(jnp.int32) * within[:, :, None], axis=1)
    far_index = (mine_owner * capacity + mine_pos).astype(jnp.int32)

    send_k = k_blocks[wanted.reshape(-1)]
    send_v = v_blocks[wanted.reshape(-1)]
    far_k, far_v = exchange(
        (send_k, send_v), "ctx", axes, split_axis=0, concat_axis=0, collective_id=1
    )

    result = attend(far_index, q_blocks, k_blocks, v_blocks, far_k, far_v, score_scale)
    result = result.reshape(local_blocks * BLOCK, width)
    (restored,) = exchange((result,), "head", axes, split_axis=0, concat_axis=1, collective_id=2)
    return restored


def solution(mesh):
    placed = (P(("ctx", "head"), None), P(("ctx", "head"), None), P(("ctx", "head"), None), P())
    return jax.shard_map(
        functools.partial(local, axes=tuple(mesh.axis_names)), mesh=mesh, in_specs=placed, out_specs=P(("ctx", "head"), None), check_vma=False
    )
```

```python
import functools
import math

import jax
import jax.numpy as jnp
from jax import lax
from jax.experimental import pallas as pl
from jax.experimental.pallas import tpu as pltpu
from jax.sharding import PartitionSpec as P

MESH = pl.DeviceIdType.MESH

HEADS = 16
HD = 128
BLOCK = 512
RSEL = 2


def exchange_kernel(*refs, axes, jobs):
    count = len(jobs)
    srcs, dsts = refs[:count], refs[count:2 * count]
    send_sems, recv_sems = refs[2 * count], refs[2 * count + 1]

    def device(axis, peer):
        return tuple(peer if name == axis else lax.axis_index(name) for name in axes)

    barrier = pltpu.get_barrier_semaphore()
    peers = 0
    for axis in sorted({job[0] for job in jobs}):
        n = lax.axis_size(axis)
        me = lax.axis_index(axis)
        for k in range(1, n):
            pl.semaphore_signal(
                barrier, inc=1, device_id=device(axis, (me + k) % n), device_id_type=MESH
            )
        peers += n - 1
    pl.semaphore_wait(barrier, peers)

    def view(ref, dim, index, n):
        size = ref.shape[dim] // n
        where = [slice(None)] * len(ref.shape)
        where[dim] = pl.ds(index * size, size)
        return ref.at[tuple(where)]

    copies = []
    for a, (axis, split_axis, concat_axis) in enumerate(jobs):
        n = lax.axis_size(axis)
        me = lax.axis_index(axis)
        own = pltpu.make_async_copy(
            view(srcs[a], split_axis, me, n), view(dsts[a], concat_axis, me, n),
            send_sems.at[a, 0],
        )
        own.start()
        copies.append(own)
        for k in range(1, n):
            peer = (me + k) % n
            copy = pltpu.make_async_remote_copy(
                src_ref=view(srcs[a], split_axis, peer, n),
                dst_ref=view(dsts[a], concat_axis, me, n),
                send_sem=send_sems.at[a, k],
                recv_sem=recv_sems.at[a, k],
                device_id=device(axis, peer),
                device_id_type=MESH,
            )
            copy.start()
            copies.append(copy)
    for copy in copies:
        copy.wait()


def exchange(arrays, jobs, axes, collective_id):
    out_shapes = []
    for x, (axis, split_axis, concat_axis) in zip(arrays, jobs):
        n = lax.axis_size(axis)
        shape = list(x.shape)
        shape[split_axis] //= n
        shape[concat_axis] *= n
        out_shapes.append(jax.ShapeDtypeStruct(tuple(shape), x.dtype))
    widest = max(lax.axis_size(job[0]) for job in jobs)
    count = len(arrays)
    return pl.pallas_call(
        functools.partial(exchange_kernel, axes=axes, jobs=tuple(jobs)),
        out_shape=tuple(out_shapes),
        in_specs=[pl.BlockSpec(memory_space=pl.ANY)] * count,
        out_specs=tuple(pl.BlockSpec(memory_space=pl.ANY) for _ in range(count)),
        scratch_shapes=[
            pltpu.SemaphoreType.DMA((count, widest)),
            pltpu.SemaphoreType.DMA((count, widest)),
        ],
        compiler_params=pltpu.CompilerParams(collective_id=collective_id, has_side_effects=True),
    )(*arrays)


def route_tables(picks, local_blocks, ctx_count):
    slots = local_blocks * RSEL
    owners = (picks // local_blocks).reshape(ctx_count, slots)
    within = (picks % local_blocks).reshape(ctx_count, slots)
    owner_ids = jnp.arange(ctx_count, dtype=jnp.int32)
    one_hot = (owners[:, :, None] == owner_ids[None, None, :]).astype(jnp.int32)
    running = jnp.cumsum(one_hot, axis=1)
    position = jnp.sum(one_hot * running, axis=-1) - 1
    return (owners, within, position)


def slot_attention(q, k, v, scale):
    scores = lax.dot_general(
        q, k, (((1,), (1,)), ((), ())), preferred_element_type=jnp.float32
    ) * scale
    row_max = jnp.max(scores, axis=1, keepdims=True)
    exponent = jnp.exp(scores - row_max)
    row_sum = jnp.sum(exponent, axis=1, keepdims=True)
    partial = jnp.dot(
        exponent.astype(jnp.bfloat16), v, preferred_element_type=jnp.float32
    )
    return row_max, row_sum, partial


def attend_kernel(
    idx_ref, q_ref, k_ref, v_ref, fk0_ref, fv0_ref, fk1_ref, fv1_ref, o_ref, *, heads_here, scale
):
    for h in range(heads_here):
        cols = slice(h * HD, (h + 1) * HD)
        q = q_ref[0, :, cols]
        parts = [
            slot_attention(q, k_ref[0, :, cols], v_ref[0, :, cols], scale),
            slot_attention(q, fk0_ref[0, :, cols], fv0_ref[0, :, cols], scale),
            slot_attention(q, fk1_ref[0, :, cols], fv1_ref[0, :, cols], scale),
        ]
        top = jnp.maximum(jnp.maximum(parts[0][0], parts[1][0]), parts[2][0])
        numer = None
        denom = None
        for row_max, row_sum, partial in parts:
            factor = jnp.exp(row_max - top)
            numer = partial * factor if numer is None else numer + partial * factor
            denom = row_sum * factor if denom is None else denom + row_sum * factor
        o_ref[0, :, cols] = (numer / denom).astype(o_ref.dtype)


def attend(far_index, q_blocks, k_blocks, v_blocks, far_k, far_v, scale):
    local_blocks, _, width = q_blocks.shape
    heads_here = width // HD
    kernel = functools.partial(attend_kernel, heads_here=heads_here, scale=scale)
    grid_spec = pltpu.PrefetchScalarGridSpec(
        num_scalar_prefetch=1,
        grid=(local_blocks,),
        in_specs=[
            pl.BlockSpec((1, BLOCK, width), lambda i, idx: (i, 0, 0)),
            pl.BlockSpec((1, BLOCK, width), lambda i, idx: (i, 0, 0)),
            pl.BlockSpec((1, BLOCK, width), lambda i, idx: (i, 0, 0)),
            pl.BlockSpec((1, BLOCK, width), lambda i, idx: (idx[i * RSEL], 0, 0)),
            pl.BlockSpec((1, BLOCK, width), lambda i, idx: (idx[i * RSEL], 0, 0)),
            pl.BlockSpec((1, BLOCK, width), lambda i, idx: (idx[i * RSEL + 1], 0, 0)),
            pl.BlockSpec((1, BLOCK, width), lambda i, idx: (idx[i * RSEL + 1], 0, 0)),
        ],
        out_specs=pl.BlockSpec((1, BLOCK, width), lambda i, idx: (i, 0, 0)),
    )
    flops = local_blocks * heads_here * 3 * 4 * BLOCK * BLOCK * HD
    return pl.pallas_call(
        kernel,
        out_shape=jax.ShapeDtypeStruct((local_blocks, BLOCK, width), jnp.bfloat16),
        grid_spec=grid_spec,
        cost_estimate=pl.CostEstimate(
            flops=flops,
            transcendentals=local_blocks * heads_here * 3 * BLOCK * BLOCK,
            bytes_accessed=local_blocks * BLOCK * width * 2 * 8,
        ),
    )(far_index, q_blocks, k_blocks, v_blocks, far_k, far_v, far_k, far_v)


def local(queries, keys, values, picks, axes):
    head_count = lax.axis_size("head")
    ctx_count = lax.axis_size("ctx")
    my_index = lax.axis_index("ctx")
    heads_here = HEADS // head_count
    width = heads_here * HD
    tok_rows = queries.shape[0]
    score_scale = 1.0 / math.sqrt(HD)
    head_in = ("head", 1, 0)
    k_heads, v_heads = exchange((keys, values), (head_in, head_in), axes, collective_id=0)
    local_blocks = k_heads.shape[0] // BLOCK
    k_blocks = k_heads.reshape(local_blocks, BLOCK, width)
    v_blocks = v_heads.reshape(local_blocks, BLOCK, width)

    capacity = (local_blocks * RSEL + ctx_count - 1) // ctx_count + 1
    owners, within, position = route_tables(picks, local_blocks, ctx_count)
    mine_owner = lax.dynamic_index_in_dim(owners, my_index, 0, keepdims=False)
    mine_pos = lax.dynamic_index_in_dim(position, my_index, 0, keepdims=False)
    slot_ids = jnp.arange(capacity, dtype=jnp.int32)
    asked = (owners == my_index)[:, :, None] & (position[:, :, None] == slot_ids[None, None, :])
    wanted = jnp.sum(asked.astype(jnp.int32) * within[:, :, None], axis=1)
    far_index = (mine_owner * capacity + mine_pos).astype(jnp.int32)

    send_k = k_blocks[wanted.reshape(-1)]
    send_v = v_blocks[wanted.reshape(-1)]
    ctx_move = ("ctx", 0, 0)
    q_heads, far_k, far_v = exchange(
        (queries, send_k, send_v), (head_in, ctx_move, ctx_move), axes, collective_id=1
    )
    q_blocks = q_heads.reshape(local_blocks, BLOCK, width)

    result = attend(far_index, q_blocks, k_blocks, v_blocks, far_k, far_v, score_scale)
    result = result.reshape(local_blocks * BLOCK, width)
    (restored,) = exchange((result,), (("head", 0, 1),), axes, collective_id=2)
    return restored


def solution(mesh):
    placed = (P(("ctx", "head"), None), P(("ctx", "head"), None), P(("ctx", "head"), None), P())
    return jax.shard_map(
        functools.partial(local, axes=tuple(mesh.axis_names)), mesh=mesh, in_specs=placed, out_specs=P(("ctx", "head"), None), check_vma=False
    )
```

```python
import functools
import math

import jax
import jax.numpy as jnp
from jax import lax
from jax.experimental import pallas as pl
from jax.experimental.pallas import tpu as pltpu
from jax.sharding import PartitionSpec as P

MESH = pl.DeviceIdType.MESH

HEADS = 16
HD = 128
BLOCK = 512
RSEL = 2


def exchange_kernel(*refs, axes, jobs):
    count = len(jobs)
    srcs, dsts = refs[:count], refs[count:2 * count]
    send_sems, recv_sems = refs[2 * count], refs[2 * count + 1]

    def device(axis, peer):
        return tuple(peer if name == axis else lax.axis_index(name) for name in axes)

    barrier = pltpu.get_barrier_semaphore()
    peers = 0
    for axis in sorted({job[0] for job in jobs}):
        n = lax.axis_size(axis)
        me = lax.axis_index(axis)
        for k in range(1, n):
            pl.semaphore_signal(
                barrier, inc=1, device_id=device(axis, (me + k) % n), device_id_type=MESH
            )
        peers += n - 1
    pl.semaphore_wait(barrier, peers)

    def view(ref, dim, index, n):
        size = ref.shape[dim] // n
        where = [slice(None)] * len(ref.shape)
        where[dim] = pl.ds(index * size, size)
        return ref.at[tuple(where)]

    copies = []
    for a, (axis, split_axis, concat_axis) in enumerate(jobs):
        n = lax.axis_size(axis)
        me = lax.axis_index(axis)
        own = pltpu.make_async_copy(
            view(srcs[a], split_axis, me, n), view(dsts[a], concat_axis, me, n),
            send_sems.at[a, 0],
        )
        own.start()
        copies.append(own)
        for k in range(1, n):
            peer = (me + k) % n
            copy = pltpu.make_async_remote_copy(
                src_ref=view(srcs[a], split_axis, peer, n),
                dst_ref=view(dsts[a], concat_axis, me, n),
                send_sem=send_sems.at[a, k],
                recv_sem=recv_sems.at[a, k],
                device_id=device(axis, peer),
                device_id_type=MESH,
            )
            copy.start()
            copies.append(copy)
    for copy in copies:
        copy.wait()


def exchange(arrays, jobs, axes, collective_id):
    out_shapes = []
    for x, (axis, split_axis, concat_axis) in zip(arrays, jobs):
        n = lax.axis_size(axis)
        shape = list(x.shape)
        shape[split_axis] //= n
        shape[concat_axis] *= n
        out_shapes.append(jax.ShapeDtypeStruct(tuple(shape), x.dtype))
    widest = max(lax.axis_size(job[0]) for job in jobs)
    count = len(arrays)
    return pl.pallas_call(
        functools.partial(exchange_kernel, axes=axes, jobs=tuple(jobs)),
        out_shape=tuple(out_shapes),
        in_specs=[pl.BlockSpec(memory_space=pl.ANY)] * count,
        out_specs=tuple(pl.BlockSpec(memory_space=pl.ANY) for _ in range(count)),
        scratch_shapes=[
            pltpu.SemaphoreType.DMA((count, widest)),
            pltpu.SemaphoreType.DMA((count, widest)),
        ],
        compiler_params=pltpu.CompilerParams(collective_id=collective_id, has_side_effects=True),
    )(*arrays)


def route_tables(picks, local_blocks, ctx_count):
    slots = local_blocks * RSEL
    owners = (picks // local_blocks).reshape(ctx_count, slots)
    within = (picks % local_blocks).reshape(ctx_count, slots)
    owner_ids = jnp.arange(ctx_count, dtype=jnp.int32)
    one_hot = (owners[:, :, None] == owner_ids[None, None, :]).astype(jnp.int32)
    running = jnp.cumsum(one_hot, axis=1)
    position = jnp.sum(one_hot * running, axis=-1) - 1
    return (owners, within, position)


def slot_attention(q, k, v, scale):
    scores = lax.dot_general(
        q, k, (((1,), (1,)), ((), ())), preferred_element_type=jnp.float32
    ) * scale
    row_max = jnp.max(scores, axis=1, keepdims=True)
    exponent = jnp.exp(scores - row_max)
    row_sum = jnp.sum(exponent, axis=1, keepdims=True)
    partial = jnp.dot(
        exponent.astype(jnp.bfloat16), v, preferred_element_type=jnp.float32
    )
    return row_max, row_sum, partial


def attend_kernel(
    idx_ref, q_ref, k_ref, v_ref, fk_ref, fv_ref, y_ref, stage, send_sems, recv_sems,
    *, axes, heads_here, scale,
):
    n = lax.axis_size("head")
    me = lax.axis_index("head")
    local_blocks = q_ref.shape[0]
    rows = y_ref.shape[0]
    width = heads_here * HD
    per_block = BLOCK // rows

    def device(peer):
        return tuple(peer if name == "head" else lax.axis_index(name) for name in axes)

    barrier = pltpu.get_barrier_semaphore()
    for k in range(1, n):
        pl.semaphore_signal(barrier, inc=1, device_id=device((me + k) % n), device_id_type=MESH)
    pl.semaphore_wait(barrier, n - 1)

    mine = y_ref.at[:, pl.ds(me * width, width)]

    def piece(i, r):
        return stage.at[i, pl.ds(r * rows, rows), :]

    def remote(i, r, dest):
        return pltpu.make_async_remote_copy(
            src_ref=piece(i, r), dst_ref=mine,
            send_sem=send_sems.at[i * per_block + r], recv_sem=recv_sems.at[me],
            device_id=device(dest), device_id_type=MESH,
        )

    def own(i, r):
        return pltpu.make_async_copy(piece(i, r), mine, send_sems.at[i * per_block + r])

    def send(i):
        for r in range(per_block):
            dest = i * per_block + r

            @pl.when(dest == me)
            def _():
                own(i, r).start()

            @pl.when(dest != me)
            def _():
                remote(i, r, dest).start()

    def finish(i):
        for r in range(per_block):
            dest = i * per_block + r

            @pl.when(dest == me)
            def _():
                own(i, r).wait()

            @pl.when(dest != me)
            def _():
                remote(i, r, dest).wait_send()

    for i in range(local_blocks):
        for h in range(heads_here):
            cols = slice(h * HD, (h + 1) * HD)
            q = q_ref[i, :, cols]
            j0 = idx_ref[i * RSEL]
            j1 = idx_ref[i * RSEL + 1]
            parts = [
                slot_attention(q, k_ref[i, :, cols], v_ref[i, :, cols], scale),
                slot_attention(q, fk_ref[j0, :, cols], fv_ref[j0, :, cols], scale),
                slot_attention(q, fk_ref[j1, :, cols], fv_ref[j1, :, cols], scale),
            ]
            top = jnp.maximum(jnp.maximum(parts[0][0], parts[1][0]), parts[2][0])
            numer = None
            denom = None
            for row_max, row_sum, partial in parts:
                factor = jnp.exp(row_max - top)
                numer = partial * factor if numer is None else numer + partial * factor
                denom = row_sum * factor if denom is None else denom + row_sum * factor
            stage[i, :, cols] = (numer / denom).astype(stage.dtype)
        if i >= 1:
            send(i - 1)
    for i in range(local_blocks - 1):
        finish(i)
    send(local_blocks - 1)
    finish(local_blocks - 1)
    for sender in range(n):

        @pl.when(sender != me)
        def _():
            pltpu.make_async_remote_copy(
                src_ref=piece(0, 0), dst_ref=mine,
                send_sem=send_sems.at[0], recv_sem=recv_sems.at[sender],
                device_id=device(sender), device_id_type=MESH,
            ).wait_recv()


def attend(far_index, q_blocks, k_blocks, v_blocks, far_k, far_v, scale, axes, tok_rows):
    local_blocks, _, width = q_blocks.shape
    heads_here = width // HD
    n = HEADS // heads_here
    kernel = functools.partial(attend_kernel, axes=axes, heads_here=heads_here, scale=scale)
    vmem = pl.BlockSpec(memory_space=pltpu.VMEM)
    flops = local_blocks * heads_here * 3 * 4 * BLOCK * BLOCK * HD
    return pl.pallas_call(
        kernel,
        out_shape=jax.ShapeDtypeStruct((tok_rows, n * width), jnp.bfloat16),
        in_specs=[pl.BlockSpec(memory_space=pltpu.SMEM)] + [vmem] * 5,
        out_specs=pl.BlockSpec(memory_space=pl.ANY),
        scratch_shapes=[
            pltpu.VMEM((local_blocks, BLOCK, width), jnp.bfloat16),
            pltpu.SemaphoreType.DMA((local_blocks * (BLOCK // tok_rows),)),
            pltpu.SemaphoreType.DMA((n,)),
        ],
        compiler_params=pltpu.CompilerParams(
            collective_id=2, has_side_effects=True, vmem_limit_bytes=48 * 1024 * 1024
        ),
        cost_estimate=pl.CostEstimate(
            flops=flops,
            transcendentals=local_blocks * heads_here * 3 * BLOCK * BLOCK,
            bytes_accessed=local_blocks * BLOCK * width * 2 * 8,
        ),
    )(far_index, q_blocks, k_blocks, v_blocks, far_k, far_v)


def local(queries, keys, values, picks, axes):
    head_count = lax.axis_size("head")
    ctx_count = lax.axis_size("ctx")
    my_index = lax.axis_index("ctx")
    heads_here = HEADS // head_count
    width = heads_here * HD
    tok_rows = queries.shape[0]
    score_scale = 1.0 / math.sqrt(HD)
    head_in = ("head", 1, 0)
    k_heads, v_heads = exchange((keys, values), (head_in, head_in), axes, collective_id=0)
    local_blocks = k_heads.shape[0] // BLOCK
    k_blocks = k_heads.reshape(local_blocks, BLOCK, width)
    v_blocks = v_heads.reshape(local_blocks, BLOCK, width)

    capacity = (local_blocks * RSEL + ctx_count - 1) // ctx_count + 1
    owners, within, position = route_tables(picks, local_blocks, ctx_count)
    mine_owner = lax.dynamic_index_in_dim(owners, my_index, 0, keepdims=False)
    mine_pos = lax.dynamic_index_in_dim(position, my_index, 0, keepdims=False)
    slot_ids = jnp.arange(capacity, dtype=jnp.int32)
    asked = (owners == my_index)[:, :, None] & (position[:, :, None] == slot_ids[None, None, :])
    wanted = jnp.sum(asked.astype(jnp.int32) * within[:, :, None], axis=1)
    far_index = (mine_owner * capacity + mine_pos).astype(jnp.int32)

    send_k = k_blocks[wanted.reshape(-1)]
    send_v = v_blocks[wanted.reshape(-1)]
    ctx_move = ("ctx", 0, 0)
    q_heads, far_k, far_v = exchange(
        (queries, send_k, send_v), (head_in, ctx_move, ctx_move), axes, collective_id=1
    )
    q_blocks = q_heads.reshape(local_blocks, BLOCK, width)

    return attend(
        far_index, q_blocks, k_blocks, v_blocks, far_k, far_v, score_scale, axes, tok_rows
    )


def solution(mesh):
    placed = (P(("ctx", "head"), None), P(("ctx", "head"), None), P(("ctx", "head"), None), P())
    return jax.shard_map(
        functools.partial(local, axes=tuple(mesh.axis_names)), mesh=mesh, in_specs=placed, out_specs=P(("ctx", "head"), None), check_vma=False
    )
```

```python
import functools
import math

import jax
import jax.numpy as jnp
from jax import lax
from jax.experimental import pallas as pl
from jax.experimental.pallas import tpu as pltpu
from jax.sharding import PartitionSpec as P

MESH = pl.DeviceIdType.MESH

HEADS = 16
HD = 128
BLOCK = 512
RSEL = 2


def exchange_kernel(*refs, axes, jobs):
    count = len(jobs)
    srcs, dsts = refs[:count], refs[count:2 * count]
    send_sems, recv_sems = refs[2 * count], refs[2 * count + 1]

    def device(axis, peer):
        return tuple(peer if name == axis else lax.axis_index(name) for name in axes)

    barrier = pltpu.get_barrier_semaphore()
    peers = 0
    for axis in sorted({job[0] for job in jobs}):
        n = lax.axis_size(axis)
        me = lax.axis_index(axis)
        for k in range(1, n):
            pl.semaphore_signal(
                barrier, inc=1, device_id=device(axis, (me + k) % n), device_id_type=MESH
            )
        peers += n - 1
    pl.semaphore_wait(barrier, peers)

    def view(ref, dim, index, n):
        size = ref.shape[dim] // n
        where = [slice(None)] * len(ref.shape)
        where[dim] = pl.ds(index * size, size)
        return ref.at[tuple(where)]

    copies = []
    for a, (axis, split_axis, concat_axis) in enumerate(jobs):
        n = lax.axis_size(axis)
        me = lax.axis_index(axis)
        own = pltpu.make_async_copy(
            view(srcs[a], split_axis, me, n), view(dsts[a], concat_axis, me, n),
            send_sems.at[a, 0],
        )
        own.start()
        copies.append(own)
        for k in range(1, n):
            peer = (me + k) % n
            copy = pltpu.make_async_remote_copy(
                src_ref=view(srcs[a], split_axis, peer, n),
                dst_ref=view(dsts[a], concat_axis, me, n),
                send_sem=send_sems.at[a, k],
                recv_sem=recv_sems.at[a, k],
                device_id=device(axis, peer),
                device_id_type=MESH,
            )
            copy.start()
            copies.append(copy)
    for copy in copies:
        copy.wait()


def exchange(arrays, jobs, axes, collective_id):
    out_shapes = []
    for x, (axis, split_axis, concat_axis) in zip(arrays, jobs):
        n = lax.axis_size(axis)
        shape = list(x.shape)
        shape[split_axis] //= n
        shape[concat_axis] *= n
        out_shapes.append(jax.ShapeDtypeStruct(tuple(shape), x.dtype))
    widest = max(lax.axis_size(job[0]) for job in jobs)
    count = len(arrays)
    return pl.pallas_call(
        functools.partial(exchange_kernel, axes=axes, jobs=tuple(jobs)),
        out_shape=tuple(out_shapes),
        in_specs=[pl.BlockSpec(memory_space=pl.ANY)] * count,
        out_specs=tuple(pl.BlockSpec(memory_space=pl.ANY) for _ in range(count)),
        scratch_shapes=[
            pltpu.SemaphoreType.DMA((count, widest)),
            pltpu.SemaphoreType.DMA((count, widest)),
        ],
        compiler_params=pltpu.CompilerParams(collective_id=collective_id, has_side_effects=True),
    )(*arrays)


def route_tables(picks, local_blocks, ctx_count):
    slots = local_blocks * RSEL
    owners = (picks // local_blocks).reshape(ctx_count, slots)
    within = (picks % local_blocks).reshape(ctx_count, slots)
    owner_ids = jnp.arange(ctx_count, dtype=jnp.int32)
    one_hot = (owners[:, :, None] == owner_ids[None, None, :]).astype(jnp.int32)
    running = jnp.cumsum(one_hot, axis=1)
    position = jnp.sum(one_hot * running, axis=-1) - 1
    return (owners, within, position)


def slot_attention(q, k, v, scale):
    scores = lax.dot_general(
        q, k, (((1,), (1,)), ((), ())), preferred_element_type=jnp.float32
    ) * scale
    row_max = jnp.max(scores, axis=1, keepdims=True)
    exponent = jnp.exp(scores - row_max)
    row_sum = jnp.sum(exponent, axis=1, keepdims=True)
    partial = jnp.dot(
        exponent.astype(jnp.bfloat16), v, preferred_element_type=jnp.float32
    )
    return row_max, row_sum, partial


def attend_kernel(
    q_ref, k_ref, v_ref, fk_ref, fv_ref, y_ref, stage, send_sems, recv_sems,
    *, axes, heads_here, scale,
):
    n = lax.axis_size("head")
    me = lax.axis_index("head")
    i = pl.program_id(0)
    local_blocks = pl.num_programs(0)
    rows = y_ref.shape[0]
    width = heads_here * HD
    per_block = BLOCK // rows

    def device(peer):
        return tuple(peer if name == "head" else lax.axis_index(name) for name in axes)

    @pl.when(i == 0)
    def _():
        barrier = pltpu.get_barrier_semaphore()
        for k in range(1, n):
            pl.semaphore_signal(
                barrier, inc=1, device_id=device((me + k) % n), device_id_type=MESH
            )
        pl.semaphore_wait(barrier, n - 1)

    mine = y_ref.at[:, pl.ds(me * width, width)]

    def piece(b, r):
        return stage.at[b, pl.ds(r * rows, rows), :]

    def remote(b, r, dest):
        return pltpu.make_async_remote_copy(
            src_ref=piece(b, r), dst_ref=mine,
            send_sem=send_sems.at[b * per_block + r], recv_sem=recv_sems.at[me],
            device_id=device(dest), device_id_type=MESH,
        )

    def own(b, r):
        return pltpu.make_async_copy(piece(b, r), mine, send_sems.at[b * per_block + r])

    def send(b):
        for r in range(per_block):
            dest = b * per_block + r

            @pl.when(dest == me)
            def _():
                own(b, r).start()

            @pl.when(dest != me)
            def _():
                remote(b, r, dest).start()

    def finish(b):
        for r in range(per_block):
            dest = b * per_block + r

            @pl.when(dest == me)
            def _():
                own(b, r).wait()

            @pl.when(dest != me)
            def _():
                remote(b, r, dest).wait_send()

    for h in range(heads_here):
        cols = slice(h * HD, (h + 1) * HD)
        q = q_ref[0, :, cols]
        parts = [
            slot_attention(q, k_ref[0, :, cols], v_ref[0, :, cols], scale),
            slot_attention(q, fk_ref[0, :, cols], fv_ref[0, :, cols], scale),
            slot_attention(q, fk_ref[1, :, cols], fv_ref[1, :, cols], scale),
        ]
        top = jnp.maximum(jnp.maximum(parts[0][0], parts[1][0]), parts[2][0])
        numer = None
        denom = None
        for row_max, row_sum, partial in parts:
            factor = jnp.exp(row_max - top)
            numer = partial * factor if numer is None else numer + partial * factor
            denom = row_sum * factor if denom is None else denom + row_sum * factor
        stage[i, :, cols] = (numer / denom).astype(stage.dtype)

    @pl.when(i >= 1)
    def _():
        send(i - 1)

    @pl.when(i == local_blocks - 1)
    def _():
        def settle(b, carry):
            finish(b)
            return carry

        lax.fori_loop(0, local_blocks - 1, settle, 0)
        send(local_blocks - 1)
        finish(local_blocks - 1)
        for sender in range(n):

            @pl.when(sender != me)
            def _():
                pltpu.make_async_remote_copy(
                    src_ref=piece(0, 0), dst_ref=mine,
                    send_sem=send_sems.at[0], recv_sem=recv_sems.at[sender],
                    device_id=device(sender), device_id_type=MESH,
                ).wait_recv()


def attend(q_blocks, k_blocks, v_blocks, near_k, near_v, scale, axes, tok_rows):
    local_blocks, _, width = q_blocks.shape
    heads_here = width // HD
    n = HEADS // heads_here
    kernel = functools.partial(attend_kernel, axes=axes, heads_here=heads_here, scale=scale)
    one = pl.BlockSpec((1, BLOCK, width), lambda i: (i, 0, 0))
    pair = pl.BlockSpec((RSEL, BLOCK, width), lambda i: (i, 0, 0))
    flops = local_blocks * heads_here * 3 * 4 * BLOCK * BLOCK * HD
    return pl.pallas_call(
        kernel,
        out_shape=jax.ShapeDtypeStruct((tok_rows, n * width), jnp.bfloat16),
        grid=(local_blocks,),
        in_specs=[one, one, one, pair, pair],
        out_specs=pl.BlockSpec(memory_space=pl.ANY),
        scratch_shapes=[
            pltpu.VMEM((local_blocks, BLOCK, width), jnp.bfloat16),
            pltpu.SemaphoreType.DMA((local_blocks * (BLOCK // tok_rows),)),
            pltpu.SemaphoreType.DMA((n,)),
        ],
        compiler_params=pltpu.CompilerParams(collective_id=2, has_side_effects=True),
        cost_estimate=pl.CostEstimate(
            flops=flops,
            transcendentals=local_blocks * heads_here * 3 * BLOCK * BLOCK,
            bytes_accessed=local_blocks * BLOCK * width * 2 * 8,
        ),
    )(q_blocks, k_blocks, v_blocks, near_k, near_v)


def local(queries, keys, values, picks, axes):
    head_count = lax.axis_size("head")
    ctx_count = lax.axis_size("ctx")
    my_index = lax.axis_index("ctx")
    heads_here = HEADS // head_count
    width = heads_here * HD
    tok_rows = queries.shape[0]
    score_scale = 1.0 / math.sqrt(HD)
    head_in = ("head", 1, 0)
    k_heads, v_heads = exchange((keys, values), (head_in, head_in), axes, collective_id=0)
    local_blocks = k_heads.shape[0] // BLOCK
    k_blocks = k_heads.reshape(local_blocks, BLOCK, width)
    v_blocks = v_heads.reshape(local_blocks, BLOCK, width)

    capacity = (local_blocks * RSEL + ctx_count - 1) // ctx_count + 1
    owners, within, position = route_tables(picks, local_blocks, ctx_count)
    mine_owner = lax.dynamic_index_in_dim(owners, my_index, 0, keepdims=False)
    mine_pos = lax.dynamic_index_in_dim(position, my_index, 0, keepdims=False)
    slot_ids = jnp.arange(capacity, dtype=jnp.int32)
    asked = (owners == my_index)[:, :, None] & (position[:, :, None] == slot_ids[None, None, :])
    wanted = jnp.sum(asked.astype(jnp.int32) * within[:, :, None], axis=1)
    far_index = (mine_owner * capacity + mine_pos).astype(jnp.int32)

    send_k = k_blocks[wanted.reshape(-1)]
    send_v = v_blocks[wanted.reshape(-1)]
    ctx_move = ("ctx", 0, 0)
    q_heads, far_k, far_v = exchange(
        (queries, send_k, send_v), (head_in, ctx_move, ctx_move), axes, collective_id=1
    )
    q_blocks = q_heads.reshape(local_blocks, BLOCK, width)

    near_k = far_k[far_index]
    near_v = far_v[far_index]
    return attend(q_blocks, k_blocks, v_blocks, near_k, near_v, score_scale, axes, tok_rows)


def solution(mesh):
    placed = (P(("ctx", "head"), None), P(("ctx", "head"), None), P(("ctx", "head"), None), P())
    return jax.shard_map(
        functools.partial(local, axes=tuple(mesh.axis_names)), mesh=mesh, in_specs=placed, out_specs=P(("ctx", "head"), None), check_vma=False
    )
```

```python
import functools
import math

import jax
import jax.numpy as jnp
from jax import lax
from jax.experimental import pallas as pl
from jax.experimental.pallas import tpu as pltpu
from jax.sharding import PartitionSpec as P

MESH = pl.DeviceIdType.MESH

HEADS = 16
HD = 128
BLOCK = 512
RSEL = 2


def exchange_kernel(*refs, axes, jobs):
    count = len(jobs)
    srcs, dsts = refs[:count], refs[count:2 * count]
    send_sems, recv_sems = refs[2 * count], refs[2 * count + 1]

    def device(axis, peer):
        return tuple(peer if name == axis else lax.axis_index(name) for name in axes)

    barrier = pltpu.get_barrier_semaphore()
    peers = 0
    for axis in sorted({job[0] for job in jobs}):
        n = lax.axis_size(axis)
        me = lax.axis_index(axis)
        for k in range(1, n):
            pl.semaphore_signal(
                barrier, inc=1, device_id=device(axis, (me + k) % n), device_id_type=MESH
            )
        peers += n - 1
    pl.semaphore_wait(barrier, peers)

    def view(ref, dim, index, n):
        size = ref.shape[dim] // n
        where = [slice(None)] * len(ref.shape)
        where[dim] = pl.ds(index * size, size)
        return ref.at[tuple(where)]

    copies = []
    for a, (axis, split_axis, concat_axis) in enumerate(jobs):
        n = lax.axis_size(axis)
        me = lax.axis_index(axis)
        own = pltpu.make_async_copy(
            view(srcs[a], split_axis, me, n), view(dsts[a], concat_axis, me, n),
            send_sems.at[a, 0],
        )
        own.start()
        copies.append(own)
        for k in range(1, n):
            peer = (me + k) % n
            copy = pltpu.make_async_remote_copy(
                src_ref=view(srcs[a], split_axis, peer, n),
                dst_ref=view(dsts[a], concat_axis, me, n),
                send_sem=send_sems.at[a, k],
                recv_sem=recv_sems.at[a, k],
                device_id=device(axis, peer),
                device_id_type=MESH,
            )
            copy.start()
            copies.append(copy)
    for copy in copies:
        copy.wait()


def exchange(arrays, jobs, axes, collective_id):
    out_shapes = []
    for x, (axis, split_axis, concat_axis) in zip(arrays, jobs):
        n = lax.axis_size(axis)
        shape = list(x.shape)
        shape[split_axis] //= n
        shape[concat_axis] *= n
        out_shapes.append(jax.ShapeDtypeStruct(tuple(shape), x.dtype))
    widest = max(lax.axis_size(job[0]) for job in jobs)
    count = len(arrays)
    return pl.pallas_call(
        functools.partial(exchange_kernel, axes=axes, jobs=tuple(jobs)),
        out_shape=tuple(out_shapes),
        in_specs=[pl.BlockSpec(memory_space=pl.ANY)] * count,
        out_specs=tuple(pl.BlockSpec(memory_space=pl.ANY) for _ in range(count)),
        scratch_shapes=[
            pltpu.SemaphoreType.DMA((count, widest)),
            pltpu.SemaphoreType.DMA((count, widest)),
        ],
        compiler_params=pltpu.CompilerParams(collective_id=collective_id, has_side_effects=True),
    )(*arrays)


def route_tables(picks, local_blocks, ctx_count):
    slots = local_blocks * RSEL
    owners = (picks // local_blocks).reshape(ctx_count, slots)
    within = (picks % local_blocks).reshape(ctx_count, slots)
    owner_ids = jnp.arange(ctx_count, dtype=jnp.int32)
    one_hot = (owners[:, :, None] == owner_ids[None, None, :]).astype(jnp.int32)
    running = jnp.cumsum(one_hot, axis=1)
    position = jnp.sum(one_hot * running, axis=-1) - 1
    return (owners, within, position)


def slot_attention(q, k, v, scale):
    scores = lax.dot_general(
        q, k, (((1,), (1,)), ((), ())), preferred_element_type=jnp.float32
    ) * scale
    row_max = jnp.max(scores, axis=1, keepdims=True)
    exponent = jnp.exp(scores - row_max)
    row_sum = jnp.sum(exponent, axis=1, keepdims=True)
    partial = jnp.dot(
        exponent.astype(jnp.bfloat16), v, preferred_element_type=jnp.float32
    )
    return row_max, row_sum, partial


def attend_kernel(
    idx_ref, q_ref, k_ref, v_ref, fk_ref, fv_ref, y_ref, stage, send_sems, recv_sems,
    *, axes, heads_here, scale,
):
    n = lax.axis_size("head")
    me = lax.axis_index("head")
    step = pl.program_id(0)
    local_blocks = pl.num_programs(0)
    rows = y_ref.shape[0]
    width = heads_here * HD
    per_block = BLOCK // rows
    turn = me // per_block
    i = (step + turn) % local_blocks

    def device(peer):
        return tuple(peer if name == "head" else lax.axis_index(name) for name in axes)

    @pl.when(step == 0)
    def _():
        barrier = pltpu.get_barrier_semaphore()
        for k in range(1, n):
            pl.semaphore_signal(
                barrier, inc=1, device_id=device((me + k) % n), device_id_type=MESH
            )
        pl.semaphore_wait(barrier, n - 1)

    mine = y_ref.at[:, pl.ds(me * width, width)]

    def piece(b, r):
        return stage.at[b, pl.ds(r * rows, rows), :]

    def remote(b, r, dest):
        return pltpu.make_async_remote_copy(
            src_ref=piece(b, r), dst_ref=mine,
            send_sem=send_sems.at[b * per_block + r], recv_sem=recv_sems.at[me],
            device_id=device(dest), device_id_type=MESH,
        )

    def own(b, r):
        return pltpu.make_async_copy(piece(b, r), mine, send_sems.at[b * per_block + r])

    def send(b):
        for r in range(per_block):
            dest = b * per_block + r

            @pl.when(dest == me)
            def _():
                own(b, r).start()

            @pl.when(dest != me)
            def _():
                remote(b, r, dest).start()

    def finish(b):
        for r in range(per_block):
            dest = b * per_block + r

            @pl.when(dest == me)
            def _():
                own(b, r).wait()

            @pl.when(dest != me)
            def _():
                remote(b, r, dest).wait_send()

    j0 = idx_ref[i * RSEL]
    j1 = idx_ref[i * RSEL + 1]
    for h in range(heads_here):
        cols = slice(h * HD, (h + 1) * HD)
        q = q_ref[0, :, cols]
        parts = [
            slot_attention(q, k_ref[0, :, cols], v_ref[0, :, cols], scale),
            slot_attention(q, fk_ref[j0, :, cols], fv_ref[j0, :, cols], scale),
            slot_attention(q, fk_ref[j1, :, cols], fv_ref[j1, :, cols], scale),
        ]
        top = jnp.maximum(jnp.maximum(parts[0][0], parts[1][0]), parts[2][0])
        numer = None
        denom = None
        for row_max, row_sum, partial in parts:
            factor = jnp.exp(row_max - top)
            numer = partial * factor if numer is None else numer + partial * factor
            denom = row_sum * factor if denom is None else denom + row_sum * factor
        stage[i, :, cols] = (numer / denom).astype(stage.dtype)

    @pl.when(step >= 1)
    def _():
        send((step - 1 + turn) % local_blocks)

    @pl.when(step == local_blocks - 1)
    def _():
        def settle(t, carry):
            finish((t + turn) % local_blocks)
            return carry

        lax.fori_loop(0, local_blocks - 1, settle, 0)
        send(i)
        finish(i)
        for sender in range(n):

            @pl.when(sender != me)
            def _():
                pltpu.make_async_remote_copy(
                    src_ref=piece(0, 0), dst_ref=mine,
                    send_sem=send_sems.at[0], recv_sem=recv_sems.at[sender],
                    device_id=device(sender), device_id_type=MESH,
                ).wait_recv()


def attend(far_index, q_blocks, k_blocks, v_blocks, far_k, far_v, scale, axes, tok_rows):
    local_blocks, _, width = q_blocks.shape
    heads_here = width // HD
    n = HEADS // heads_here
    kernel = functools.partial(attend_kernel, axes=axes, heads_here=heads_here, scale=scale)
    per_block = BLOCK // tok_rows

    def rotated(i):
        return ((i + lax.axis_index("head") // per_block) % local_blocks, 0, 0)

    one = pl.BlockSpec((1, BLOCK, width), rotated)
    whole = pl.BlockSpec(far_k.shape, lambda i: (0, 0, 0), pipeline_mode=pl.Buffered(1))
    smem = pl.BlockSpec(memory_space=pltpu.SMEM)
    flops = local_blocks * heads_here * 3 * 4 * BLOCK * BLOCK * HD
    return pl.pallas_call(
        kernel,
        out_shape=jax.ShapeDtypeStruct((tok_rows, n * width), jnp.bfloat16),
        grid=(local_blocks,),
        in_specs=[smem, one, one, one, whole, whole],
        out_specs=pl.BlockSpec(memory_space=pl.ANY),
        scratch_shapes=[
            pltpu.VMEM((local_blocks, BLOCK, width), jnp.bfloat16),
            pltpu.SemaphoreType.DMA((local_blocks * (BLOCK // tok_rows),)),
            pltpu.SemaphoreType.DMA((n,)),
        ],
        compiler_params=pltpu.CompilerParams(collective_id=2, has_side_effects=True),
        cost_estimate=pl.CostEstimate(
            flops=flops,
            transcendentals=local_blocks * heads_here * 3 * BLOCK * BLOCK,
            bytes_accessed=local_blocks * BLOCK * width * 2 * 8,
        ),
    )(far_index, q_blocks, k_blocks, v_blocks, far_k, far_v)


def local(queries, keys, values, picks, axes):
    head_count = lax.axis_size("head")
    ctx_count = lax.axis_size("ctx")
    my_index = lax.axis_index("ctx")
    heads_here = HEADS // head_count
    width = heads_here * HD
    tok_rows = queries.shape[0]
    score_scale = 1.0 / math.sqrt(HD)
    head_in = ("head", 1, 0)
    k_heads, v_heads = exchange((keys, values), (head_in, head_in), axes, collective_id=0)
    local_blocks = k_heads.shape[0] // BLOCK
    k_blocks = k_heads.reshape(local_blocks, BLOCK, width)
    v_blocks = v_heads.reshape(local_blocks, BLOCK, width)

    capacity = (local_blocks * RSEL + ctx_count - 1) // ctx_count + 1
    owners, within, position = route_tables(picks, local_blocks, ctx_count)
    mine_owner = lax.dynamic_index_in_dim(owners, my_index, 0, keepdims=False)
    mine_pos = lax.dynamic_index_in_dim(position, my_index, 0, keepdims=False)
    slot_ids = jnp.arange(capacity, dtype=jnp.int32)
    asked = (owners == my_index)[:, :, None] & (position[:, :, None] == slot_ids[None, None, :])
    wanted = jnp.sum(asked.astype(jnp.int32) * within[:, :, None], axis=1)
    far_index = (mine_owner * capacity + mine_pos).astype(jnp.int32)

    send_k = k_blocks[wanted.reshape(-1)]
    send_v = v_blocks[wanted.reshape(-1)]
    ctx_move = ("ctx", 0, 0)
    q_heads, far_k, far_v = exchange(
        (queries, send_k, send_v), (head_in, ctx_move, ctx_move), axes, collective_id=1
    )
    q_blocks = q_heads.reshape(local_blocks, BLOCK, width)

    return attend(
        far_index, q_blocks, k_blocks, v_blocks, far_k, far_v, score_scale, axes, tok_rows
    )


def solution(mesh):
    placed = (P(("ctx", "head"), None), P(("ctx", "head"), None), P(("ctx", "head"), None), P())
    return jax.shard_map(
        functools.partial(local, axes=tuple(mesh.axis_names)), mesh=mesh, in_specs=placed, out_specs=P(("ctx", "head"), None), check_vma=False
    )
```

```python
import functools
import math

import jax
import jax.numpy as jnp
from jax import lax
from jax.experimental import pallas as pl
from jax.experimental.pallas import tpu as pltpu
from jax.sharding import PartitionSpec as P

MESH = pl.DeviceIdType.MESH

HEADS = 16
HD = 128
BLOCK = 512
RSEL = 2


def exchange_kernel(*refs, axes, jobs):
    count = len(jobs)
    srcs, dsts = refs[:count], refs[count:2 * count]
    send_sems, recv_sems = refs[2 * count], refs[2 * count + 1]

    def device(axis, peer):
        return tuple(peer if name == axis else lax.axis_index(name) for name in axes)

    barrier = pltpu.get_barrier_semaphore()
    peers = 0
    for axis in sorted({job[0] for job in jobs}):
        n = lax.axis_size(axis)
        me = lax.axis_index(axis)
        for k in range(1, n):
            pl.semaphore_signal(
                barrier, inc=1, device_id=device(axis, (me + k) % n), device_id_type=MESH
            )
        peers += n - 1
    pl.semaphore_wait(barrier, peers)

    def view(ref, dim, index, n):
        size = ref.shape[dim] // n
        where = [slice(None)] * len(ref.shape)
        where[dim] = pl.ds(index * size, size)
        return ref.at[tuple(where)]

    copies = []
    for a, (axis, split_axis, concat_axis) in enumerate(jobs):
        n = lax.axis_size(axis)
        me = lax.axis_index(axis)
        own = pltpu.make_async_copy(
            view(srcs[a], split_axis, me, n), view(dsts[a], concat_axis, me, n),
            send_sems.at[a, 0],
        )
        own.start()
        copies.append(own)
        for k in range(1, n):
            peer = (me + k) % n
            copy = pltpu.make_async_remote_copy(
                src_ref=view(srcs[a], split_axis, peer, n),
                dst_ref=view(dsts[a], concat_axis, me, n),
                send_sem=send_sems.at[a, k],
                recv_sem=recv_sems.at[a, k],
                device_id=device(axis, peer),
                device_id_type=MESH,
            )
            copy.start()
            copies.append(copy)
    for copy in copies:
        copy.wait()


def exchange(arrays, jobs, axes, collective_id):
    out_shapes = []
    for x, (axis, split_axis, concat_axis) in zip(arrays, jobs):
        n = lax.axis_size(axis)
        shape = list(x.shape)
        shape[split_axis] //= n
        shape[concat_axis] *= n
        out_shapes.append(jax.ShapeDtypeStruct(tuple(shape), x.dtype))
    widest = max(lax.axis_size(job[0]) for job in jobs)
    count = len(arrays)
    return pl.pallas_call(
        functools.partial(exchange_kernel, axes=axes, jobs=tuple(jobs)),
        out_shape=tuple(out_shapes),
        in_specs=[pl.BlockSpec(memory_space=pl.ANY)] * count,
        out_specs=tuple(pl.BlockSpec(memory_space=pl.ANY) for _ in range(count)),
        scratch_shapes=[
            pltpu.SemaphoreType.DMA((count, widest)),
            pltpu.SemaphoreType.DMA((count, widest)),
        ],
        compiler_params=pltpu.CompilerParams(collective_id=collective_id, has_side_effects=True),
    )(*arrays)


def route_tables(picks, local_blocks, ctx_count):
    slots = local_blocks * RSEL
    owners = (picks // local_blocks).reshape(ctx_count, slots)
    within = (picks % local_blocks).reshape(ctx_count, slots)
    owner_ids = jnp.arange(ctx_count, dtype=jnp.int32)
    one_hot = (owners[:, :, None] == owner_ids[None, None, :]).astype(jnp.int32)
    running = jnp.cumsum(one_hot, axis=1)
    position = jnp.sum(one_hot * running, axis=-1) - 1
    return (owners, within, position)


def slot_attention(q, k, v, scale):
    scores = lax.dot_general(
        q, k, (((1,), (1,)), ((), ())), preferred_element_type=jnp.float32
    ) * scale
    row_max = jnp.max(scores, axis=1, keepdims=True)
    exponent = jnp.exp(scores - row_max)
    row_sum = jnp.sum(exponent, axis=1, keepdims=True)
    partial = jnp.dot(
        exponent.astype(jnp.bfloat16), v, preferred_element_type=jnp.float32
    )
    return row_max, row_sum, partial


def attend_kernel(
    idx_ref, q_ref, k_ref, v_ref, fk_ref, fv_ref, y_ref, stage, send_sems, recv_sems,
    *, axes, heads_here, scale,
):
    n = lax.axis_size("head")
    me = lax.axis_index("head")
    step = pl.program_id(0)
    local_blocks = pl.num_programs(0)
    rows = y_ref.shape[0]
    width = heads_here * HD
    per_block = BLOCK // rows
    turn = me // per_block
    i = (step + turn) % local_blocks

    def device(peer):
        return tuple(peer if name == "head" else lax.axis_index(name) for name in axes)

    @pl.when(step == 0)
    def _():
        barrier = pltpu.get_barrier_semaphore()
        for k in range(1, n):
            pl.semaphore_signal(
                barrier, inc=1, device_id=device((me + k) % n), device_id_type=MESH
            )
        pl.semaphore_wait(barrier, n - 1)

    mine = y_ref.at[:, pl.ds(me * width, width)]

    def piece(b, r):
        return stage.at[b, pl.ds(r * rows, rows), :]

    def remote(b, r, dest):
        return pltpu.make_async_remote_copy(
            src_ref=piece(b, r), dst_ref=mine,
            send_sem=send_sems.at[b * per_block + r], recv_sem=recv_sems.at[me],
            device_id=device(dest), device_id_type=MESH,
        )

    def own(b, r):
        return pltpu.make_async_copy(piece(b, r), mine, send_sems.at[b * per_block + r])

    def send(b):
        for r in range(per_block):
            dest = b * per_block + r

            @pl.when(dest == me)
            def _():
                own(b, r).start()

            @pl.when(dest != me)
            def _():
                remote(b, r, dest).start()

    def finish(b):
        for r in range(per_block):
            dest = b * per_block + r

            @pl.when(dest == me)
            def _():
                own(b, r).wait()

            @pl.when(dest != me)
            def _():
                remote(b, r, dest).wait_send()

    j0 = idx_ref[i * RSEL]
    j1 = idx_ref[i * RSEL + 1]
    for h in range(heads_here):
        cols = slice(h * HD, (h + 1) * HD)
        q = q_ref[0, :, cols]
        parts = [
            slot_attention(q, k_ref[0, :, cols], v_ref[0, :, cols], scale),
            slot_attention(q, fk_ref[j0, :, cols], fv_ref[j0, :, cols], scale),
            slot_attention(q, fk_ref[j1, :, cols], fv_ref[j1, :, cols], scale),
        ]
        top = jnp.maximum(jnp.maximum(parts[0][0], parts[1][0]), parts[2][0])
        numer = None
        denom = None
        for row_max, row_sum, partial in parts:
            factor = jnp.exp(row_max - top)
            numer = partial * factor if numer is None else numer + partial * factor
            denom = row_sum * factor if denom is None else denom + row_sum * factor
        stage[i, :, cols] = (numer / denom).astype(stage.dtype)

    @pl.when(step >= 1)
    def _():
        send((step - 1 + turn) % local_blocks)

    @pl.when(step == local_blocks - 1)
    def _():
        def settle(t, carry):
            finish((t + turn) % local_blocks)
            return carry

        lax.fori_loop(0, local_blocks - 1, settle, 0)
        send(i)
        finish(i)
        for sender in range(n):

            @pl.when(sender != me)
            def _():
                pltpu.make_async_remote_copy(
                    src_ref=piece(0, 0), dst_ref=mine,
                    send_sem=send_sems.at[0], recv_sem=recv_sems.at[sender],
                    device_id=device(sender), device_id_type=MESH,
                ).wait_recv()


def attend(far_index, q_blocks, k_blocks, v_blocks, far_k, far_v, scale, axes, tok_rows):
    local_blocks, _, width = q_blocks.shape
    heads_here = width // HD
    n = HEADS // heads_here
    kernel = functools.partial(attend_kernel, axes=axes, heads_here=heads_here, scale=scale)
    per_block = BLOCK // tok_rows

    def rotated(i):
        return ((i + lax.axis_index("head") // per_block) % local_blocks, 0, 0)

    one = pl.BlockSpec((1, BLOCK, width), rotated)
    whole = pl.BlockSpec(far_k.shape, lambda i: (0, 0, 0), pipeline_mode=pl.Buffered(1))
    smem = pl.BlockSpec(memory_space=pltpu.SMEM)
    flops = local_blocks * heads_here * 3 * 4 * BLOCK * BLOCK * HD
    return pl.pallas_call(
        kernel,
        out_shape=jax.ShapeDtypeStruct((tok_rows, n * width), jnp.bfloat16),
        grid=(local_blocks,),
        in_specs=[smem, one, one, one, whole, whole],
        out_specs=pl.BlockSpec(memory_space=pl.ANY),
        scratch_shapes=[
            pltpu.VMEM((local_blocks, BLOCK, width), jnp.bfloat16),
            pltpu.SemaphoreType.DMA((local_blocks * (BLOCK // tok_rows),)),
            pltpu.SemaphoreType.DMA((n,)),
        ],
        compiler_params=pltpu.CompilerParams(collective_id=2, has_side_effects=True),
        cost_estimate=pl.CostEstimate(
            flops=flops,
            transcendentals=local_blocks * heads_here * 3 * BLOCK * BLOCK,
            bytes_accessed=local_blocks * BLOCK * width * 2 * 8,
        ),
    )(far_index, q_blocks, k_blocks, v_blocks, far_k, far_v)


def local(queries, keys, values, picks, axes):
    head_count = lax.axis_size("head")
    ctx_count = lax.axis_size("ctx")
    my_index = lax.axis_index("ctx")
    heads_here = HEADS // head_count
    width = heads_here * HD
    tok_rows = queries.shape[0]
    score_scale = 1.0 / math.sqrt(HD)
    head_in = ("head", 1, 0)
    ctx_move = ("ctx", 0, 0)
    (k_heads,) = exchange((keys,), (head_in,), axes, collective_id=0)
    local_blocks = k_heads.shape[0] // BLOCK
    k_blocks = k_heads.reshape(local_blocks, BLOCK, width)

    capacity = (local_blocks * RSEL + ctx_count - 1) // ctx_count + 1
    owners, within, position = route_tables(picks, local_blocks, ctx_count)
    mine_owner = lax.dynamic_index_in_dim(owners, my_index, 0, keepdims=False)
    mine_pos = lax.dynamic_index_in_dim(position, my_index, 0, keepdims=False)
    slot_ids = jnp.arange(capacity, dtype=jnp.int32)
    asked = (owners == my_index)[:, :, None] & (position[:, :, None] == slot_ids[None, None, :])
    wanted = jnp.sum(asked.astype(jnp.int32) * within[:, :, None], axis=1)
    far_index = (mine_owner * capacity + mine_pos).astype(jnp.int32)

    send_k = k_blocks[wanted.reshape(-1)]
    far_k, v_heads, q_heads = exchange(
        (send_k, values, queries), (ctx_move, head_in, head_in), axes, collective_id=1
    )
    q_blocks = q_heads.reshape(local_blocks, BLOCK, width)
    v_blocks = v_heads.reshape(local_blocks, BLOCK, width)
    send_v = v_blocks[wanted.reshape(-1)]
    (far_v,) = exchange((send_v,), (ctx_move,), axes, collective_id=3)
    return attend(
        far_index, q_blocks, k_blocks, v_blocks, far_k, far_v, score_scale, axes, tok_rows
    )


def solution(mesh):
    placed = (P(("ctx", "head"), None), P(("ctx", "head"), None), P(("ctx", "head"), None), P())
    return jax.shard_map(
        functools.partial(local, axes=tuple(mesh.axis_names)), mesh=mesh, in_specs=placed, out_specs=P(("ctx", "head"), None), check_vma=False
    )
```

```python
import functools
import math

import jax
import jax.numpy as jnp
from jax import lax
from jax.experimental import pallas as pl
from jax.experimental.pallas import tpu as pltpu
from jax.sharding import PartitionSpec as P

MESH = pl.DeviceIdType.MESH

HEADS = 16
HD = 128
BLOCK = 512
RSEL = 2


def exchange_kernel(*refs, axes, jobs):
    count = len(jobs)
    srcs, dsts = refs[:count], refs[count:2 * count]
    send_sems, recv_sems = refs[2 * count], refs[2 * count + 1]

    def device(axis, peer):
        return tuple(peer if name == axis else lax.axis_index(name) for name in axes)

    barrier = pltpu.get_barrier_semaphore()
    peers = 0
    for axis in sorted({job[0] for job in jobs}):
        n = lax.axis_size(axis)
        me = lax.axis_index(axis)
        for k in range(1, n):
            pl.semaphore_signal(
                barrier, inc=1, device_id=device(axis, (me + k) % n), device_id_type=MESH
            )
        peers += n - 1
    pl.semaphore_wait(barrier, peers)

    def view(ref, dim, index, n):
        size = ref.shape[dim] // n
        where = [slice(None)] * len(ref.shape)
        where[dim] = pl.ds(index * size, size)
        return ref.at[tuple(where)]

    copies = []
    for a, (axis, split_axis, concat_axis) in enumerate(jobs):
        n = lax.axis_size(axis)
        me = lax.axis_index(axis)
        own = pltpu.make_async_copy(
            view(srcs[a], split_axis, me, n), view(dsts[a], concat_axis, me, n),
            send_sems.at[a, 0],
        )
        own.start()
        copies.append(own)
        for k in range(1, n):
            peer = (me + k) % n
            copy = pltpu.make_async_remote_copy(
                src_ref=view(srcs[a], split_axis, peer, n),
                dst_ref=view(dsts[a], concat_axis, me, n),
                send_sem=send_sems.at[a, k],
                recv_sem=recv_sems.at[a, k],
                device_id=device(axis, peer),
                device_id_type=MESH,
            )
            copy.start()
            copies.append(copy)
    for copy in copies:
        copy.wait()


def exchange(arrays, jobs, axes, collective_id):
    out_shapes = []
    for x, (axis, split_axis, concat_axis) in zip(arrays, jobs):
        n = lax.axis_size(axis)
        shape = list(x.shape)
        shape[split_axis] //= n
        shape[concat_axis] *= n
        out_shapes.append(jax.ShapeDtypeStruct(tuple(shape), x.dtype))
    widest = max(lax.axis_size(job[0]) for job in jobs)
    count = len(arrays)
    return pl.pallas_call(
        functools.partial(exchange_kernel, axes=axes, jobs=tuple(jobs)),
        out_shape=tuple(out_shapes),
        in_specs=[pl.BlockSpec(memory_space=pl.ANY)] * count,
        out_specs=tuple(pl.BlockSpec(memory_space=pl.ANY) for _ in range(count)),
        scratch_shapes=[
            pltpu.SemaphoreType.DMA((count, widest)),
            pltpu.SemaphoreType.DMA((count, widest)),
        ],
        compiler_params=pltpu.CompilerParams(collective_id=collective_id, has_side_effects=True),
    )(*arrays)


def route_tables(picks, local_blocks, ctx_count):
    slots = local_blocks * RSEL
    owners = (picks // local_blocks).reshape(ctx_count, slots)
    within = (picks % local_blocks).reshape(ctx_count, slots)
    owner_ids = jnp.arange(ctx_count, dtype=jnp.int32)
    one_hot = (owners[:, :, None] == owner_ids[None, None, :]).astype(jnp.int32)
    running = jnp.cumsum(one_hot, axis=1)
    position = jnp.sum(one_hot * running, axis=-1) - 1
    return (owners, within, position)


def slot_attention(q, k, v, scale):
    scores = lax.dot_general(
        q, k, (((1,), (1,)), ((), ())), preferred_element_type=jnp.float32
    ) * scale
    row_max = jnp.max(scores, axis=1, keepdims=True)
    exponent = jnp.exp(scores - row_max)
    row_sum = jnp.sum(exponent, axis=1, keepdims=True)
    partial = jnp.dot(
        exponent.astype(jnp.bfloat16), v, preferred_element_type=jnp.float32
    )
    return row_max, row_sum, partial


def finish_kernel(
    idx_ref, q_hbm, k_hbm, v_hbm, fk_hbm, sv_hbm, y_ref,
    qv, kv, vv, fkv, fvv, wts, base, fac, stage,
    load_sems, ctx_send, ctx_recv, out_send, out_recv,
    *, axes, heads_here, scale, capacity,
):
    n = lax.axis_size("head")
    me = lax.axis_index("head")
    m_ctx = lax.axis_size("ctx")
    c_me = lax.axis_index("ctx")
    local_blocks = qv.shape[0]
    rows = y_ref.shape[0]
    width = heads_here * HD
    per_block = BLOCK // rows
    turn = me // per_block

    def device(axis, peer):
        return tuple(peer if name == axis else lax.axis_index(name) for name in axes)

    barrier = pltpu.get_barrier_semaphore()
    for k in range(1, m_ctx):
        pl.semaphore_signal(
            barrier, inc=1, device_id=device("ctx", (c_me + k) % m_ctx), device_id_type=MESH
        )
    for k in range(1, n):
        pl.semaphore_signal(
            barrier, inc=1, device_id=device("head", (me + k) % n), device_id_type=MESH
        )
    pl.semaphore_wait(barrier, m_ctx - 1 + n - 1)

    def rows_of(ref, index):
        return ref.at[pl.ds(index * capacity, capacity)]

    v_copies = [pltpu.make_async_copy(rows_of(sv_hbm, c_me), rows_of(fvv, c_me), ctx_send.at[0])]
    v_copies[0].start()
    for k in range(1, m_ctx):
        peer = (c_me + k) % m_ctx
        copy = pltpu.make_async_remote_copy(
            src_ref=rows_of(sv_hbm, peer), dst_ref=rows_of(fvv, c_me),
            send_sem=ctx_send.at[k], recv_sem=ctx_recv.at[k],
            device_id=device("ctx", peer), device_id_type=MESH,
        )
        copy.start()
        v_copies.append(copy)

    loads = [
        pltpu.make_async_copy(src, dst, load_sems.at[a])
        for a, (src, dst) in enumerate(((q_hbm, qv), (k_hbm, kv), (v_hbm, vv), (fk_hbm, fkv)))
    ]
    for load in loads:
        load.start()
    for load in loads:
        load.wait()

    def prepare(i, carry):
        j0 = idx_ref[i * RSEL]
        j1 = idx_ref[i * RSEL + 1]
        for h in range(heads_here):
            cols = pl.ds(h * HD, HD)
            q = qv[i, :, cols]
            m0, l0, acc0 = slot_attention(q, kv[i, :, cols], vv[i, :, cols], scale)
            stats = []
            for slot, j in enumerate((j0, j1)):
                scores = lax.dot_general(
                    q, fkv[j, :, cols], (((1,), (1,)), ((), ())),
                    preferred_element_type=jnp.float32,
                ) * scale
                row_max = jnp.max(scores, axis=1, keepdims=True)
                exponent = jnp.exp(scores - row_max)
                stats.append((row_max, jnp.sum(exponent, axis=1, keepdims=True)))
                wts[i, h * RSEL + slot] = exponent.astype(jnp.bfloat16)
            top = jnp.maximum(jnp.maximum(m0, stats[0][0]), stats[1][0])
            f0 = jnp.exp(m0 - top)
            f1 = jnp.exp(stats[0][0] - top)
            f2 = jnp.exp(stats[1][0] - top)
            base[i, :, cols] = acc0 * f0
            fac[i, h * 3] = f1
            fac[i, h * 3 + 1] = f2
            fac[i, h * 3 + 2] = l0 * f0 + stats[0][1] * f1 + stats[1][1] * f2
        return carry

    lax.fori_loop(0, local_blocks, prepare, 0)
    for copy in v_copies:
        copy.wait()

    mine = y_ref.at[:, pl.ds(me * width, width)]

    def piece(b, r):
        return stage.at[b, pl.ds(r * rows, rows), :]

    def remote(b, r, dest):
        return pltpu.make_async_remote_copy(
            src_ref=piece(b, r), dst_ref=mine,
            send_sem=out_send.at[b * per_block + r], recv_sem=out_recv.at[me],
            device_id=device("head", dest), device_id_type=MESH,
        )

    def own(b, r):
        return pltpu.make_async_copy(piece(b, r), mine, out_send.at[b * per_block + r])

    def send(b):
        for r in range(per_block):
            dest = b * per_block + r

            @pl.when(dest == me)
            def _():
                own(b, r).start()

            @pl.when(dest != me)
            def _():
                remote(b, r, dest).start()

    def finish(b):
        for r in range(per_block):
            dest = b * per_block + r

            @pl.when(dest == me)
            def _():
                own(b, r).wait()

            @pl.when(dest != me)
            def _():
                remote(b, r, dest).wait_send()

    def complete(t, carry):
        i = (t + turn) % local_blocks
        j0 = idx_ref[i * RSEL]
        j1 = idx_ref[i * RSEL + 1]
        for h in range(heads_here):
            cols = pl.ds(h * HD, HD)
            p1 = jnp.dot(wts[i, h * RSEL], fvv[j0, :, cols], preferred_element_type=jnp.float32)
            p2 = jnp.dot(
                wts[i, h * RSEL + 1], fvv[j1, :, cols], preferred_element_type=jnp.float32
            )
            numer = base[i, :, cols] + p1 * fac[i, h * 3] + p2 * fac[i, h * 3 + 1]
            stage[i, :, cols] = (numer / fac[i, h * 3 + 2]).astype(stage.dtype)

        @pl.when(t >= 1)
        def _():
            send((t - 1 + turn) % local_blocks)

        return carry

    lax.fori_loop(0, local_blocks, complete, 0)

    def settle(t, carry):
        finish((t + turn) % local_blocks)
        return carry

    lax.fori_loop(0, local_blocks - 1, settle, 0)
    last = (local_blocks - 1 + turn) % local_blocks
    send(last)
    finish(last)
    for sender in range(n):

        @pl.when(sender != me)
        def _():
            pltpu.make_async_remote_copy(
                src_ref=piece(0, 0), dst_ref=mine,
                send_sem=out_send.at[0], recv_sem=out_recv.at[sender],
                device_id=device("head", sender), device_id_type=MESH,
            ).wait_recv()


def finish_attention(
    far_index, q_blocks, k_blocks, v_blocks, far_k, send_v, scale, axes, tok_rows, capacity
):
    local_blocks, _, width = q_blocks.shape
    heads_here = width // HD
    n = HEADS // heads_here
    m_ctx = send_v.shape[0] // capacity
    kernel = functools.partial(
        finish_kernel, axes=axes, heads_here=heads_here, scale=scale, capacity=capacity
    )
    anywhere = pl.BlockSpec(memory_space=pl.ANY)
    flops = local_blocks * heads_here * 3 * 4 * BLOCK * BLOCK * HD
    return pl.pallas_call(
        kernel,
        out_shape=jax.ShapeDtypeStruct((tok_rows, n * width), jnp.bfloat16),
        in_specs=[pl.BlockSpec(memory_space=pltpu.SMEM)] + [anywhere] * 5,
        out_specs=anywhere,
        scratch_shapes=[
            pltpu.VMEM(q_blocks.shape, jnp.bfloat16),
            pltpu.VMEM(k_blocks.shape, jnp.bfloat16),
            pltpu.VMEM(v_blocks.shape, jnp.bfloat16),
            pltpu.VMEM(far_k.shape, jnp.bfloat16),
            pltpu.VMEM(send_v.shape, jnp.bfloat16),
            pltpu.VMEM((local_blocks, heads_here * RSEL, BLOCK, BLOCK), jnp.bfloat16),
            pltpu.VMEM((local_blocks, BLOCK, width), jnp.float32),
            pltpu.VMEM((local_blocks, heads_here * 3, BLOCK, 1), jnp.float32),
            pltpu.VMEM((local_blocks, BLOCK, width), jnp.bfloat16),
            pltpu.SemaphoreType.DMA((4,)),
            pltpu.SemaphoreType.DMA((m_ctx,)),
            pltpu.SemaphoreType.DMA((m_ctx,)),
            pltpu.SemaphoreType.DMA((local_blocks * (BLOCK // tok_rows),)),
            pltpu.SemaphoreType.DMA((n,)),
        ],
        compiler_params=pltpu.CompilerParams(
            collective_id=2, has_side_effects=True, vmem_limit_bytes=60 * 1024 * 1024
        ),
        cost_estimate=pl.CostEstimate(
            flops=flops,
            transcendentals=local_blocks * heads_here * 3 * BLOCK * BLOCK,
            bytes_accessed=local_blocks * BLOCK * width * 2 * 8,
        ),
    )(far_index, q_blocks, k_blocks, v_blocks, far_k, send_v)


def local(queries, keys, values, picks, axes):
    head_count = lax.axis_size("head")
    ctx_count = lax.axis_size("ctx")
    my_index = lax.axis_index("ctx")
    heads_here = HEADS // head_count
    width = heads_here * HD
    tok_rows = queries.shape[0]
    score_scale = 1.0 / math.sqrt(HD)
    head_in = ("head", 1, 0)
    ctx_move = ("ctx", 0, 0)
    (k_heads,) = exchange((keys,), (head_in,), axes, collective_id=0)
    local_blocks = k_heads.shape[0] // BLOCK
    k_blocks = k_heads.reshape(local_blocks, BLOCK, width)

    capacity = (local_blocks * RSEL + ctx_count - 1) // ctx_count + 1
    owners, within, position = route_tables(picks, local_blocks, ctx_count)
    mine_owner = lax.dynamic_index_in_dim(owners, my_index, 0, keepdims=False)
    mine_pos = lax.dynamic_index_in_dim(position, my_index, 0, keepdims=False)
    slot_ids = jnp.arange(capacity, dtype=jnp.int32)
    asked = (owners == my_index)[:, :, None] & (position[:, :, None] == slot_ids[None, None, :])
    wanted = jnp.sum(asked.astype(jnp.int32) * within[:, :, None], axis=1)
    far_index = (mine_owner * capacity + mine_pos).astype(jnp.int32)

    send_k = k_blocks[wanted.reshape(-1)]
    far_k, v_heads, q_heads = exchange(
        (send_k, values, queries), (ctx_move, head_in, head_in), axes, collective_id=1
    )
    q_blocks = q_heads.reshape(local_blocks, BLOCK, width)
    v_blocks = v_heads.reshape(local_blocks, BLOCK, width)
    send_v = v_blocks[wanted.reshape(-1)]
    return finish_attention(
        far_index, q_blocks, k_blocks, v_blocks, far_k, send_v, score_scale, axes, tok_rows,
        capacity,
    )


def solution(mesh):
    placed = (P(("ctx", "head"), None), P(("ctx", "head"), None), P(("ctx", "head"), None), P())
    return jax.shard_map(
        functools.partial(local, axes=tuple(mesh.axis_names)), mesh=mesh, in_specs=placed, out_specs=P(("ctx", "head"), None), check_vma=False
    )
```

```python
import functools
import math

import jax
import jax.numpy as jnp
from jax import lax
from jax.experimental import pallas as pl
from jax.experimental.pallas import tpu as pltpu
from jax.sharding import PartitionSpec as P

MESH = pl.DeviceIdType.MESH

HEADS = 16
HD = 128
BLOCK = 512
RSEL = 2


def exchange_kernel(*refs, axes, jobs):
    count = len(jobs)
    srcs, dsts = refs[:count], refs[count:2 * count]
    send_sems, recv_sems = refs[2 * count], refs[2 * count + 1]

    def device(axis, peer):
        return tuple(peer if name == axis else lax.axis_index(name) for name in axes)

    barrier = pltpu.get_barrier_semaphore()
    peers = 0
    for axis in sorted({job[0] for job in jobs}):
        n = lax.axis_size(axis)
        me = lax.axis_index(axis)
        for k in range(1, n):
            pl.semaphore_signal(
                barrier, inc=1, device_id=device(axis, (me + k) % n), device_id_type=MESH
            )
        peers += n - 1
    pl.semaphore_wait(barrier, peers)

    def view(ref, dim, index, n):
        size = ref.shape[dim] // n
        where = [slice(None)] * len(ref.shape)
        where[dim] = pl.ds(index * size, size)
        return ref.at[tuple(where)]

    copies = []
    for a, (axis, split_axis, concat_axis) in enumerate(jobs):
        n = lax.axis_size(axis)
        me = lax.axis_index(axis)
        own = pltpu.make_async_copy(
            view(srcs[a], split_axis, me, n), view(dsts[a], concat_axis, me, n),
            send_sems.at[a, 0],
        )
        own.start()
        copies.append(own)
        for k in range(1, n):
            peer = (me + k) % n
            copy = pltpu.make_async_remote_copy(
                src_ref=view(srcs[a], split_axis, peer, n),
                dst_ref=view(dsts[a], concat_axis, me, n),
                send_sem=send_sems.at[a, k],
                recv_sem=recv_sems.at[a, k],
                device_id=device(axis, peer),
                device_id_type=MESH,
            )
            copy.start()
            copies.append(copy)
    for copy in copies:
        copy.wait()


def exchange(arrays, jobs, axes, collective_id):
    out_shapes = []
    for x, (axis, split_axis, concat_axis) in zip(arrays, jobs):
        n = lax.axis_size(axis)
        shape = list(x.shape)
        shape[split_axis] //= n
        shape[concat_axis] *= n
        out_shapes.append(jax.ShapeDtypeStruct(tuple(shape), x.dtype))
    widest = max(lax.axis_size(job[0]) for job in jobs)
    count = len(arrays)
    return pl.pallas_call(
        functools.partial(exchange_kernel, axes=axes, jobs=tuple(jobs)),
        out_shape=tuple(out_shapes),
        in_specs=[pl.BlockSpec(memory_space=pl.ANY)] * count,
        out_specs=tuple(pl.BlockSpec(memory_space=pl.ANY) for _ in range(count)),
        scratch_shapes=[
            pltpu.SemaphoreType.DMA((count, widest)),
            pltpu.SemaphoreType.DMA((count, widest)),
        ],
        compiler_params=pltpu.CompilerParams(collective_id=collective_id, has_side_effects=True),
    )(*arrays)


def pick_kernel(order_ref, *refs):
    out_ref = refs[-1]
    for t, ref in enumerate(refs[:-1]):
        out_ref[t] = ref[0]


def pick_blocks(table, order, per_step=4):
    slots = order.shape[0]
    _, block, width = table.shape
    if slots % per_step:
        per_step = 1

    def spec(t):
        return pl.BlockSpec((1, block, width), lambda s, order_ref: (order_ref[s * per_step + t], 0, 0))

    grid_spec = pltpu.PrefetchScalarGridSpec(
        num_scalar_prefetch=1,
        grid=(slots // per_step,),
        in_specs=[spec(t) for t in range(per_step)],
        out_specs=pl.BlockSpec((per_step, block, width), lambda s, order_ref: (s, 0, 0)),
    )
    return pl.pallas_call(
        pick_kernel,
        out_shape=jax.ShapeDtypeStruct((slots, block, width), table.dtype),
        grid_spec=grid_spec,
    )(order, *([table] * per_step))


def route_tables(picks, local_blocks, ctx_count):
    slots = local_blocks * RSEL
    owners = (picks // local_blocks).reshape(ctx_count, slots)
    within = (picks % local_blocks).reshape(ctx_count, slots)
    owner_ids = jnp.arange(ctx_count, dtype=jnp.int32)
    one_hot = (owners[:, :, None] == owner_ids[None, None, :]).astype(jnp.int32)
    running = jnp.cumsum(one_hot, axis=1)
    position = jnp.sum(one_hot * running, axis=-1) - 1
    return (owners, within, position)


def slot_attention(q, k, v, scale):
    scores = lax.dot_general(
        q, k, (((1,), (1,)), ((), ())), preferred_element_type=jnp.float32
    ) * scale
    row_max = jnp.max(scores, axis=1, keepdims=True)
    exponent = jnp.exp(scores - row_max)
    row_sum = jnp.sum(exponent, axis=1, keepdims=True)
    partial = jnp.dot(
        exponent.astype(jnp.bfloat16), v, preferred_element_type=jnp.float32
    )
    return row_max, row_sum, partial


def finish_kernel(
    idx_ref, q_hbm, k_hbm, v_hbm, fk_hbm, sv_hbm, y_ref,
    qv, kv, vv, fkv, fvv, wts, base, fac, stage,
    load_sems, ctx_send, ctx_recv, out_send, out_recv,
    *, axes, heads_here, scale, capacity,
):
    n = lax.axis_size("head")
    me = lax.axis_index("head")
    m_ctx = lax.axis_size("ctx")
    c_me = lax.axis_index("ctx")
    local_blocks = qv.shape[0]
    rows = y_ref.shape[0]
    width = heads_here * HD
    per_block = BLOCK // rows
    turn = me // per_block

    def device(axis, peer):
        return tuple(peer if name == axis else lax.axis_index(name) for name in axes)

    barrier = pltpu.get_barrier_semaphore()
    for k in range(1, m_ctx):
        pl.semaphore_signal(
            barrier, inc=1, device_id=device("ctx", (c_me + k) % m_ctx), device_id_type=MESH
        )
    for k in range(1, n):
        pl.semaphore_signal(
            barrier, inc=1, device_id=device("head", (me + k) % n), device_id_type=MESH
        )
    pl.semaphore_wait(barrier, m_ctx - 1 + n - 1)

    def rows_of(ref, index):
        return ref.at[pl.ds(index * capacity, capacity)]

    v_copies = [pltpu.make_async_copy(rows_of(sv_hbm, c_me), rows_of(fvv, c_me), ctx_send.at[0])]
    v_copies[0].start()
    for k in range(1, m_ctx):
        peer = (c_me + k) % m_ctx
        copy = pltpu.make_async_remote_copy(
            src_ref=rows_of(sv_hbm, peer), dst_ref=rows_of(fvv, c_me),
            send_sem=ctx_send.at[k], recv_sem=ctx_recv.at[k],
            device_id=device("ctx", peer), device_id_type=MESH,
        )
        copy.start()
        v_copies.append(copy)

    loads = [
        pltpu.make_async_copy(src, dst, load_sems.at[a])
        for a, (src, dst) in enumerate(((q_hbm, qv), (k_hbm, kv), (v_hbm, vv), (fk_hbm, fkv)))
    ]
    for load in loads:
        load.start()
    for load in loads:
        load.wait()

    def prepare(i, carry):
        j0 = idx_ref[i * RSEL]
        j1 = idx_ref[i * RSEL + 1]
        for h in range(heads_here):
            cols = pl.ds(h * HD, HD)
            q = qv[i, :, cols]
            m0, l0, acc0 = slot_attention(q, kv[i, :, cols], vv[i, :, cols], scale)
            stats = []
            for slot, j in enumerate((j0, j1)):
                scores = lax.dot_general(
                    q, fkv[j, :, cols], (((1,), (1,)), ((), ())),
                    preferred_element_type=jnp.float32,
                ) * scale
                row_max = jnp.max(scores, axis=1, keepdims=True)
                exponent = jnp.exp(scores - row_max)
                stats.append((row_max, jnp.sum(exponent, axis=1, keepdims=True)))
                wts[i, h * RSEL + slot] = exponent.astype(jnp.bfloat16)
            top = jnp.maximum(jnp.maximum(m0, stats[0][0]), stats[1][0])
            f0 = jnp.exp(m0 - top)
            f1 = jnp.exp(stats[0][0] - top)
            f2 = jnp.exp(stats[1][0] - top)
            base[i, :, cols] = acc0 * f0
            fac[i, h * 3] = f1
            fac[i, h * 3 + 1] = f2
            fac[i, h * 3 + 2] = l0 * f0 + stats[0][1] * f1 + stats[1][1] * f2
        return carry

    lax.fori_loop(0, local_blocks, prepare, 0)
    for copy in v_copies:
        copy.wait()

    mine = y_ref.at[:, pl.ds(me * width, width)]

    def piece(b, r):
        return stage.at[b, pl.ds(r * rows, rows), :]

    def remote(b, r, dest):
        return pltpu.make_async_remote_copy(
            src_ref=piece(b, r), dst_ref=mine,
            send_sem=out_send.at[b * per_block + r], recv_sem=out_recv.at[me],
            device_id=device("head", dest), device_id_type=MESH,
        )

    def own(b, r):
        return pltpu.make_async_copy(piece(b, r), mine, out_send.at[b * per_block + r])

    def send(b):
        for r in range(per_block):
            dest = b * per_block + r

            @pl.when(dest == me)
            def _():
                own(b, r).start()

            @pl.when(dest != me)
            def _():
                remote(b, r, dest).start()

    def finish(b):
        for r in range(per_block):
            dest = b * per_block + r

            @pl.when(dest == me)
            def _():
                own(b, r).wait()

            @pl.when(dest != me)
            def _():
                remote(b, r, dest).wait_send()

    def complete(t, carry):
        i = (t + turn) % local_blocks
        j0 = idx_ref[i * RSEL]
        j1 = idx_ref[i * RSEL + 1]
        for h in range(heads_here):
            cols = pl.ds(h * HD, HD)
            p1 = jnp.dot(wts[i, h * RSEL], fvv[j0, :, cols], preferred_element_type=jnp.float32)
            p2 = jnp.dot(
                wts[i, h * RSEL + 1], fvv[j1, :, cols], preferred_element_type=jnp.float32
            )
            numer = base[i, :, cols] + p1 * fac[i, h * 3] + p2 * fac[i, h * 3 + 1]
            stage[i, :, cols] = (numer / fac[i, h * 3 + 2]).astype(stage.dtype)

        @pl.when(t >= 1)
        def _():
            send((t - 1 + turn) % local_blocks)

        return carry

    lax.fori_loop(0, local_blocks, complete, 0)

    def settle(t, carry):
        finish((t + turn) % local_blocks)
        return carry

    lax.fori_loop(0, local_blocks - 1, settle, 0)
    last = (local_blocks - 1 + turn) % local_blocks
    send(last)
    finish(last)
    for sender in range(n):

        @pl.when(sender != me)
        def _():
            pltpu.make_async_remote_copy(
                src_ref=piece(0, 0), dst_ref=mine,
                send_sem=out_send.at[0], recv_sem=out_recv.at[sender],
                device_id=device("head", sender), device_id_type=MESH,
            ).wait_recv()


def finish_attention(
    far_index, q_blocks, k_blocks, v_blocks, far_k, send_v, scale, axes, tok_rows, capacity
):
    local_blocks, _, width = q_blocks.shape
    heads_here = width // HD
    n = HEADS // heads_here
    m_ctx = send_v.shape[0] // capacity
    kernel = functools.partial(
        finish_kernel, axes=axes, heads_here=heads_here, scale=scale, capacity=capacity
    )
    anywhere = pl.BlockSpec(memory_space=pl.ANY)
    flops = local_blocks * heads_here * 3 * 4 * BLOCK * BLOCK * HD
    return pl.pallas_call(
        kernel,
        out_shape=jax.ShapeDtypeStruct((tok_rows, n * width), jnp.bfloat16),
        in_specs=[pl.BlockSpec(memory_space=pltpu.SMEM)] + [anywhere] * 5,
        out_specs=anywhere,
        scratch_shapes=[
            pltpu.VMEM(q_blocks.shape, jnp.bfloat16),
            pltpu.VMEM(k_blocks.shape, jnp.bfloat16),
            pltpu.VMEM(v_blocks.shape, jnp.bfloat16),
            pltpu.VMEM(far_k.shape, jnp.bfloat16),
            pltpu.VMEM(send_v.shape, jnp.bfloat16),
            pltpu.VMEM((local_blocks, heads_here * RSEL, BLOCK, BLOCK), jnp.bfloat16),
            pltpu.VMEM((local_blocks, BLOCK, width), jnp.float32),
            pltpu.VMEM((local_blocks, heads_here * 3, BLOCK, 1), jnp.float32),
            pltpu.VMEM((local_blocks, BLOCK, width), jnp.bfloat16),
            pltpu.SemaphoreType.DMA((4,)),
            pltpu.SemaphoreType.DMA((m_ctx,)),
            pltpu.SemaphoreType.DMA((m_ctx,)),
            pltpu.SemaphoreType.DMA((local_blocks * (BLOCK // tok_rows),)),
            pltpu.SemaphoreType.DMA((n,)),
        ],
        compiler_params=pltpu.CompilerParams(
            collective_id=2, has_side_effects=True, vmem_limit_bytes=60 * 1024 * 1024
        ),
        cost_estimate=pl.CostEstimate(
            flops=flops,
            transcendentals=local_blocks * heads_here * 3 * BLOCK * BLOCK,
            bytes_accessed=local_blocks * BLOCK * width * 2 * 8,
        ),
    )(far_index, q_blocks, k_blocks, v_blocks, far_k, send_v)


def local(queries, keys, values, picks, axes):
    head_count = lax.axis_size("head")
    ctx_count = lax.axis_size("ctx")
    my_index = lax.axis_index("ctx")
    heads_here = HEADS // head_count
    width = heads_here * HD
    tok_rows = queries.shape[0]
    score_scale = 1.0 / math.sqrt(HD)
    head_in = ("head", 1, 0)
    ctx_move = ("ctx", 0, 0)
    (k_heads,) = exchange((keys,), (head_in,), axes, collective_id=0)
    local_blocks = k_heads.shape[0] // BLOCK
    k_blocks = k_heads.reshape(local_blocks, BLOCK, width)

    capacity = (local_blocks * RSEL + ctx_count - 1) // ctx_count + 1
    owners, within, position = route_tables(picks, local_blocks, ctx_count)
    mine_owner = lax.dynamic_index_in_dim(owners, my_index, 0, keepdims=False)
    mine_pos = lax.dynamic_index_in_dim(position, my_index, 0, keepdims=False)
    slot_ids = jnp.arange(capacity, dtype=jnp.int32)
    asked = (owners == my_index)[:, :, None] & (position[:, :, None] == slot_ids[None, None, :])
    wanted = jnp.sum(asked.astype(jnp.int32) * within[:, :, None], axis=1)
    far_index = (mine_owner * capacity + mine_pos).astype(jnp.int32)

    send_k = pick_blocks(k_blocks, wanted.reshape(-1).astype(jnp.int32))
    far_k, v_heads, q_heads = exchange(
        (send_k, values, queries), (ctx_move, head_in, head_in), axes, collective_id=1
    )
    q_blocks = q_heads.reshape(local_blocks, BLOCK, width)
    v_blocks = v_heads.reshape(local_blocks, BLOCK, width)
    send_v = pick_blocks(v_blocks, wanted.reshape(-1).astype(jnp.int32))
    return finish_attention(
        far_index, q_blocks, k_blocks, v_blocks, far_k, send_v, score_scale, axes, tok_rows,
        capacity,
    )


def solution(mesh):
    placed = (P(("ctx", "head"), None), P(("ctx", "head"), None), P(("ctx", "head"), None), P())
    return jax.shard_map(
        functools.partial(local, axes=tuple(mesh.axis_names)), mesh=mesh, in_specs=placed, out_specs=P(("ctx", "head"), None), check_vma=False
    )
```

```python
import functools
import math

import jax
import jax.numpy as jnp
from jax import lax
from jax.experimental import pallas as pl
from jax.experimental.pallas import tpu as pltpu
from jax.sharding import PartitionSpec as P

MESH = pl.DeviceIdType.MESH

HEADS = 16
HD = 128
BLOCK = 512
RSEL = 2


def exchange_kernel(*refs, axes, jobs):
    count = len(jobs)
    srcs, dsts = refs[:count], refs[count:2 * count]
    send_sems, recv_sems = refs[2 * count], refs[2 * count + 1]

    def device(axis, peer):
        return tuple(peer if name == axis else lax.axis_index(name) for name in axes)

    barrier = pltpu.get_barrier_semaphore()
    peers = 0
    for axis in sorted({job[0] for job in jobs}):
        n = lax.axis_size(axis)
        me = lax.axis_index(axis)
        for k in range(1, n):
            pl.semaphore_signal(
                barrier, inc=1, device_id=device(axis, (me + k) % n), device_id_type=MESH
            )
        peers += n - 1
    pl.semaphore_wait(barrier, peers)

    def view(ref, dim, index, n):
        size = ref.shape[dim] // n
        where = [slice(None)] * len(ref.shape)
        where[dim] = pl.ds(index * size, size)
        return ref.at[tuple(where)]

    copies = []
    for a, (axis, split_axis, concat_axis) in enumerate(jobs):
        n = lax.axis_size(axis)
        me = lax.axis_index(axis)
        own = pltpu.make_async_copy(
            view(srcs[a], split_axis, me, n), view(dsts[a], concat_axis, me, n),
            send_sems.at[a, 0],
        )
        own.start()
        copies.append(own)
        for k in range(1, n):
            peer = (me + k) % n
            copy = pltpu.make_async_remote_copy(
                src_ref=view(srcs[a], split_axis, peer, n),
                dst_ref=view(dsts[a], concat_axis, me, n),
                send_sem=send_sems.at[a, k],
                recv_sem=recv_sems.at[a, k],
                device_id=device(axis, peer),
                device_id_type=MESH,
            )
            copy.start()
            copies.append(copy)
    for copy in copies:
        copy.wait()


def exchange(arrays, jobs, axes, collective_id):
    out_shapes = []
    for x, (axis, split_axis, concat_axis) in zip(arrays, jobs):
        n = lax.axis_size(axis)
        shape = list(x.shape)
        shape[split_axis] //= n
        shape[concat_axis] *= n
        out_shapes.append(jax.ShapeDtypeStruct(tuple(shape), x.dtype))
    widest = max(lax.axis_size(job[0]) for job in jobs)
    count = len(arrays)
    return pl.pallas_call(
        functools.partial(exchange_kernel, axes=axes, jobs=tuple(jobs)),
        out_shape=tuple(out_shapes),
        in_specs=[pl.BlockSpec(memory_space=pl.ANY)] * count,
        out_specs=tuple(pl.BlockSpec(memory_space=pl.ANY) for _ in range(count)),
        scratch_shapes=[
            pltpu.SemaphoreType.DMA((count, widest)),
            pltpu.SemaphoreType.DMA((count, widest)),
        ],
        compiler_params=pltpu.CompilerParams(collective_id=collective_id, has_side_effects=True),
    )(*arrays)


def route_tables(picks, local_blocks, ctx_count):
    slots = local_blocks * RSEL
    owners = (picks // local_blocks).reshape(ctx_count, slots)
    within = (picks % local_blocks).reshape(ctx_count, slots)
    owner_ids = jnp.arange(ctx_count, dtype=jnp.int32)
    one_hot = (owners[:, :, None] == owner_ids[None, None, :]).astype(jnp.int32)
    running = jnp.cumsum(one_hot, axis=1)
    position = jnp.sum(one_hot * running, axis=-1) - 1
    return (owners, within, position)


def slot_attention(q, k, v, scale):
    scores = lax.dot_general(
        q, k, (((1,), (1,)), ((), ())), preferred_element_type=jnp.float32
    ) * scale
    row_max = jnp.max(scores, axis=1, keepdims=True)
    exponent = jnp.exp(scores - row_max)
    row_sum = jnp.sum(exponent, axis=1, keepdims=True)
    partial = jnp.dot(
        exponent.astype(jnp.bfloat16), v, preferred_element_type=jnp.float32
    )
    return row_max, row_sum, partial


def finish_kernel(
    idx_ref, q_hbm, k_hbm, v_hbm, fk_hbm, sv_hbm, y_ref,
    qv, kv, vv, fkv, fvv, wts, base, fac, stage,
    load_sems, ctx_send, ctx_recv, out_send, out_recv, q_send, q_recv,
    *, axes, heads_here, scale, capacity,
):
    n = lax.axis_size("head")
    me = lax.axis_index("head")
    m_ctx = lax.axis_size("ctx")
    c_me = lax.axis_index("ctx")
    local_blocks = qv.shape[0]
    rows = y_ref.shape[0]
    width = heads_here * HD
    per_block = BLOCK // rows
    turn = me // per_block

    def device(axis, peer):
        return tuple(peer if name == axis else lax.axis_index(name) for name in axes)

    barrier = pltpu.get_barrier_semaphore()
    for k in range(1, m_ctx):
        pl.semaphore_signal(
            barrier, inc=1, device_id=device("ctx", (c_me + k) % m_ctx), device_id_type=MESH
        )
    for k in range(1, n):
        pl.semaphore_signal(
            barrier, inc=1, device_id=device("head", (me + k) % n), device_id_type=MESH
        )
    pl.semaphore_wait(barrier, m_ctx - 1 + n - 1)

    def rows_of(ref, index):
        return ref.at[pl.ds(index * capacity, capacity)]

    v_copies = [pltpu.make_async_copy(rows_of(sv_hbm, c_me), rows_of(fvv, c_me), ctx_send.at[0])]
    v_copies[0].start()
    for k in range(1, m_ctx):
        peer = (c_me + k) % m_ctx
        copy = pltpu.make_async_remote_copy(
            src_ref=rows_of(sv_hbm, peer), dst_ref=rows_of(fvv, c_me),
            send_sem=ctx_send.at[k], recv_sem=ctx_recv.at[k],
            device_id=device("ctx", peer), device_id_type=MESH,
        )
        copy.start()
        v_copies.append(copy)

    def q_rows(owner):
        return qv.at[owner // per_block, pl.ds((owner % per_block) * rows, rows), :]

    def q_cols(peer):
        return q_hbm.at[:, pl.ds(peer * width, width)]

    loads = [pltpu.make_async_copy(q_cols(me), q_rows(me), q_send.at[0])]
    loads[0].start()
    for k in range(1, n):
        peer = (me + k) % n
        copy = pltpu.make_async_remote_copy(
            src_ref=q_cols(peer), dst_ref=q_rows(me),
            send_sem=q_send.at[k], recv_sem=q_recv.at[k],
            device_id=device("head", peer), device_id_type=MESH,
        )
        copy.start()
        loads.append(copy)
    for a, (src, dst) in enumerate(((k_hbm, kv), (v_hbm, vv), (fk_hbm, fkv))):
        load = pltpu.make_async_copy(src, dst, load_sems.at[a])
        load.start()
        loads.append(load)
    for load in loads:
        load.wait()

    def prepare(i, carry):
        j0 = idx_ref[i * RSEL]
        j1 = idx_ref[i * RSEL + 1]
        for h in range(heads_here):
            cols = pl.ds(h * HD, HD)
            q = qv[i, :, cols]
            m0, l0, acc0 = slot_attention(q, kv[i, :, cols], vv[i, :, cols], scale)
            stats = []
            for slot, j in enumerate((j0, j1)):
                scores = lax.dot_general(
                    q, fkv[j, :, cols], (((1,), (1,)), ((), ())),
                    preferred_element_type=jnp.float32,
                ) * scale
                row_max = jnp.max(scores, axis=1, keepdims=True)
                exponent = jnp.exp(scores - row_max)
                stats.append((row_max, jnp.sum(exponent, axis=1, keepdims=True)))
                wts[i, h * RSEL + slot] = exponent.astype(jnp.bfloat16)
            top = jnp.maximum(jnp.maximum(m0, stats[0][0]), stats[1][0])
            f0 = jnp.exp(m0 - top)
            f1 = jnp.exp(stats[0][0] - top)
            f2 = jnp.exp(stats[1][0] - top)
            base[i, :, cols] = acc0 * f0
            fac[i, h * 3] = f1
            fac[i, h * 3 + 1] = f2
            fac[i, h * 3 + 2] = l0 * f0 + stats[0][1] * f1 + stats[1][1] * f2
        return carry

    lax.fori_loop(0, local_blocks, prepare, 0)
    for copy in v_copies:
        copy.wait()

    mine = y_ref.at[:, pl.ds(me * width, width)]

    def piece(b, r):
        return stage.at[b, pl.ds(r * rows, rows), :]

    def remote(b, r, dest):
        return pltpu.make_async_remote_copy(
            src_ref=piece(b, r), dst_ref=mine,
            send_sem=out_send.at[b * per_block + r], recv_sem=out_recv.at[me],
            device_id=device("head", dest), device_id_type=MESH,
        )

    def own(b, r):
        return pltpu.make_async_copy(piece(b, r), mine, out_send.at[b * per_block + r])

    def send(b):
        for r in range(per_block):
            dest = b * per_block + r

            @pl.when(dest == me)
            def _():
                own(b, r).start()

            @pl.when(dest != me)
            def _():
                remote(b, r, dest).start()

    def finish(b):
        for r in range(per_block):
            dest = b * per_block + r

            @pl.when(dest == me)
            def _():
                own(b, r).wait()

            @pl.when(dest != me)
            def _():
                remote(b, r, dest).wait_send()

    def complete(t, carry):
        i = (t + turn) % local_blocks
        j0 = idx_ref[i * RSEL]
        j1 = idx_ref[i * RSEL + 1]
        for h in range(heads_here):
            cols = pl.ds(h * HD, HD)
            p1 = jnp.dot(wts[i, h * RSEL], fvv[j0, :, cols], preferred_element_type=jnp.float32)
            p2 = jnp.dot(
                wts[i, h * RSEL + 1], fvv[j1, :, cols], preferred_element_type=jnp.float32
            )
            numer = base[i, :, cols] + p1 * fac[i, h * 3] + p2 * fac[i, h * 3 + 1]
            stage[i, :, cols] = (numer / fac[i, h * 3 + 2]).astype(stage.dtype)

        @pl.when(t >= 1)
        def _():
            send((t - 1 + turn) % local_blocks)

        return carry

    lax.fori_loop(0, local_blocks, complete, 0)

    def settle(t, carry):
        finish((t + turn) % local_blocks)
        return carry

    lax.fori_loop(0, local_blocks - 1, settle, 0)
    last = (local_blocks - 1 + turn) % local_blocks
    send(last)
    finish(last)
    for sender in range(n):

        @pl.when(sender != me)
        def _():
            pltpu.make_async_remote_copy(
                src_ref=piece(0, 0), dst_ref=mine,
                send_sem=out_send.at[0], recv_sem=out_recv.at[sender],
                device_id=device("head", sender), device_id_type=MESH,
            ).wait_recv()


def finish_attention(
    far_index, queries, k_blocks, v_blocks, far_k, send_v, scale, axes, tok_rows, capacity
):
    local_blocks, _, width = k_blocks.shape
    heads_here = width // HD
    n = HEADS // heads_here
    m_ctx = send_v.shape[0] // capacity
    kernel = functools.partial(
        finish_kernel, axes=axes, heads_here=heads_here, scale=scale, capacity=capacity
    )
    anywhere = pl.BlockSpec(memory_space=pl.ANY)
    flops = local_blocks * heads_here * 3 * 4 * BLOCK * BLOCK * HD
    return pl.pallas_call(
        kernel,
        out_shape=jax.ShapeDtypeStruct((tok_rows, n * width), jnp.bfloat16),
        in_specs=[pl.BlockSpec(memory_space=pltpu.SMEM)] + [anywhere] * 5,
        out_specs=anywhere,
        scratch_shapes=[
            pltpu.VMEM(k_blocks.shape, jnp.bfloat16),
            pltpu.VMEM(k_blocks.shape, jnp.bfloat16),
            pltpu.VMEM(v_blocks.shape, jnp.bfloat16),
            pltpu.VMEM(far_k.shape, jnp.bfloat16),
            pltpu.VMEM(send_v.shape, jnp.bfloat16),
            pltpu.VMEM((local_blocks, heads_here * RSEL, BLOCK, BLOCK), jnp.bfloat16),
            pltpu.VMEM((local_blocks, BLOCK, width), jnp.float32),
            pltpu.VMEM((local_blocks, heads_here * 3, BLOCK, 1), jnp.float32),
            pltpu.VMEM((local_blocks, BLOCK, width), jnp.bfloat16),
            pltpu.SemaphoreType.DMA((4,)),
            pltpu.SemaphoreType.DMA((m_ctx,)),
            pltpu.SemaphoreType.DMA((m_ctx,)),
            pltpu.SemaphoreType.DMA((local_blocks * (BLOCK // tok_rows),)),
            pltpu.SemaphoreType.DMA((n,)),
            pltpu.SemaphoreType.DMA((n,)),
            pltpu.SemaphoreType.DMA((n,)),
        ],
        compiler_params=pltpu.CompilerParams(
            collective_id=2, has_side_effects=True, vmem_limit_bytes=60 * 1024 * 1024
        ),
        cost_estimate=pl.CostEstimate(
            flops=flops,
            transcendentals=local_blocks * heads_here * 3 * BLOCK * BLOCK,
            bytes_accessed=local_blocks * BLOCK * width * 2 * 8,
        ),
    )(far_index, queries, k_blocks, v_blocks, far_k, send_v)


def local(queries, keys, values, picks, axes):
    head_count = lax.axis_size("head")
    ctx_count = lax.axis_size("ctx")
    my_index = lax.axis_index("ctx")
    heads_here = HEADS // head_count
    width = heads_here * HD
    tok_rows = queries.shape[0]
    score_scale = 1.0 / math.sqrt(HD)
    head_in = ("head", 1, 0)
    ctx_move = ("ctx", 0, 0)
    (k_heads,) = exchange((keys,), (head_in,), axes, collective_id=0)
    local_blocks = k_heads.shape[0] // BLOCK
    k_blocks = k_heads.reshape(local_blocks, BLOCK, width)

    capacity = (local_blocks * RSEL + ctx_count - 1) // ctx_count + 1
    owners, within, position = route_tables(picks, local_blocks, ctx_count)
    mine_owner = lax.dynamic_index_in_dim(owners, my_index, 0, keepdims=False)
    mine_pos = lax.dynamic_index_in_dim(position, my_index, 0, keepdims=False)
    slot_ids = jnp.arange(capacity, dtype=jnp.int32)
    asked = (owners == my_index)[:, :, None] & (position[:, :, None] == slot_ids[None, None, :])
    wanted = jnp.sum(asked.astype(jnp.int32) * within[:, :, None], axis=1)
    far_index = (mine_owner * capacity + mine_pos).astype(jnp.int32)

    send_k = k_blocks[wanted.reshape(-1)]
    far_k, v_heads = exchange((send_k, values), (ctx_move, head_in), axes, collective_id=1)
    v_blocks = v_heads.reshape(local_blocks, BLOCK, width)
    send_v = v_blocks[wanted.reshape(-1)]
    return finish_attention(
        far_index, queries, k_blocks, v_blocks, far_k, send_v, score_scale, axes, tok_rows,
        capacity,
    )


def solution(mesh):
    placed = (P(("ctx", "head"), None), P(("ctx", "head"), None), P(("ctx", "head"), None), P())
    return jax.shard_map(
        functools.partial(local, axes=tuple(mesh.axis_names)), mesh=mesh, in_specs=placed, out_specs=P(("ctx", "head"), None), check_vma=False
    )
```

```python
import functools
import math

import jax
import jax.numpy as jnp
from jax import lax
from jax.experimental import pallas as pl
from jax.experimental.pallas import tpu as pltpu
from jax.sharding import PartitionSpec as P

MESH = pl.DeviceIdType.MESH

HEADS = 16
HD = 128
BLOCK = 512
RSEL = 2


def peer_order(axis, n):
    if axis != "ctx" or n % 2:
        return list(range(1, n))
    ring = n // 2

    def reach(k):
        step = k % ring
        return min(step, ring - step) + 2 * (k // ring)

    return sorted(range(1, n), key=lambda k: (-reach(k), k))


def exchange_kernel(*refs, axes, jobs):
    count = len(jobs)
    srcs, dsts = refs[:count], refs[count:2 * count]
    send_sems, recv_sems = refs[2 * count], refs[2 * count + 1]

    def device(axis, peer):
        return tuple(peer if name == axis else lax.axis_index(name) for name in axes)

    barrier = pltpu.get_barrier_semaphore()
    peers = 0
    for axis in sorted({job[0] for job in jobs}):
        n = lax.axis_size(axis)
        me = lax.axis_index(axis)
        for k in range(1, n):
            pl.semaphore_signal(
                barrier, inc=1, device_id=device(axis, (me + k) % n), device_id_type=MESH
            )
        peers += n - 1
    pl.semaphore_wait(barrier, peers)

    def view(ref, dim, index, n):
        size = ref.shape[dim] // n
        where = [slice(None)] * len(ref.shape)
        where[dim] = pl.ds(index * size, size)
        return ref.at[tuple(where)]

    copies = []
    for a, (axis, split_axis, concat_axis) in enumerate(jobs):
        n = lax.axis_size(axis)
        me = lax.axis_index(axis)
        own = pltpu.make_async_copy(
            view(srcs[a], split_axis, me, n), view(dsts[a], concat_axis, me, n),
            send_sems.at[a, 0],
        )
        own.start()
        copies.append(own)
        for k in peer_order(axis, n):
            peer = (me + k) % n
            copy = pltpu.make_async_remote_copy(
                src_ref=view(srcs[a], split_axis, peer, n),
                dst_ref=view(dsts[a], concat_axis, me, n),
                send_sem=send_sems.at[a, k],
                recv_sem=recv_sems.at[a, k],
                device_id=device(axis, peer),
                device_id_type=MESH,
            )
            copy.start()
            copies.append(copy)
    for copy in copies:
        copy.wait()


def exchange(arrays, jobs, axes, collective_id):
    out_shapes = []
    for x, (axis, split_axis, concat_axis) in zip(arrays, jobs):
        n = lax.axis_size(axis)
        shape = list(x.shape)
        shape[split_axis] //= n
        shape[concat_axis] *= n
        out_shapes.append(jax.ShapeDtypeStruct(tuple(shape), x.dtype))
    widest = max(lax.axis_size(job[0]) for job in jobs)
    count = len(arrays)
    return pl.pallas_call(
        functools.partial(exchange_kernel, axes=axes, jobs=tuple(jobs)),
        out_shape=tuple(out_shapes),
        in_specs=[pl.BlockSpec(memory_space=pl.ANY)] * count,
        out_specs=tuple(pl.BlockSpec(memory_space=pl.ANY) for _ in range(count)),
        scratch_shapes=[
            pltpu.SemaphoreType.DMA((count, widest)),
            pltpu.SemaphoreType.DMA((count, widest)),
        ],
        compiler_params=pltpu.CompilerParams(collective_id=collective_id, has_side_effects=True),
    )(*arrays)


def route_tables(picks, local_blocks, ctx_count):
    slots = local_blocks * RSEL
    owners = (picks // local_blocks).reshape(ctx_count, slots)
    within = (picks % local_blocks).reshape(ctx_count, slots)
    owner_ids = jnp.arange(ctx_count, dtype=jnp.int32)
    one_hot = (owners[:, :, None] == owner_ids[None, None, :]).astype(jnp.int32)
    running = jnp.cumsum(one_hot, axis=1)
    position = jnp.sum(one_hot * running, axis=-1) - 1
    return (owners, within, position)


def slot_attention(q, k, v, scale):
    scores = lax.dot_general(
        q, k, (((1,), (1,)), ((), ())), preferred_element_type=jnp.float32
    ) * scale
    row_max = jnp.max(scores, axis=1, keepdims=True)
    exponent = jnp.exp(scores - row_max)
    row_sum = jnp.sum(exponent, axis=1, keepdims=True)
    partial = jnp.dot(
        exponent.astype(jnp.bfloat16), v, preferred_element_type=jnp.float32
    )
    return row_max, row_sum, partial


def finish_kernel(
    idx_ref, q_hbm, k_hbm, v_hbm, fk_hbm, sv_hbm, y_ref,
    qv, kv, vv, fkv, fvv, wts, base, fac, stage,
    load_sems, ctx_send, ctx_recv, out_send, out_recv, q_send, q_recv,
    *, axes, heads_here, scale, capacity,
):
    n = lax.axis_size("head")
    me = lax.axis_index("head")
    m_ctx = lax.axis_size("ctx")
    c_me = lax.axis_index("ctx")
    local_blocks = qv.shape[0]
    rows = y_ref.shape[0]
    width = heads_here * HD
    per_block = BLOCK // rows
    turn = me // per_block

    def device(axis, peer):
        return tuple(peer if name == axis else lax.axis_index(name) for name in axes)

    barrier = pltpu.get_barrier_semaphore()
    for k in range(1, m_ctx):
        pl.semaphore_signal(
            barrier, inc=1, device_id=device("ctx", (c_me + k) % m_ctx), device_id_type=MESH
        )
    for k in range(1, n):
        pl.semaphore_signal(
            barrier, inc=1, device_id=device("head", (me + k) % n), device_id_type=MESH
        )
    pl.semaphore_wait(barrier, m_ctx - 1 + n - 1)

    def rows_of(ref, index):
        return ref.at[pl.ds(index * capacity, capacity)]

    v_copies = [pltpu.make_async_copy(rows_of(sv_hbm, c_me), rows_of(fvv, c_me), ctx_send.at[0])]
    v_copies[0].start()
    for k in peer_order("ctx", m_ctx):
        peer = (c_me + k) % m_ctx
        copy = pltpu.make_async_remote_copy(
            src_ref=rows_of(sv_hbm, peer), dst_ref=rows_of(fvv, c_me),
            send_sem=ctx_send.at[k], recv_sem=ctx_recv.at[k],
            device_id=device("ctx", peer), device_id_type=MESH,
        )
        copy.start()
        v_copies.append(copy)

    def q_rows(owner):
        return qv.at[owner // per_block, pl.ds((owner % per_block) * rows, rows), :]

    def q_cols(peer):
        return q_hbm.at[:, pl.ds(peer * width, width)]

    loads = [pltpu.make_async_copy(q_cols(me), q_rows(me), q_send.at[0])]
    loads[0].start()
    for k in range(1, n):
        peer = (me + k) % n
        copy = pltpu.make_async_remote_copy(
            src_ref=q_cols(peer), dst_ref=q_rows(me),
            send_sem=q_send.at[k], recv_sem=q_recv.at[k],
            device_id=device("head", peer), device_id_type=MESH,
        )
        copy.start()
        loads.append(copy)
    for a, (src, dst) in enumerate(((k_hbm, kv), (v_hbm, vv), (fk_hbm, fkv))):
        load = pltpu.make_async_copy(src, dst, load_sems.at[a])
        load.start()
        loads.append(load)
    for load in loads:
        load.wait()

    def prepare(i, carry):
        j0 = idx_ref[i * RSEL]
        j1 = idx_ref[i * RSEL + 1]
        for h in range(heads_here):
            cols = pl.ds(h * HD, HD)
            q = qv[i, :, cols]
            m0, l0, acc0 = slot_attention(q, kv[i, :, cols], vv[i, :, cols], scale)
            stats = []
            for slot, j in enumerate((j0, j1)):
                scores = lax.dot_general(
                    q, fkv[j, :, cols], (((1,), (1,)), ((), ())),
                    preferred_element_type=jnp.float32,
                ) * scale
                row_max = jnp.max(scores, axis=1, keepdims=True)
                exponent = jnp.exp(scores - row_max)
                stats.append((row_max, jnp.sum(exponent, axis=1, keepdims=True)))
                wts[i, h * RSEL + slot] = exponent.astype(jnp.bfloat16)
            top = jnp.maximum(jnp.maximum(m0, stats[0][0]), stats[1][0])
            f0 = jnp.exp(m0 - top)
            f1 = jnp.exp(stats[0][0] - top)
            f2 = jnp.exp(stats[1][0] - top)
            base[i, :, cols] = acc0 * f0
            fac[i, h * 3] = f1
            fac[i, h * 3 + 1] = f2
            fac[i, h * 3 + 2] = l0 * f0 + stats[0][1] * f1 + stats[1][1] * f2
        return carry

    lax.fori_loop(0, local_blocks, prepare, 0)
    for copy in v_copies:
        copy.wait()

    mine = y_ref.at[:, pl.ds(me * width, width)]

    def piece(b, r):
        return stage.at[b, pl.ds(r * rows, rows), :]

    def remote(b, r, dest):
        return pltpu.make_async_remote_copy(
            src_ref=piece(b, r), dst_ref=mine,
            send_sem=out_send.at[b * per_block + r], recv_sem=out_recv.at[me],
            device_id=device("head", dest), device_id_type=MESH,
        )

    def own(b, r):
        return pltpu.make_async_copy(piece(b, r), mine, out_send.at[b * per_block + r])

    def send(b):
        for r in range(per_block):
            dest = b * per_block + r

            @pl.when(dest == me)
            def _():
                own(b, r).start()

            @pl.when(dest != me)
            def _():
                remote(b, r, dest).start()

    def finish(b):
        for r in range(per_block):
            dest = b * per_block + r

            @pl.when(dest == me)
            def _():
                own(b, r).wait()

            @pl.when(dest != me)
            def _():
                remote(b, r, dest).wait_send()

    def complete(t, carry):
        i = (t + turn) % local_blocks
        j0 = idx_ref[i * RSEL]
        j1 = idx_ref[i * RSEL + 1]
        for h in range(heads_here):
            cols = pl.ds(h * HD, HD)
            p1 = jnp.dot(wts[i, h * RSEL], fvv[j0, :, cols], preferred_element_type=jnp.float32)
            p2 = jnp.dot(
                wts[i, h * RSEL + 1], fvv[j1, :, cols], preferred_element_type=jnp.float32
            )
            numer = base[i, :, cols] + p1 * fac[i, h * 3] + p2 * fac[i, h * 3 + 1]
            stage[i, :, cols] = (numer / fac[i, h * 3 + 2]).astype(stage.dtype)

        @pl.when(t >= 1)
        def _():
            send((t - 1 + turn) % local_blocks)

        return carry

    lax.fori_loop(0, local_blocks, complete, 0)

    def settle(t, carry):
        finish((t + turn) % local_blocks)
        return carry

    lax.fori_loop(0, local_blocks - 1, settle, 0)
    last = (local_blocks - 1 + turn) % local_blocks
    send(last)
    finish(last)
    for sender in range(n):

        @pl.when(sender != me)
        def _():
            pltpu.make_async_remote_copy(
                src_ref=piece(0, 0), dst_ref=mine,
                send_sem=out_send.at[0], recv_sem=out_recv.at[sender],
                device_id=device("head", sender), device_id_type=MESH,
            ).wait_recv()


def finish_attention(
    far_index, queries, k_blocks, v_blocks, far_k, send_v, scale, axes, tok_rows, capacity
):
    local_blocks, _, width = k_blocks.shape
    heads_here = width // HD
    n = HEADS // heads_here
    m_ctx = send_v.shape[0] // capacity
    kernel = functools.partial(
        finish_kernel, axes=axes, heads_here=heads_here, scale=scale, capacity=capacity
    )
    anywhere = pl.BlockSpec(memory_space=pl.ANY)
    flops = local_blocks * heads_here * 3 * 4 * BLOCK * BLOCK * HD
    return pl.pallas_call(
        kernel,
        out_shape=jax.ShapeDtypeStruct((tok_rows, n * width), jnp.bfloat16),
        in_specs=[pl.BlockSpec(memory_space=pltpu.SMEM)] + [anywhere] * 5,
        out_specs=anywhere,
        scratch_shapes=[
            pltpu.VMEM(k_blocks.shape, jnp.bfloat16),
            pltpu.VMEM(k_blocks.shape, jnp.bfloat16),
            pltpu.VMEM(v_blocks.shape, jnp.bfloat16),
            pltpu.VMEM(far_k.shape, jnp.bfloat16),
            pltpu.VMEM(send_v.shape, jnp.bfloat16),
            pltpu.VMEM((local_blocks, heads_here * RSEL, BLOCK, BLOCK), jnp.bfloat16),
            pltpu.VMEM((local_blocks, BLOCK, width), jnp.float32),
            pltpu.VMEM((local_blocks, heads_here * 3, BLOCK, 1), jnp.float32),
            pltpu.VMEM((local_blocks, BLOCK, width), jnp.bfloat16),
            pltpu.SemaphoreType.DMA((4,)),
            pltpu.SemaphoreType.DMA((m_ctx,)),
            pltpu.SemaphoreType.DMA((m_ctx,)),
            pltpu.SemaphoreType.DMA((local_blocks * (BLOCK // tok_rows),)),
            pltpu.SemaphoreType.DMA((n,)),
            pltpu.SemaphoreType.DMA((n,)),
            pltpu.SemaphoreType.DMA((n,)),
        ],
        compiler_params=pltpu.CompilerParams(
            collective_id=2, has_side_effects=True, vmem_limit_bytes=60 * 1024 * 1024
        ),
        cost_estimate=pl.CostEstimate(
            flops=flops,
            transcendentals=local_blocks * heads_here * 3 * BLOCK * BLOCK,
            bytes_accessed=local_blocks * BLOCK * width * 2 * 8,
        ),
    )(far_index, queries, k_blocks, v_blocks, far_k, send_v)


def local(queries, keys, values, picks, axes):
    head_count = lax.axis_size("head")
    ctx_count = lax.axis_size("ctx")
    my_index = lax.axis_index("ctx")
    heads_here = HEADS // head_count
    width = heads_here * HD
    tok_rows = queries.shape[0]
    score_scale = 1.0 / math.sqrt(HD)
    head_in = ("head", 1, 0)
    ctx_move = ("ctx", 0, 0)
    (k_heads,) = exchange((keys,), (head_in,), axes, collective_id=0)
    local_blocks = k_heads.shape[0] // BLOCK
    k_blocks = k_heads.reshape(local_blocks, BLOCK, width)

    capacity = (local_blocks * RSEL + ctx_count - 1) // ctx_count + 1
    owners, within, position = route_tables(picks, local_blocks, ctx_count)
    mine_owner = lax.dynamic_index_in_dim(owners, my_index, 0, keepdims=False)
    mine_pos = lax.dynamic_index_in_dim(position, my_index, 0, keepdims=False)
    slot_ids = jnp.arange(capacity, dtype=jnp.int32)
    asked = (owners == my_index)[:, :, None] & (position[:, :, None] == slot_ids[None, None, :])
    wanted = jnp.sum(asked.astype(jnp.int32) * within[:, :, None], axis=1)
    far_index = (mine_owner * capacity + mine_pos).astype(jnp.int32)

    send_k = k_blocks[wanted.reshape(-1)]
    far_k, v_heads = exchange((send_k, values), (ctx_move, head_in), axes, collective_id=1)
    v_blocks = v_heads.reshape(local_blocks, BLOCK, width)
    send_v = v_blocks[wanted.reshape(-1)]
    return finish_attention(
        far_index, queries, k_blocks, v_blocks, far_k, send_v, score_scale, axes, tok_rows,
        capacity,
    )


def solution(mesh):
    placed = (P(("ctx", "head"), None), P(("ctx", "head"), None), P(("ctx", "head"), None), P())
    return jax.shard_map(
        functools.partial(local, axes=tuple(mesh.axis_names)), mesh=mesh, in_specs=placed, out_specs=P(("ctx", "head"), None), check_vma=False
    )
```

```python
import functools
import math

import jax
import jax.numpy as jnp
from jax import lax
from jax.experimental import pallas as pl
from jax.experimental.pallas import tpu as pltpu
from jax.sharding import PartitionSpec as P

MESH = pl.DeviceIdType.MESH

HEADS = 16
HD = 128
BLOCK = 512
RSEL = 2


def exchange_kernel(*refs, axes, jobs):
    count = len(jobs)
    srcs, dsts = refs[:count], refs[count:2 * count]
    send_sems, recv_sems = refs[2 * count], refs[2 * count + 1]

    def device(axis, peer):
        return tuple(peer if name == axis else lax.axis_index(name) for name in axes)

    barrier = pltpu.get_barrier_semaphore()
    peers = 0
    for axis in sorted({job[0] for job in jobs}):
        n = lax.axis_size(axis)
        me = lax.axis_index(axis)
        for k in range(1, n):
            pl.semaphore_signal(
                barrier, inc=1, device_id=device(axis, (me + k) % n), device_id_type=MESH
            )
        peers += n - 1
    pl.semaphore_wait(barrier, peers)

    def view(ref, dim, index, n):
        size = ref.shape[dim] // n
        where = [slice(None)] * len(ref.shape)
        where[dim] = pl.ds(index * size, size)
        return ref.at[tuple(where)]

    copies = []
    for a, (axis, split_axis, concat_axis) in enumerate(jobs):
        n = lax.axis_size(axis)
        me = lax.axis_index(axis)
        own = pltpu.make_async_copy(
            view(srcs[a], split_axis, me, n), view(dsts[a], concat_axis, me, n),
            send_sems.at[a, 0],
        )
        own.start()
        copies.append(own)
        for k in range(1, n):
            peer = (me + k) % n
            copy = pltpu.make_async_remote_copy(
                src_ref=view(srcs[a], split_axis, peer, n),
                dst_ref=view(dsts[a], concat_axis, me, n),
                send_sem=send_sems.at[a, k],
                recv_sem=recv_sems.at[a, k],
                device_id=device(axis, peer),
                device_id_type=MESH,
            )
            copy.start()
            copies.append(copy)
    for copy in copies:
        copy.wait()


def exchange(arrays, jobs, axes, collective_id):
    out_shapes = []
    for x, (axis, split_axis, concat_axis) in zip(arrays, jobs):
        n = lax.axis_size(axis)
        shape = list(x.shape)
        shape[split_axis] //= n
        shape[concat_axis] *= n
        out_shapes.append(jax.ShapeDtypeStruct(tuple(shape), x.dtype))
    widest = max(lax.axis_size(job[0]) for job in jobs)
    count = len(arrays)
    return pl.pallas_call(
        functools.partial(exchange_kernel, axes=axes, jobs=tuple(jobs)),
        out_shape=tuple(out_shapes),
        in_specs=[pl.BlockSpec(memory_space=pl.ANY)] * count,
        out_specs=tuple(pl.BlockSpec(memory_space=pl.ANY) for _ in range(count)),
        scratch_shapes=[
            pltpu.SemaphoreType.DMA((count, widest)),
            pltpu.SemaphoreType.DMA((count, widest)),
        ],
        compiler_params=pltpu.CompilerParams(collective_id=collective_id, has_side_effects=True),
    )(*arrays)


def route_tables(picks, local_blocks, ctx_count):
    slots = local_blocks * RSEL
    owners = (picks // local_blocks).reshape(ctx_count, slots)
    within = (picks % local_blocks).reshape(ctx_count, slots)
    owner_ids = jnp.arange(ctx_count, dtype=jnp.int32)
    one_hot = (owners[:, :, None] == owner_ids[None, None, :]).astype(jnp.int32)
    running = jnp.cumsum(one_hot, axis=1)
    position = jnp.sum(one_hot * running, axis=-1) - 1
    return (owners, within, position)


def slot_attention(q, k, v, scale):
    scores = lax.dot_general(
        q, k, (((1,), (1,)), ((), ())), preferred_element_type=jnp.float32
    ) * scale
    row_max = jnp.max(scores, axis=1, keepdims=True)
    exponent = jnp.exp(scores - row_max)
    row_sum = jnp.sum(exponent, axis=1, keepdims=True)
    partial = jnp.dot(
        exponent.astype(jnp.bfloat16), v, preferred_element_type=jnp.float32
    )
    return row_max, row_sum, partial


def finish_kernel(
    idx_ref, q_hbm, k_hbm, v_hbm, fk_hbm, sv_hbm, y_ref,
    qv, kv, vv, fkv, fvv, wts, base, fac, stage,
    load_sems, ctx_send, ctx_recv, out_send, out_recv, q_send, q_recv,
    *, axes, heads_here, scale, capacity,
):
    n = lax.axis_size("head")
    me = lax.axis_index("head")
    m_ctx = lax.axis_size("ctx")
    c_me = lax.axis_index("ctx")
    local_blocks = qv.shape[0]
    rows = y_ref.shape[0]
    width = heads_here * HD
    per_block = BLOCK // rows
    turn = me // per_block

    def device(axis, peer):
        return tuple(peer if name == axis else lax.axis_index(name) for name in axes)

    barrier = pltpu.get_barrier_semaphore()
    for k in range(1, m_ctx):
        pl.semaphore_signal(
            barrier, inc=1, device_id=device("ctx", (c_me + k) % m_ctx), device_id_type=MESH
        )
    for k in range(1, n):
        pl.semaphore_signal(
            barrier, inc=1, device_id=device("head", (me + k) % n), device_id_type=MESH
        )
    pl.semaphore_wait(barrier, m_ctx - 1 + n - 1)

    def rows_of(ref, index):
        return ref.at[pl.ds(index * capacity, capacity)]

    v_copies = [pltpu.make_async_copy(rows_of(sv_hbm, c_me), rows_of(fvv, c_me), ctx_send.at[0])]
    v_copies[0].start()
    for k in range(1, m_ctx):
        peer = (c_me + k) % m_ctx
        copy = pltpu.make_async_remote_copy(
            src_ref=rows_of(sv_hbm, peer), dst_ref=rows_of(fvv, c_me),
            send_sem=ctx_send.at[k], recv_sem=ctx_recv.at[k],
            device_id=device("ctx", peer), device_id_type=MESH,
        )
        copy.start()
        v_copies.append(copy)

    def q_rows(owner):
        return qv.at[owner // per_block, pl.ds((owner % per_block) * rows, rows), :]

    def q_cols(peer):
        return q_hbm.at[:, pl.ds(peer * width, width)]

    loads = [pltpu.make_async_copy(q_cols(me), q_rows(me), q_send.at[0])]
    loads[0].start()
    for k in range(1, n):
        peer = (me + k) % n
        copy = pltpu.make_async_remote_copy(
            src_ref=q_cols(peer), dst_ref=q_rows(me),
            send_sem=q_send.at[k], recv_sem=q_recv.at[k],
            device_id=device("head", peer), device_id_type=MESH,
        )
        copy.start()
        loads.append(copy)
    for a, (src, dst) in enumerate(((k_hbm, kv), (v_hbm, vv), (fk_hbm, fkv))):
        load = pltpu.make_async_copy(src, dst, load_sems.at[a])
        load.start()
        loads.append(load)
    for load in loads:
        load.wait()

    def prepare(i, carry):
        j0 = idx_ref[i * RSEL]
        j1 = idx_ref[i * RSEL + 1]
        for h in range(heads_here):
            cols = pl.ds(h * HD, HD)
            q = qv[i, :, cols]
            m0, l0, acc0 = slot_attention(q, kv[i, :, cols], vv[i, :, cols], scale)
            stats = []
            for slot, j in enumerate((j0, j1)):
                scores = lax.dot_general(
                    q, fkv[j, :, cols], (((1,), (1,)), ((), ())),
                    preferred_element_type=jnp.float32,
                ) * scale
                row_max = jnp.max(scores, axis=1, keepdims=True)
                exponent = jnp.exp(scores - row_max)
                stats.append((row_max, jnp.sum(exponent, axis=1, keepdims=True)))
                wts[i, h * RSEL + slot] = exponent.astype(jnp.bfloat16)
            top = jnp.maximum(jnp.maximum(m0, stats[0][0]), stats[1][0])
            f0 = jnp.exp(m0 - top)
            f1 = jnp.exp(stats[0][0] - top)
            f2 = jnp.exp(stats[1][0] - top)
            scale_back = 1.0 / (l0 * f0 + stats[0][1] * f1 + stats[1][1] * f2)
            base[i, :, cols] = acc0 * (f0 * scale_back)
            fac[i, h * 2] = f1 * scale_back
            fac[i, h * 2 + 1] = f2 * scale_back
        return carry

    lax.fori_loop(0, local_blocks, prepare, 0)
    for copy in v_copies:
        copy.wait()

    mine = y_ref.at[:, pl.ds(me * width, width)]

    def piece(b, r):
        return stage.at[b, pl.ds(r * rows, rows), :]

    def remote(b, r, dest):
        return pltpu.make_async_remote_copy(
            src_ref=piece(b, r), dst_ref=mine,
            send_sem=out_send.at[b * per_block + r], recv_sem=out_recv.at[me],
            device_id=device("head", dest), device_id_type=MESH,
        )

    def own(b, r):
        return pltpu.make_async_copy(piece(b, r), mine, out_send.at[b * per_block + r])

    def send(b):
        for r in range(per_block):
            dest = b * per_block + r

            @pl.when(dest == me)
            def _():
                own(b, r).start()

            @pl.when(dest != me)
            def _():
                remote(b, r, dest).start()

    def finish(b):
        for r in range(per_block):
            dest = b * per_block + r

            @pl.when(dest == me)
            def _():
                own(b, r).wait()

            @pl.when(dest != me)
            def _():
                remote(b, r, dest).wait_send()

    def complete(t, carry):
        i = (t + turn) % local_blocks
        j0 = idx_ref[i * RSEL]
        j1 = idx_ref[i * RSEL + 1]
        for h in range(heads_here):
            cols = pl.ds(h * HD, HD)
            p1 = jnp.dot(wts[i, h * RSEL], fvv[j0, :, cols], preferred_element_type=jnp.float32)
            p2 = jnp.dot(
                wts[i, h * RSEL + 1], fvv[j1, :, cols], preferred_element_type=jnp.float32
            )
            numer = base[i, :, cols] + p1 * fac[i, h * 2] + p2 * fac[i, h * 2 + 1]
            stage[i, :, cols] = numer.astype(stage.dtype)

        @pl.when(t >= 1)
        def _():
            send((t - 1 + turn) % local_blocks)

        return carry

    lax.fori_loop(0, local_blocks, complete, 0)

    def settle(t, carry):
        finish((t + turn) % local_blocks)
        return carry

    lax.fori_loop(0, local_blocks - 1, settle, 0)
    last = (local_blocks - 1 + turn) % local_blocks
    send(last)
    finish(last)
    for sender in range(n):

        @pl.when(sender != me)
        def _():
            pltpu.make_async_remote_copy(
                src_ref=piece(0, 0), dst_ref=mine,
                send_sem=out_send.at[0], recv_sem=out_recv.at[sender],
                device_id=device("head", sender), device_id_type=MESH,
            ).wait_recv()


def finish_attention(
    far_index, queries, k_blocks, v_blocks, far_k, send_v, scale, axes, tok_rows, capacity
):
    local_blocks, _, width = k_blocks.shape
    heads_here = width // HD
    n = HEADS // heads_here
    m_ctx = send_v.shape[0] // capacity
    kernel = functools.partial(
        finish_kernel, axes=axes, heads_here=heads_here, scale=scale, capacity=capacity
    )
    anywhere = pl.BlockSpec(memory_space=pl.ANY)
    flops = local_blocks * heads_here * 3 * 4 * BLOCK * BLOCK * HD
    return pl.pallas_call(
        kernel,
        out_shape=jax.ShapeDtypeStruct((tok_rows, n * width), jnp.bfloat16),
        in_specs=[pl.BlockSpec(memory_space=pltpu.SMEM)] + [anywhere] * 5,
        out_specs=anywhere,
        scratch_shapes=[
            pltpu.VMEM(k_blocks.shape, jnp.bfloat16),
            pltpu.VMEM(k_blocks.shape, jnp.bfloat16),
            pltpu.VMEM(v_blocks.shape, jnp.bfloat16),
            pltpu.VMEM(far_k.shape, jnp.bfloat16),
            pltpu.VMEM(send_v.shape, jnp.bfloat16),
            pltpu.VMEM((local_blocks, heads_here * RSEL, BLOCK, BLOCK), jnp.bfloat16),
            pltpu.VMEM((local_blocks, BLOCK, width), jnp.float32),
            pltpu.VMEM((local_blocks, heads_here * 2, BLOCK, 1), jnp.float32),
            pltpu.VMEM((local_blocks, BLOCK, width), jnp.bfloat16),
            pltpu.SemaphoreType.DMA((4,)),
            pltpu.SemaphoreType.DMA((m_ctx,)),
            pltpu.SemaphoreType.DMA((m_ctx,)),
            pltpu.SemaphoreType.DMA((local_blocks * (BLOCK // tok_rows),)),
            pltpu.SemaphoreType.DMA((n,)),
            pltpu.SemaphoreType.DMA((n,)),
            pltpu.SemaphoreType.DMA((n,)),
        ],
        compiler_params=pltpu.CompilerParams(
            collective_id=2, has_side_effects=True, vmem_limit_bytes=60 * 1024 * 1024
        ),
        cost_estimate=pl.CostEstimate(
            flops=flops,
            transcendentals=local_blocks * heads_here * 3 * BLOCK * BLOCK,
            bytes_accessed=local_blocks * BLOCK * width * 2 * 8,
        ),
    )(far_index, queries, k_blocks, v_blocks, far_k, send_v)


def local(queries, keys, values, picks, axes):
    head_count = lax.axis_size("head")
    ctx_count = lax.axis_size("ctx")
    my_index = lax.axis_index("ctx")
    heads_here = HEADS // head_count
    width = heads_here * HD
    tok_rows = queries.shape[0]
    score_scale = 1.0 / math.sqrt(HD)
    head_in = ("head", 1, 0)
    ctx_move = ("ctx", 0, 0)
    (k_heads,) = exchange((keys,), (head_in,), axes, collective_id=0)
    local_blocks = k_heads.shape[0] // BLOCK
    k_blocks = k_heads.reshape(local_blocks, BLOCK, width)

    capacity = (local_blocks * RSEL + ctx_count - 1) // ctx_count + 1
    owners, within, position = route_tables(picks, local_blocks, ctx_count)
    mine_owner = lax.dynamic_index_in_dim(owners, my_index, 0, keepdims=False)
    mine_pos = lax.dynamic_index_in_dim(position, my_index, 0, keepdims=False)
    slot_ids = jnp.arange(capacity, dtype=jnp.int32)
    asked = (owners == my_index)[:, :, None] & (position[:, :, None] == slot_ids[None, None, :])
    wanted = jnp.sum(asked.astype(jnp.int32) * within[:, :, None], axis=1)
    far_index = (mine_owner * capacity + mine_pos).astype(jnp.int32)

    send_k = k_blocks[wanted.reshape(-1)]
    far_k, v_heads = exchange((send_k, values), (ctx_move, head_in), axes, collective_id=1)
    v_blocks = v_heads.reshape(local_blocks, BLOCK, width)
    send_v = v_blocks[wanted.reshape(-1)]
    return finish_attention(
        far_index, queries, k_blocks, v_blocks, far_k, send_v, score_scale, axes, tok_rows,
        capacity,
    )


def solution(mesh):
    placed = (P(("ctx", "head"), None), P(("ctx", "head"), None), P(("ctx", "head"), None), P())
    return jax.shard_map(
        functools.partial(local, axes=tuple(mesh.axis_names)), mesh=mesh, in_specs=placed, out_specs=P(("ctx", "head"), None), check_vma=False
    )
```

```python
import functools
import math

import jax
import jax.numpy as jnp
from jax import lax
from jax.experimental import pallas as pl
from jax.experimental.pallas import tpu as pltpu
from jax.sharding import PartitionSpec as P

MESH = pl.DeviceIdType.MESH

HEADS = 16
HD = 128
BLOCK = 512
RSEL = 2


def exchange_kernel(*refs, axes, jobs):
    count = len(jobs)
    srcs, dsts = refs[:count], refs[count:2 * count]
    send_sems, recv_sems = refs[2 * count], refs[2 * count + 1]

    def device(axis, peer):
        return tuple(peer if name == axis else lax.axis_index(name) for name in axes)

    barrier = pltpu.get_barrier_semaphore()
    peers = 0
    for axis in sorted({job[0] for job in jobs}):
        n = lax.axis_size(axis)
        me = lax.axis_index(axis)
        for k in range(1, n):
            pl.semaphore_signal(
                barrier, inc=1, device_id=device(axis, (me + k) % n), device_id_type=MESH
            )
        peers += n - 1
    pl.semaphore_wait(barrier, peers)

    def view(ref, dim, index, n):
        size = ref.shape[dim] // n
        where = [slice(None)] * len(ref.shape)
        where[dim] = pl.ds(index * size, size)
        return ref.at[tuple(where)]

    copies = []
    for a, (axis, split_axis, concat_axis) in enumerate(jobs):
        n = lax.axis_size(axis)
        me = lax.axis_index(axis)
        own = pltpu.make_async_copy(
            view(srcs[a], split_axis, me, n), view(dsts[a], concat_axis, me, n),
            send_sems.at[a, 0],
        )
        own.start()
        copies.append(own)
        for k in range(1, n):
            peer = (me + k) % n
            copy = pltpu.make_async_remote_copy(
                src_ref=view(srcs[a], split_axis, peer, n),
                dst_ref=view(dsts[a], concat_axis, me, n),
                send_sem=send_sems.at[a, k],
                recv_sem=recv_sems.at[a, k],
                device_id=device(axis, peer),
                device_id_type=MESH,
            )
            copy.start()
            copies.append(copy)
    for copy in copies:
        copy.wait()


def exchange(arrays, jobs, axes, collective_id):
    out_shapes = []
    for x, (axis, split_axis, concat_axis) in zip(arrays, jobs):
        n = lax.axis_size(axis)
        shape = list(x.shape)
        shape[split_axis] //= n
        shape[concat_axis] *= n
        out_shapes.append(jax.ShapeDtypeStruct(tuple(shape), x.dtype))
    widest = max(lax.axis_size(job[0]) for job in jobs)
    count = len(arrays)
    return pl.pallas_call(
        functools.partial(exchange_kernel, axes=axes, jobs=tuple(jobs)),
        out_shape=tuple(out_shapes),
        in_specs=[pl.BlockSpec(memory_space=pl.ANY)] * count,
        out_specs=tuple(pl.BlockSpec(memory_space=pl.ANY) for _ in range(count)),
        scratch_shapes=[
            pltpu.SemaphoreType.DMA((count, widest)),
            pltpu.SemaphoreType.DMA((count, widest)),
        ],
        compiler_params=pltpu.CompilerParams(collective_id=collective_id, has_side_effects=True),
    )(*arrays)


def route_tables(picks, local_blocks, ctx_count):
    slots = local_blocks * RSEL
    owners = (picks // local_blocks).reshape(ctx_count, slots)
    within = (picks % local_blocks).reshape(ctx_count, slots)
    order = jnp.arange(slots, dtype=jnp.int32)
    earlier = (owners[:, :, None] == owners[:, None, :]) & (order[None, None, :] < order[None, :, None])
    position = jnp.sum(earlier.astype(jnp.int32), axis=-1)
    return (owners, within, position)


def slot_attention(q, k, v, scale):
    scores = lax.dot_general(
        q, k, (((1,), (1,)), ((), ())), preferred_element_type=jnp.float32
    ) * scale
    row_max = jnp.max(scores, axis=1, keepdims=True)
    exponent = jnp.exp(scores - row_max)
    row_sum = jnp.sum(exponent, axis=1, keepdims=True)
    partial = jnp.dot(
        exponent.astype(jnp.bfloat16), v, preferred_element_type=jnp.float32
    )
    return row_max, row_sum, partial


def finish_kernel(
    idx_ref, q_hbm, k_hbm, v_hbm, fk_hbm, sv_hbm, y_ref,
    qv, kv, vv, fkv, fvv, wts, base, fac, stage,
    load_sems, ctx_send, ctx_recv, out_send, out_recv, q_send, q_recv,
    *, axes, heads_here, scale, capacity,
):
    n = lax.axis_size("head")
    me = lax.axis_index("head")
    m_ctx = lax.axis_size("ctx")
    c_me = lax.axis_index("ctx")
    local_blocks = qv.shape[0]
    rows = y_ref.shape[0]
    width = heads_here * HD
    per_block = BLOCK // rows
    turn = me // per_block

    def device(axis, peer):
        return tuple(peer if name == axis else lax.axis_index(name) for name in axes)

    barrier = pltpu.get_barrier_semaphore()
    for k in range(1, m_ctx):
        pl.semaphore_signal(
            barrier, inc=1, device_id=device("ctx", (c_me + k) % m_ctx), device_id_type=MESH
        )
    for k in range(1, n):
        pl.semaphore_signal(
            barrier, inc=1, device_id=device("head", (me + k) % n), device_id_type=MESH
        )
    pl.semaphore_wait(barrier, m_ctx - 1 + n - 1)

    def rows_of(ref, index):
        return ref.at[pl.ds(index * capacity, capacity)]

    v_copies = [pltpu.make_async_copy(rows_of(sv_hbm, c_me), rows_of(fvv, c_me), ctx_send.at[0])]
    v_copies[0].start()
    for k in range(1, m_ctx):
        peer = (c_me + k) % m_ctx
        copy = pltpu.make_async_remote_copy(
            src_ref=rows_of(sv_hbm, peer), dst_ref=rows_of(fvv, c_me),
            send_sem=ctx_send.at[k], recv_sem=ctx_recv.at[k],
            device_id=device("ctx", peer), device_id_type=MESH,
        )
        copy.start()
        v_copies.append(copy)

    def q_rows(owner):
        return qv.at[owner // per_block, pl.ds((owner % per_block) * rows, rows), :]

    def q_cols(peer):
        return q_hbm.at[:, pl.ds(peer * width, width)]

    loads = [pltpu.make_async_copy(q_cols(me), q_rows(me), q_send.at[0])]
    loads[0].start()
    for k in range(1, n):
        peer = (me + k) % n
        copy = pltpu.make_async_remote_copy(
            src_ref=q_cols(peer), dst_ref=q_rows(me),
            send_sem=q_send.at[k], recv_sem=q_recv.at[k],
            device_id=device("head", peer), device_id_type=MESH,
        )
        copy.start()
        loads.append(copy)
    for a, (src, dst) in enumerate(((k_hbm, kv), (v_hbm, vv), (fk_hbm, fkv))):
        load = pltpu.make_async_copy(src, dst, load_sems.at[a])
        load.start()
        loads.append(load)
    for load in loads:
        load.wait()

    def prepare(i, carry):
        j0 = idx_ref[i * RSEL]
        j1 = idx_ref[i * RSEL + 1]
        for h in range(heads_here):
            cols = pl.ds(h * HD, HD)
            q = qv[i, :, cols]
            m0, l0, acc0 = slot_attention(q, kv[i, :, cols], vv[i, :, cols], scale)
            stats = []
            for slot, j in enumerate((j0, j1)):
                scores = lax.dot_general(
                    q, fkv[j, :, cols], (((1,), (1,)), ((), ())),
                    preferred_element_type=jnp.float32,
                ) * scale
                row_max = jnp.max(scores, axis=1, keepdims=True)
                exponent = jnp.exp(scores - row_max)
                stats.append((row_max, jnp.sum(exponent, axis=1, keepdims=True)))
                wts[i, h * RSEL + slot] = exponent.astype(jnp.bfloat16)
            top = jnp.maximum(jnp.maximum(m0, stats[0][0]), stats[1][0])
            f0 = jnp.exp(m0 - top)
            f1 = jnp.exp(stats[0][0] - top)
            f2 = jnp.exp(stats[1][0] - top)
            base[i, :, cols] = acc0 * f0
            fac[i, h * 3] = f1
            fac[i, h * 3 + 1] = f2
            fac[i, h * 3 + 2] = l0 * f0 + stats[0][1] * f1 + stats[1][1] * f2
        return carry

    lax.fori_loop(0, local_blocks, prepare, 0)
    for copy in v_copies:
        copy.wait()

    mine = y_ref.at[:, pl.ds(me * width, width)]

    def piece(b, r):
        return stage.at[b, pl.ds(r * rows, rows), :]

    def remote(b, r, dest):
        return pltpu.make_async_remote_copy(
            src_ref=piece(b, r), dst_ref=mine,
            send_sem=out_send.at[b * per_block + r], recv_sem=out_recv.at[me],
            device_id=device("head", dest), device_id_type=MESH,
        )

    def own(b, r):
        return pltpu.make_async_copy(piece(b, r), mine, out_send.at[b * per_block + r])

    def send(b):
        for r in range(per_block):
            dest = b * per_block + r

            @pl.when(dest == me)
            def _():
                own(b, r).start()

            @pl.when(dest != me)
            def _():
                remote(b, r, dest).start()

    def finish(b):
        for r in range(per_block):
            dest = b * per_block + r

            @pl.when(dest == me)
            def _():
                own(b, r).wait()

            @pl.when(dest != me)
            def _():
                remote(b, r, dest).wait_send()

    def complete(t, carry):
        i = (t + turn) % local_blocks
        j0 = idx_ref[i * RSEL]
        j1 = idx_ref[i * RSEL + 1]
        for h in range(heads_here):
            cols = pl.ds(h * HD, HD)
            p1 = jnp.dot(wts[i, h * RSEL], fvv[j0, :, cols], preferred_element_type=jnp.float32)
            p2 = jnp.dot(
                wts[i, h * RSEL + 1], fvv[j1, :, cols], preferred_element_type=jnp.float32
            )
            numer = base[i, :, cols] + p1 * fac[i, h * 3] + p2 * fac[i, h * 3 + 1]
            stage[i, :, cols] = (numer / fac[i, h * 3 + 2]).astype(stage.dtype)

        @pl.when(t >= 1)
        def _():
            send((t - 1 + turn) % local_blocks)

        return carry

    lax.fori_loop(0, local_blocks, complete, 0)

    def settle(t, carry):
        finish((t + turn) % local_blocks)
        return carry

    lax.fori_loop(0, local_blocks - 1, settle, 0)
    last = (local_blocks - 1 + turn) % local_blocks
    send(last)
    finish(last)
    for sender in range(n):

        @pl.when(sender != me)
        def _():
            pltpu.make_async_remote_copy(
                src_ref=piece(0, 0), dst_ref=mine,
                send_sem=out_send.at[0], recv_sem=out_recv.at[sender],
                device_id=device("head", sender), device_id_type=MESH,
            ).wait_recv()


def finish_attention(
    far_index, queries, k_blocks, v_blocks, far_k, send_v, scale, axes, tok_rows, capacity
):
    local_blocks, _, width = k_blocks.shape
    heads_here = width // HD
    n = HEADS // heads_here
    m_ctx = send_v.shape[0] // capacity
    kernel = functools.partial(
        finish_kernel, axes=axes, heads_here=heads_here, scale=scale, capacity=capacity
    )
    anywhere = pl.BlockSpec(memory_space=pl.ANY)
    flops = local_blocks * heads_here * 3 * 4 * BLOCK * BLOCK * HD
    return pl.pallas_call(
        kernel,
        out_shape=jax.ShapeDtypeStruct((tok_rows, n * width), jnp.bfloat16),
        in_specs=[pl.BlockSpec(memory_space=pltpu.SMEM)] + [anywhere] * 5,
        out_specs=anywhere,
        scratch_shapes=[
            pltpu.VMEM(k_blocks.shape, jnp.bfloat16),
            pltpu.VMEM(k_blocks.shape, jnp.bfloat16),
            pltpu.VMEM(v_blocks.shape, jnp.bfloat16),
            pltpu.VMEM(far_k.shape, jnp.bfloat16),
            pltpu.VMEM(send_v.shape, jnp.bfloat16),
            pltpu.VMEM((local_blocks, heads_here * RSEL, BLOCK, BLOCK), jnp.bfloat16),
            pltpu.VMEM((local_blocks, BLOCK, width), jnp.float32),
            pltpu.VMEM((local_blocks, heads_here * 3, BLOCK, 1), jnp.float32),
            pltpu.VMEM((local_blocks, BLOCK, width), jnp.bfloat16),
            pltpu.SemaphoreType.DMA((4,)),
            pltpu.SemaphoreType.DMA((m_ctx,)),
            pltpu.SemaphoreType.DMA((m_ctx,)),
            pltpu.SemaphoreType.DMA((local_blocks * (BLOCK // tok_rows),)),
            pltpu.SemaphoreType.DMA((n,)),
            pltpu.SemaphoreType.DMA((n,)),
            pltpu.SemaphoreType.DMA((n,)),
        ],
        compiler_params=pltpu.CompilerParams(
            collective_id=2, has_side_effects=True, vmem_limit_bytes=60 * 1024 * 1024
        ),
        cost_estimate=pl.CostEstimate(
            flops=flops,
            transcendentals=local_blocks * heads_here * 3 * BLOCK * BLOCK,
            bytes_accessed=local_blocks * BLOCK * width * 2 * 8,
        ),
    )(far_index, queries, k_blocks, v_blocks, far_k, send_v)


def local(queries, keys, values, picks, axes):
    head_count = lax.axis_size("head")
    ctx_count = lax.axis_size("ctx")
    my_index = lax.axis_index("ctx")
    heads_here = HEADS // head_count
    width = heads_here * HD
    tok_rows = queries.shape[0]
    score_scale = 1.0 / math.sqrt(HD)
    head_in = ("head", 1, 0)
    ctx_move = ("ctx", 0, 0)
    (k_heads,) = exchange((keys,), (head_in,), axes, collective_id=0)
    local_blocks = k_heads.shape[0] // BLOCK
    k_blocks = k_heads.reshape(local_blocks, BLOCK, width)

    capacity = (local_blocks * RSEL + ctx_count - 1) // ctx_count + 1
    owners, within, position = route_tables(picks, local_blocks, ctx_count)
    mine_owner = lax.dynamic_index_in_dim(owners, my_index, 0, keepdims=False)
    mine_pos = lax.dynamic_index_in_dim(position, my_index, 0, keepdims=False)
    slot_ids = jnp.arange(capacity, dtype=jnp.int32)
    asked = (owners == my_index)[:, :, None] & (position[:, :, None] == slot_ids[None, None, :])
    wanted = jnp.sum(asked.astype(jnp.int32) * within[:, :, None], axis=1)
    far_index = (mine_owner * capacity + mine_pos).astype(jnp.int32)

    send_k = k_blocks[wanted.reshape(-1)]
    far_k, v_heads = exchange((send_k, values), (ctx_move, head_in), axes, collective_id=1)
    v_blocks = v_heads.reshape(local_blocks, BLOCK, width)
    send_v = v_blocks[wanted.reshape(-1)]
    return finish_attention(
        far_index, queries, k_blocks, v_blocks, far_k, send_v, score_scale, axes, tok_rows,
        capacity,
    )


def solution(mesh):
    placed = (P(("ctx", "head"), None), P(("ctx", "head"), None), P(("ctx", "head"), None), P())
    return jax.shard_map(
        functools.partial(local, axes=tuple(mesh.axis_names)), mesh=mesh, in_specs=placed, out_specs=P(("ctx", "head"), None), check_vma=False
    )
```

```python
import functools
import math

import jax
import jax.numpy as jnp
from jax import lax
from jax.experimental import pallas as pl
from jax.experimental.pallas import tpu as pltpu
from jax.sharding import PartitionSpec as P

MESH = pl.DeviceIdType.MESH

HEADS = 16
HD = 128
BLOCK = 512
RSEL = 2


def exchange_kernel(*refs, axes, jobs):
    count = len(jobs)
    srcs, dsts = refs[:count], refs[count:2 * count]
    send_sems, recv_sems = refs[2 * count], refs[2 * count + 1]

    def device(axis, peer):
        return tuple(peer if name == axis else lax.axis_index(name) for name in axes)

    barrier = pltpu.get_barrier_semaphore()
    peers = 0
    for axis in sorted({job[0] for job in jobs}):
        n = lax.axis_size(axis)
        me = lax.axis_index(axis)
        for k in range(1, n):
            pl.semaphore_signal(
                barrier, inc=1, device_id=device(axis, (me + k) % n), device_id_type=MESH
            )
        peers += n - 1
    pl.semaphore_wait(barrier, peers)

    def view(ref, dim, index, n):
        size = ref.shape[dim] // n
        where = [slice(None)] * len(ref.shape)
        where[dim] = pl.ds(index * size, size)
        return ref.at[tuple(where)]

    copies = []
    for a, (axis, split_axis, concat_axis) in enumerate(jobs):
        n = lax.axis_size(axis)
        me = lax.axis_index(axis)
        own = pltpu.make_async_copy(
            view(srcs[a], split_axis, me, n), view(dsts[a], concat_axis, me, n),
            send_sems.at[a, 0],
        )
        own.start()
        copies.append(own)
        for k in range(1, n):
            peer = (me + k) % n
            copy = pltpu.make_async_remote_copy(
                src_ref=view(srcs[a], split_axis, peer, n),
                dst_ref=view(dsts[a], concat_axis, me, n),
                send_sem=send_sems.at[a, k],
                recv_sem=recv_sems.at[a, k],
                device_id=device(axis, peer),
                device_id_type=MESH,
            )
            copy.start()
            copies.append(copy)
    for copy in copies:
        copy.wait()


def exchange(arrays, jobs, axes, collective_id):
    out_shapes = []
    for x, (axis, split_axis, concat_axis) in zip(arrays, jobs):
        n = lax.axis_size(axis)
        shape = list(x.shape)
        shape[split_axis] //= n
        shape[concat_axis] *= n
        out_shapes.append(jax.ShapeDtypeStruct(tuple(shape), x.dtype))
    widest = max(lax.axis_size(job[0]) for job in jobs)
    count = len(arrays)
    return pl.pallas_call(
        functools.partial(exchange_kernel, axes=axes, jobs=tuple(jobs)),
        out_shape=tuple(out_shapes),
        in_specs=[pl.BlockSpec(memory_space=pl.ANY)] * count,
        out_specs=tuple(pl.BlockSpec(memory_space=pl.ANY) for _ in range(count)),
        scratch_shapes=[
            pltpu.SemaphoreType.DMA((count, widest)),
            pltpu.SemaphoreType.DMA((count, widest)),
        ],
        compiler_params=pltpu.CompilerParams(collective_id=collective_id, has_side_effects=True),
    )(*arrays)


def route_tables(picks, local_blocks, ctx_count):
    slots = local_blocks * RSEL
    owners = (picks // local_blocks).reshape(ctx_count, slots)
    within = (picks % local_blocks).reshape(ctx_count, slots)
    owner_ids = jnp.arange(ctx_count, dtype=jnp.int32)
    one_hot = (owners[:, :, None] == owner_ids[None, None, :]).astype(jnp.int32)
    running = jnp.cumsum(one_hot, axis=1)
    position = jnp.sum(one_hot * running, axis=-1) - 1
    return (owners, within, position)


def slot_attention(q, k, v, scale):
    scores = lax.dot_general(
        q, k, (((1,), (1,)), ((), ())), preferred_element_type=jnp.float32
    ) * scale
    row_max = jnp.max(scores, axis=1, keepdims=True)
    exponent = jnp.exp(scores - row_max)
    row_sum = jnp.sum(exponent, axis=1, keepdims=True)
    partial = jnp.dot(
        exponent.astype(jnp.bfloat16), v, preferred_element_type=jnp.float32
    )
    return row_max, row_sum, partial


def finish_kernel(
    idx_ref, q_hbm, k_hbm, v_hbm, fk_hbm, sv_hbm, y_ref,
    qv, kv, vv, fkv, fvv, wts, base, fac, stage,
    load_sems, ctx_send, ctx_recv, out_send, out_recv, q_send, q_recv,
    *, axes, heads_here, scale, capacity,
):
    n = lax.axis_size("head")
    me = lax.axis_index("head")
    m_ctx = lax.axis_size("ctx")
    c_me = lax.axis_index("ctx")
    local_blocks = qv.shape[0]
    rows = y_ref.shape[0]
    width = heads_here * HD
    per_block = BLOCK // rows
    turn = me // per_block

    def device(axis, peer):
        return tuple(peer if name == axis else lax.axis_index(name) for name in axes)

    barrier = pltpu.get_barrier_semaphore()
    for k in range(1, m_ctx):
        pl.semaphore_signal(
            barrier, inc=1, device_id=device("ctx", (c_me + k) % m_ctx), device_id_type=MESH
        )
    for k in range(1, n):
        pl.semaphore_signal(
            barrier, inc=1, device_id=device("head", (me + k) % n), device_id_type=MESH
        )
    pl.semaphore_wait(barrier, m_ctx - 1 + n - 1)

    def rows_of(ref, index):
        return ref.at[pl.ds(index * capacity, capacity)]

    v_copies = [pltpu.make_async_copy(rows_of(sv_hbm, c_me), rows_of(fvv, c_me), ctx_send.at[0])]
    v_copies[0].start()
    for k in range(1, m_ctx):
        peer = (c_me + k) % m_ctx
        copy = pltpu.make_async_remote_copy(
            src_ref=rows_of(sv_hbm, peer), dst_ref=rows_of(fvv, c_me),
            send_sem=ctx_send.at[k], recv_sem=ctx_recv.at[k],
            device_id=device("ctx", peer), device_id_type=MESH,
        )
        copy.start()
        v_copies.append(copy)

    def q_rows(owner):
        return qv.at[owner // per_block, pl.ds((owner % per_block) * rows, rows), :]

    def q_cols(peer):
        return q_hbm.at[:, pl.ds(peer * width, width)]

    loads = [pltpu.make_async_copy(q_cols(me), q_rows(me), q_send.at[0])]
    loads[0].start()
    for k in range(1, n):
        peer = (me + k) % n
        copy = pltpu.make_async_remote_copy(
            src_ref=q_cols(peer), dst_ref=q_rows(me),
            send_sem=q_send.at[k], recv_sem=q_recv.at[k],
            device_id=device("head", peer), device_id_type=MESH,
        )
        copy.start()
        loads.append(copy)
    for a, (src, dst) in enumerate(((k_hbm, kv), (v_hbm, vv), (fk_hbm, fkv))):
        load = pltpu.make_async_copy(src, dst, load_sems.at[a])
        load.start()
        loads.append(load)
    for load in loads:
        load.wait()

    def prepare(i, carry):
        j0 = idx_ref[i * RSEL]
        j1 = idx_ref[i * RSEL + 1]
        for h in range(heads_here):
            cols = pl.ds(h * HD, HD)
            q = qv[i, :, cols]
            m0, l0, acc0 = slot_attention(q, kv[i, :, cols], vv[i, :, cols], scale)
            stats = []
            for slot, j in enumerate((j0, j1)):
                scores = lax.dot_general(
                    q, fkv[j, :, cols], (((1,), (1,)), ((), ())),
                    preferred_element_type=jnp.float32,
                ) * scale
                row_max = jnp.max(scores, axis=1, keepdims=True)
                exponent = jnp.exp(scores - row_max)
                stats.append((row_max, jnp.sum(exponent, axis=1, keepdims=True)))
                wts[i, h * RSEL + slot] = exponent.astype(jnp.bfloat16)
            top = jnp.maximum(jnp.maximum(m0, stats[0][0]), stats[1][0])
            f0 = jnp.exp(m0 - top)
            f1 = jnp.exp(stats[0][0] - top)
            f2 = jnp.exp(stats[1][0] - top)
            base[i, :, cols] = acc0 * f0
            fac[i, h * 3] = f1
            fac[i, h * 3 + 1] = f2
            fac[i, h * 3 + 2] = l0 * f0 + stats[0][1] * f1 + stats[1][1] * f2
        return carry

    lax.fori_loop(0, local_blocks, prepare, 0)
    for copy in v_copies:
        copy.wait()

    mine = y_ref.at[:, pl.ds(me * width, width)]

    def piece(b, r):
        return stage.at[b, pl.ds(r * rows, rows), :]

    def remote(b, r, dest):
        return pltpu.make_async_remote_copy(
            src_ref=piece(b, r), dst_ref=mine,
            send_sem=out_send.at[b * per_block + r], recv_sem=out_recv.at[me],
            device_id=device("head", dest), device_id_type=MESH,
        )

    def own(b, r):
        return pltpu.make_async_copy(piece(b, r), mine, out_send.at[b * per_block + r])

    def send(b):
        for r in range(per_block):
            dest = b * per_block + r

            @pl.when(dest == me)
            def _():
                own(b, r).start()

            @pl.when(dest != me)
            def _():
                remote(b, r, dest).start()

    def finish(b):
        for r in range(per_block):
            dest = b * per_block + r

            @pl.when(dest == me)
            def _():
                own(b, r).wait()

            @pl.when(dest != me)
            def _():
                remote(b, r, dest).wait_send()

    def complete(t, carry):
        i = (t + turn) % local_blocks
        j0 = idx_ref[i * RSEL]
        j1 = idx_ref[i * RSEL + 1]
        for h in range(heads_here):
            cols = pl.ds(h * HD, HD)
            p1 = jnp.dot(wts[i, h * RSEL], fvv[j0, :, cols], preferred_element_type=jnp.float32)
            p2 = jnp.dot(
                wts[i, h * RSEL + 1], fvv[j1, :, cols], preferred_element_type=jnp.float32
            )
            numer = base[i, :, cols] + p1 * fac[i, h * 3] + p2 * fac[i, h * 3 + 1]
            stage[i, :, cols] = (numer / fac[i, h * 3 + 2]).astype(stage.dtype)

        @pl.when(t >= 1)
        def _():
            send((t - 1 + turn) % local_blocks)

        return carry

    lax.fori_loop(0, local_blocks, complete, 0)

    def settle(t, carry):
        finish((t + turn) % local_blocks)
        return carry

    lax.fori_loop(0, local_blocks - 1, settle, 0)
    last = (local_blocks - 1 + turn) % local_blocks
    send(last)
    finish(last)
    for sender in range(n):

        @pl.when(sender != me)
        def _():
            pltpu.make_async_remote_copy(
                src_ref=piece(0, 0), dst_ref=mine,
                send_sem=out_send.at[0], recv_sem=out_recv.at[sender],
                device_id=device("head", sender), device_id_type=MESH,
            ).wait_recv()


def finish_attention(
    far_index, queries, k_blocks, v_blocks, far_k, send_v, scale, axes, tok_rows, capacity
):
    local_blocks, _, width = k_blocks.shape
    heads_here = width // HD
    n = HEADS // heads_here
    m_ctx = send_v.shape[0] // capacity
    kernel = functools.partial(
        finish_kernel, axes=axes, heads_here=heads_here, scale=scale, capacity=capacity
    )
    anywhere = pl.BlockSpec(memory_space=pl.ANY)
    flops = local_blocks * heads_here * 3 * 4 * BLOCK * BLOCK * HD
    return pl.pallas_call(
        kernel,
        out_shape=jax.ShapeDtypeStruct((tok_rows, n * width), jnp.bfloat16),
        in_specs=[pl.BlockSpec(memory_space=pltpu.SMEM)] + [anywhere] * 5,
        out_specs=anywhere,
        scratch_shapes=[
            pltpu.VMEM(k_blocks.shape, jnp.bfloat16),
            pltpu.VMEM(k_blocks.shape, jnp.bfloat16),
            pltpu.VMEM(v_blocks.shape, jnp.bfloat16),
            pltpu.VMEM(far_k.shape, jnp.bfloat16),
            pltpu.VMEM(send_v.shape, jnp.bfloat16),
            pltpu.VMEM((local_blocks, heads_here * RSEL, BLOCK, BLOCK), jnp.bfloat16),
            pltpu.VMEM((local_blocks, BLOCK, width), jnp.float32),
            pltpu.VMEM((local_blocks, heads_here * 3, BLOCK, 1), jnp.float32),
            pltpu.VMEM((local_blocks, BLOCK, width), jnp.bfloat16),
            pltpu.SemaphoreType.DMA((4,)),
            pltpu.SemaphoreType.DMA((m_ctx,)),
            pltpu.SemaphoreType.DMA((m_ctx,)),
            pltpu.SemaphoreType.DMA((local_blocks * (BLOCK // tok_rows),)),
            pltpu.SemaphoreType.DMA((n,)),
            pltpu.SemaphoreType.DMA((n,)),
            pltpu.SemaphoreType.DMA((n,)),
        ],
        compiler_params=pltpu.CompilerParams(
            collective_id=2, has_side_effects=True, vmem_limit_bytes=60 * 1024 * 1024
        ),
        cost_estimate=pl.CostEstimate(
            flops=flops,
            transcendentals=local_blocks * heads_here * 3 * BLOCK * BLOCK,
            bytes_accessed=local_blocks * BLOCK * width * 2 * 8,
        ),
    )(far_index, queries, k_blocks, v_blocks, far_k, send_v)


def local(queries, keys, values, picks, axes):
    head_count = lax.axis_size("head")
    ctx_count = lax.axis_size("ctx")
    my_index = lax.axis_index("ctx")
    heads_here = HEADS // head_count
    width = heads_here * HD
    tok_rows = queries.shape[0]
    score_scale = 1.0 / math.sqrt(HD)
    head_in = ("head", 1, 0)
    ctx_move = ("ctx", 0, 0)
    k_heads, v_heads = exchange((keys, values), (head_in, head_in), axes, collective_id=0)
    local_blocks = k_heads.shape[0] // BLOCK
    k_blocks = k_heads.reshape(local_blocks, BLOCK, width)

    capacity = (local_blocks * RSEL + ctx_count - 1) // ctx_count + 1
    owners, within, position = route_tables(picks, local_blocks, ctx_count)
    mine_owner = lax.dynamic_index_in_dim(owners, my_index, 0, keepdims=False)
    mine_pos = lax.dynamic_index_in_dim(position, my_index, 0, keepdims=False)
    slot_ids = jnp.arange(capacity, dtype=jnp.int32)
    asked = (owners == my_index)[:, :, None] & (position[:, :, None] == slot_ids[None, None, :])
    wanted = jnp.sum(asked.astype(jnp.int32) * within[:, :, None], axis=1)
    far_index = (mine_owner * capacity + mine_pos).astype(jnp.int32)

    send_k = k_blocks[wanted.reshape(-1)]
    v_blocks = v_heads.reshape(local_blocks, BLOCK, width)
    send_v = v_blocks[wanted.reshape(-1)]
    (far_k,) = exchange((send_k,), (ctx_move,), axes, collective_id=1)
    return finish_attention(
        far_index, queries, k_blocks, v_blocks, far_k, send_v, score_scale, axes, tok_rows,
        capacity,
    )


def solution(mesh):
    placed = (P(("ctx", "head"), None), P(("ctx", "head"), None), P(("ctx", "head"), None), P())
    return jax.shard_map(
        functools.partial(local, axes=tuple(mesh.axis_names)), mesh=mesh, in_specs=placed, out_specs=P(("ctx", "head"), None), check_vma=False
    )
```

```python
import functools
import math

import jax
import jax.numpy as jnp
from jax import lax
from jax.experimental import pallas as pl
from jax.experimental.pallas import tpu as pltpu
from jax.sharding import PartitionSpec as P

MESH = pl.DeviceIdType.MESH

HEADS = 16
HD = 128
BLOCK = 512
RSEL = 2


def exchange_kernel(*refs, axes, jobs):
    count = len(jobs)
    srcs, dsts = refs[:count], refs[count:2 * count]
    send_sems, recv_sems = refs[2 * count], refs[2 * count + 1]

    def device(axis, peer):
        return tuple(peer if name == axis else lax.axis_index(name) for name in axes)

    barrier = pltpu.get_barrier_semaphore()
    peers = 0
    for axis in sorted({job[0] for job in jobs}):
        n = lax.axis_size(axis)
        me = lax.axis_index(axis)
        for k in range(1, n):
            pl.semaphore_signal(
                barrier, inc=1, device_id=device(axis, (me + k) % n), device_id_type=MESH
            )
        peers += n - 1
    pl.semaphore_wait(barrier, peers)

    def view(ref, dim, index, n):
        size = ref.shape[dim] // n
        where = [slice(None)] * len(ref.shape)
        where[dim] = pl.ds(index * size, size)
        return ref.at[tuple(where)]

    copies = []
    halves = []
    for a, (axis, split_axis, concat_axis, parity) in enumerate(jobs):
        n = lax.axis_size(axis)
        me = lax.axis_index(axis)
        if parity is None:
            own = pltpu.make_async_copy(
                view(srcs[a], split_axis, me, n), view(dsts[a], concat_axis, me, n),
                send_sems.at[a, 0],
            )
            own.start()
            copies.append(own)
            for k in range(1, n):
                peer = (me + k) % n
                copy = pltpu.make_async_remote_copy(
                    src_ref=view(srcs[a], split_axis, peer, n),
                    dst_ref=view(dsts[a], concat_axis, me, n),
                    send_sem=send_sems.at[a, k],
                    recv_sem=recv_sems.at[a, k],
                    device_id=device(axis, peer),
                    device_id_type=MESH,
                )
                copy.start()
                copies.append(copy)
            continue
        half = n // 2
        slot = me // 2

        def own_half(a=a, n=n, me=me, slot=slot, half=half, split_axis=split_axis,
                     concat_axis=concat_axis):
            return pltpu.make_async_copy(
                view(srcs[a], split_axis, me, n), view(dsts[a], concat_axis, slot, half),
                send_sems.at[a, 0],
            )

        def out_half(k, a=a, n=n, me=me, slot=slot, half=half, axis=axis,
                     split_axis=split_axis, concat_axis=concat_axis):
            peer = (me + k) % n
            return pltpu.make_async_remote_copy(
                src_ref=view(srcs[a], split_axis, peer, n),
                dst_ref=view(dsts[a], concat_axis, slot, half),
                send_sem=send_sems.at[a, k],
                recv_sem=recv_sems.at[a, slot],
                device_id=device(axis, peer),
                device_id_type=MESH,
            )

        @pl.when(me % 2 == parity)
        def _():
            own_half().start()
            for k in range(1, n):
                out_half(k).start()

        halves.append((me, n, parity, own_half, out_half, a))
    for copy in copies:
        copy.wait()
    for me, n, parity, own_half, out_half, a in halves:

        @pl.when(me % 2 == parity)
        def _():
            own_half().wait()
            for k in range(1, n):
                out_half(k).wait_send()

        for j in range(n // 2):
            sender = 2 * j + parity

            @pl.when(sender != me)
            def _():
                pltpu.make_async_remote_copy(
                    src_ref=view(srcs[a], jobs[a][1], 0, n),
                    dst_ref=view(dsts[a], jobs[a][2], j, n // 2),
                    send_sem=send_sems.at[a, 0],
                    recv_sem=recv_sems.at[a, j],
                    device_id=device(jobs[a][0], sender),
                    device_id_type=MESH,
                ).wait_recv()


def exchange(arrays, jobs, axes, collective_id):
    out_shapes = []
    for x, (axis, split_axis, concat_axis, parity) in zip(arrays, jobs):
        n = lax.axis_size(axis)
        shape = list(x.shape)
        shape[split_axis] //= n
        shape[concat_axis] *= n if parity is None else n // 2
        out_shapes.append(jax.ShapeDtypeStruct(tuple(shape), x.dtype))
    widest = max(lax.axis_size(job[0]) for job in jobs)
    count = len(arrays)
    return pl.pallas_call(
        functools.partial(exchange_kernel, axes=axes, jobs=tuple(jobs)),
        out_shape=tuple(out_shapes),
        in_specs=[pl.BlockSpec(memory_space=pl.ANY)] * count,
        out_specs=tuple(pl.BlockSpec(memory_space=pl.ANY) for _ in range(count)),
        scratch_shapes=[
            pltpu.SemaphoreType.DMA((count, widest)),
            pltpu.SemaphoreType.DMA((count, widest)),
        ],
        compiler_params=pltpu.CompilerParams(collective_id=collective_id, has_side_effects=True),
    )(*arrays)


def route_tables(picks, local_blocks, ctx_count):
    slots = local_blocks * RSEL
    owners = (picks // local_blocks).reshape(ctx_count, slots)
    within = (picks % local_blocks).reshape(ctx_count, slots)
    owner_ids = jnp.arange(ctx_count, dtype=jnp.int32)
    one_hot = (owners[:, :, None] == owner_ids[None, None, :]).astype(jnp.int32)
    running = jnp.cumsum(one_hot, axis=1)
    position = jnp.sum(one_hot * running, axis=-1) - 1
    return (owners, within, position)


def slot_attention(q, k, v, scale):
    scores = lax.dot_general(
        q, k, (((1,), (1,)), ((), ())), preferred_element_type=jnp.float32
    ) * scale
    row_max = jnp.max(scores, axis=1, keepdims=True)
    exponent = jnp.exp(scores - row_max)
    row_sum = jnp.sum(exponent, axis=1, keepdims=True)
    partial = jnp.dot(
        exponent.astype(jnp.bfloat16), v, preferred_element_type=jnp.float32
    )
    return row_max, row_sum, partial


def finish_kernel(
    idx_ref, q_hbm, ka_hbm, kb_hbm, v_hbm, fka_hbm, fkb_hbm, sv_hbm, y_ref,
    qv, kv, vv, fkv, fvv, wts, base, fac, stage,
    load_sems, ctx_send, ctx_recv, out_send, out_recv, q_send, q_recv,
    *, axes, heads_here, scale, capacity,
):
    n = lax.axis_size("head")
    me = lax.axis_index("head")
    m_ctx = lax.axis_size("ctx")
    c_me = lax.axis_index("ctx")
    local_blocks = qv.shape[0]
    rows = y_ref.shape[0]
    width = heads_here * HD
    per_block = BLOCK // rows
    turn = me // per_block

    def device(axis, peer):
        return tuple(peer if name == axis else lax.axis_index(name) for name in axes)

    barrier = pltpu.get_barrier_semaphore()
    for k in range(1, m_ctx):
        pl.semaphore_signal(
            barrier, inc=1, device_id=device("ctx", (c_me + k) % m_ctx), device_id_type=MESH
        )
    for k in range(1, n):
        pl.semaphore_signal(
            barrier, inc=1, device_id=device("head", (me + k) % n), device_id_type=MESH
        )
    pl.semaphore_wait(barrier, m_ctx - 1 + n - 1)

    def rows_of(ref, index):
        return ref.at[pl.ds(index * capacity, capacity)]

    v_copies = [pltpu.make_async_copy(rows_of(sv_hbm, c_me), rows_of(fvv, c_me), ctx_send.at[0])]
    v_copies[0].start()
    for k in range(1, m_ctx):
        peer = (c_me + k) % m_ctx
        copy = pltpu.make_async_remote_copy(
            src_ref=rows_of(sv_hbm, peer), dst_ref=rows_of(fvv, c_me),
            send_sem=ctx_send.at[k], recv_sem=ctx_recv.at[k],
            device_id=device("ctx", peer), device_id_type=MESH,
        )
        copy.start()
        v_copies.append(copy)

    def q_rows(owner):
        return qv.at[owner // per_block, pl.ds((owner % per_block) * rows, rows), :]

    def q_cols(peer):
        return q_hbm.at[:, pl.ds(peer * width, width)]

    loads = [pltpu.make_async_copy(q_cols(me), q_rows(me), q_send.at[0])]
    loads[0].start()
    for k in range(1, n):
        peer = (me + k) % n
        copy = pltpu.make_async_remote_copy(
            src_ref=q_cols(peer), dst_ref=q_rows(me),
            send_sem=q_send.at[k], recv_sem=q_recv.at[k],
            device_id=device("head", peer), device_id_type=MESH,
        )
        copy.start()
        loads.append(copy)
    top_rows = pl.ds(0, BLOCK // 2)
    low_rows = pl.ds(BLOCK // 2, BLOCK // 2)
    pairs = (
        (ka_hbm, kv.at[:, top_rows, :]), (kb_hbm, kv.at[:, low_rows, :]), (v_hbm, vv),
        (fka_hbm, fkv.at[:, top_rows, :]), (fkb_hbm, fkv.at[:, low_rows, :]),
    )
    for a, (src, dst) in enumerate(pairs):
        load = pltpu.make_async_copy(src, dst, load_sems.at[a])
        load.start()
        loads.append(load)
    for load in loads:
        load.wait()

    def prepare(i, carry):
        j0 = idx_ref[i * RSEL]
        j1 = idx_ref[i * RSEL + 1]
        for h in range(heads_here):
            cols = pl.ds(h * HD, HD)
            q = qv[i, :, cols]
            m0, l0, acc0 = slot_attention(q, kv[i, :, cols], vv[i, :, cols], scale)
            stats = []
            for slot, j in enumerate((j0, j1)):
                scores = lax.dot_general(
                    q, fkv[j, :, cols], (((1,), (1,)), ((), ())),
                    preferred_element_type=jnp.float32,
                ) * scale
                row_max = jnp.max(scores, axis=1, keepdims=True)
                exponent = jnp.exp(scores - row_max)
                stats.append((row_max, jnp.sum(exponent, axis=1, keepdims=True)))
                wts[i, h * RSEL + slot] = exponent.astype(jnp.bfloat16)
            top = jnp.maximum(jnp.maximum(m0, stats[0][0]), stats[1][0])
            f0 = jnp.exp(m0 - top)
            f1 = jnp.exp(stats[0][0] - top)
            f2 = jnp.exp(stats[1][0] - top)
            base[i, :, cols] = acc0 * f0
            fac[i, h * 3] = f1
            fac[i, h * 3 + 1] = f2
            fac[i, h * 3 + 2] = l0 * f0 + stats[0][1] * f1 + stats[1][1] * f2
        return carry

    lax.fori_loop(0, local_blocks, prepare, 0)
    for copy in v_copies:
        copy.wait()

    mine = y_ref.at[:, pl.ds(me * width, width)]

    def piece(b, r):
        return stage.at[b, pl.ds(r * rows, rows), :]

    def remote(b, r, dest):
        return pltpu.make_async_remote_copy(
            src_ref=piece(b, r), dst_ref=mine,
            send_sem=out_send.at[b * per_block + r], recv_sem=out_recv.at[me],
            device_id=device("head", dest), device_id_type=MESH,
        )

    def own(b, r):
        return pltpu.make_async_copy(piece(b, r), mine, out_send.at[b * per_block + r])

    def send(b):
        for r in range(per_block):
            dest = b * per_block + r

            @pl.when(dest == me)
            def _():
                own(b, r).start()

            @pl.when(dest != me)
            def _():
                remote(b, r, dest).start()

    def finish(b):
        for r in range(per_block):
            dest = b * per_block + r

            @pl.when(dest == me)
            def _():
                own(b, r).wait()

            @pl.when(dest != me)
            def _():
                remote(b, r, dest).wait_send()

    def complete(t, carry):
        i = (t + turn) % local_blocks
        j0 = idx_ref[i * RSEL]
        j1 = idx_ref[i * RSEL + 1]
        for h in range(heads_here):
            cols = pl.ds(h * HD, HD)
            p1 = jnp.dot(wts[i, h * RSEL], fvv[j0, :, cols], preferred_element_type=jnp.float32)
            p2 = jnp.dot(
                wts[i, h * RSEL + 1], fvv[j1, :, cols], preferred_element_type=jnp.float32
            )
            numer = base[i, :, cols] + p1 * fac[i, h * 3] + p2 * fac[i, h * 3 + 1]
            stage[i, :, cols] = (numer / fac[i, h * 3 + 2]).astype(stage.dtype)

        @pl.when(t >= 1)
        def _():
            send((t - 1 + turn) % local_blocks)

        return carry

    lax.fori_loop(0, local_blocks, complete, 0)

    def settle(t, carry):
        finish((t + turn) % local_blocks)
        return carry

    lax.fori_loop(0, local_blocks - 1, settle, 0)
    last = (local_blocks - 1 + turn) % local_blocks
    send(last)
    finish(last)
    for sender in range(n):

        @pl.when(sender != me)
        def _():
            pltpu.make_async_remote_copy(
                src_ref=piece(0, 0), dst_ref=mine,
                send_sem=out_send.at[0], recv_sem=out_recv.at[sender],
                device_id=device("head", sender), device_id_type=MESH,
            ).wait_recv()


def finish_attention(
    far_index, queries, k_parts, v_blocks, far_parts, send_v, scale, axes, tok_rows, capacity
):
    local_blocks, _, width = v_blocks.shape
    heads_here = width // HD
    n = HEADS // heads_here
    m_ctx = send_v.shape[0] // capacity
    kernel = functools.partial(
        finish_kernel, axes=axes, heads_here=heads_here, scale=scale, capacity=capacity
    )
    anywhere = pl.BlockSpec(memory_space=pl.ANY)
    flops = local_blocks * heads_here * 3 * 4 * BLOCK * BLOCK * HD
    return pl.pallas_call(
        kernel,
        out_shape=jax.ShapeDtypeStruct((tok_rows, n * width), jnp.bfloat16),
        in_specs=[pl.BlockSpec(memory_space=pltpu.SMEM)] + [anywhere] * 7,
        out_specs=anywhere,
        scratch_shapes=[
            pltpu.VMEM(v_blocks.shape, jnp.bfloat16),
            pltpu.VMEM(v_blocks.shape, jnp.bfloat16),
            pltpu.VMEM(v_blocks.shape, jnp.bfloat16),
            pltpu.VMEM(send_v.shape, jnp.bfloat16),
            pltpu.VMEM(send_v.shape, jnp.bfloat16),
            pltpu.VMEM((local_blocks, heads_here * RSEL, BLOCK, BLOCK), jnp.bfloat16),
            pltpu.VMEM((local_blocks, BLOCK, width), jnp.float32),
            pltpu.VMEM((local_blocks, heads_here * 3, BLOCK, 1), jnp.float32),
            pltpu.VMEM((local_blocks, BLOCK, width), jnp.bfloat16),
            pltpu.SemaphoreType.DMA((6,)),
            pltpu.SemaphoreType.DMA((m_ctx,)),
            pltpu.SemaphoreType.DMA((m_ctx,)),
            pltpu.SemaphoreType.DMA((local_blocks * (BLOCK // tok_rows),)),
            pltpu.SemaphoreType.DMA((n,)),
            pltpu.SemaphoreType.DMA((n,)),
            pltpu.SemaphoreType.DMA((n,)),
        ],
        compiler_params=pltpu.CompilerParams(
            collective_id=2, has_side_effects=True, vmem_limit_bytes=60 * 1024 * 1024
        ),
        cost_estimate=pl.CostEstimate(
            flops=flops,
            transcendentals=local_blocks * heads_here * 3 * BLOCK * BLOCK,
            bytes_accessed=local_blocks * BLOCK * width * 2 * 8,
        ),
    )(far_index, queries, *k_parts, v_blocks, *far_parts, send_v)


def local(queries, keys, values, picks, axes):
    head_count = lax.axis_size("head")
    ctx_count = lax.axis_size("ctx")
    my_index = lax.axis_index("ctx")
    heads_here = HEADS // head_count
    width = heads_here * HD
    tok_rows = queries.shape[0]
    score_scale = 1.0 / math.sqrt(HD)
    head_in = ("head", 1, 0, None)
    ctx_move = ("ctx", 0, 0, None)
    (k_even,) = exchange((keys,), (("head", 1, 0, 0),), axes, collective_id=0)
    local_blocks = k_even.shape[0] * 2 // BLOCK
    half_rows = BLOCK // 2
    k_even = k_even.reshape(local_blocks, half_rows, width)

    capacity = (local_blocks * RSEL + ctx_count - 1) // ctx_count + 1
    owners, within, position = route_tables(picks, local_blocks, ctx_count)
    mine_owner = lax.dynamic_index_in_dim(owners, my_index, 0, keepdims=False)
    mine_pos = lax.dynamic_index_in_dim(position, my_index, 0, keepdims=False)
    slot_ids = jnp.arange(capacity, dtype=jnp.int32)
    asked = (owners == my_index)[:, :, None] & (position[:, :, None] == slot_ids[None, None, :])
    wanted = jnp.sum(asked.astype(jnp.int32) * within[:, :, None], axis=1)
    far_index = (mine_owner * capacity + mine_pos).astype(jnp.int32)

    pick = wanted.reshape(-1)
    far_even, k_odd, v_heads = exchange(
        (k_even[pick], keys, values), (ctx_move, ("head", 1, 0, 1), head_in), axes,
        collective_id=1,
    )
    k_odd = k_odd.reshape(local_blocks, half_rows, width)
    (far_odd,) = exchange((k_odd[pick],), (ctx_move,), axes, collective_id=3)
    v_blocks = v_heads.reshape(local_blocks, BLOCK, width)
    send_v = v_blocks[pick]
    return finish_attention(
        far_index, queries, (k_even, k_odd), v_blocks, (far_even, far_odd), send_v, score_scale,
        axes, tok_rows,
        capacity,
    )


def solution(mesh):
    placed = (P(("ctx", "head"), None), P(("ctx", "head"), None), P(("ctx", "head"), None), P())
    return jax.shard_map(
        functools.partial(local, axes=tuple(mesh.axis_names)), mesh=mesh, in_specs=placed, out_specs=P(("ctx", "head"), None), check_vma=False
    )
```

```python
import functools
import math

import jax
import jax.numpy as jnp
from jax import lax
from jax.experimental import pallas as pl
from jax.experimental.pallas import tpu as pltpu
from jax.sharding import PartitionSpec as P

MESH = pl.DeviceIdType.MESH

HEADS = 16
HD = 128
BLOCK = 512
RSEL = 2


def exchange_kernel(*refs, axes, jobs):
    count = len(jobs)
    srcs, dsts = refs[:count], refs[count:2 * count]
    send_sems, recv_sems = refs[2 * count], refs[2 * count + 1]

    def device(axis, peer):
        return tuple(peer if name == axis else lax.axis_index(name) for name in axes)

    barrier = pltpu.get_barrier_semaphore()
    peers = 0
    for axis in sorted({job[0] for job in jobs}):
        n = lax.axis_size(axis)
        me = lax.axis_index(axis)
        for k in range(1, n):
            pl.semaphore_signal(
                barrier, inc=1, device_id=device(axis, (me + k) % n), device_id_type=MESH
            )
        peers += n - 1
    pl.semaphore_wait(barrier, peers)

    def view(ref, dim, index, n):
        size = ref.shape[dim] // n
        where = [slice(None)] * len(ref.shape)
        where[dim] = pl.ds(index * size, size)
        return ref.at[tuple(where)]

    copies = []
    halves = []
    for a, (axis, split_axis, concat_axis, parity) in enumerate(jobs):
        n = lax.axis_size(axis)
        me = lax.axis_index(axis)
        if parity is None:
            own = pltpu.make_async_copy(
                view(srcs[a], split_axis, me, n), view(dsts[a], concat_axis, me, n),
                send_sems.at[a, 0],
            )
            own.start()
            copies.append(own)
            for k in range(1, n):
                peer = (me + k) % n
                copy = pltpu.make_async_remote_copy(
                    src_ref=view(srcs[a], split_axis, peer, n),
                    dst_ref=view(dsts[a], concat_axis, me, n),
                    send_sem=send_sems.at[a, k],
                    recv_sem=recv_sems.at[a, k],
                    device_id=device(axis, peer),
                    device_id_type=MESH,
                )
                copy.start()
                copies.append(copy)
            continue
        half = n // 2
        slot = me // 2

        def own_half(a=a, n=n, me=me, slot=slot, half=half, split_axis=split_axis,
                     concat_axis=concat_axis):
            return pltpu.make_async_copy(
                view(srcs[a], split_axis, me, n), view(dsts[a], concat_axis, slot, half),
                send_sems.at[a, 0],
            )

        def out_half(k, a=a, n=n, me=me, slot=slot, half=half, axis=axis,
                     split_axis=split_axis, concat_axis=concat_axis):
            peer = (me + k) % n
            return pltpu.make_async_remote_copy(
                src_ref=view(srcs[a], split_axis, peer, n),
                dst_ref=view(dsts[a], concat_axis, slot, half),
                send_sem=send_sems.at[a, k],
                recv_sem=recv_sems.at[a, slot],
                device_id=device(axis, peer),
                device_id_type=MESH,
            )

        @pl.when(me % 2 == parity)
        def _():
            own_half().start()
            for k in range(1, n):
                out_half(k).start()

        halves.append((me, n, parity, own_half, out_half, a))
    for copy in copies:
        copy.wait()
    for me, n, parity, own_half, out_half, a in halves:

        @pl.when(me % 2 == parity)
        def _():
            own_half().wait()
            for k in range(1, n):
                out_half(k).wait_send()

        for j in range(n // 2):
            sender = 2 * j + parity

            @pl.when(sender != me)
            def _():
                pltpu.make_async_remote_copy(
                    src_ref=view(srcs[a], jobs[a][1], 0, n),
                    dst_ref=view(dsts[a], jobs[a][2], j, n // 2),
                    send_sem=send_sems.at[a, 0],
                    recv_sem=recv_sems.at[a, j],
                    device_id=device(jobs[a][0], sender),
                    device_id_type=MESH,
                ).wait_recv()


def exchange(arrays, jobs, axes, collective_id):
    out_shapes = []
    for x, (axis, split_axis, concat_axis, parity) in zip(arrays, jobs):
        n = lax.axis_size(axis)
        shape = list(x.shape)
        shape[split_axis] //= n
        shape[concat_axis] *= n if parity is None else n // 2
        out_shapes.append(jax.ShapeDtypeStruct(tuple(shape), x.dtype))
    widest = max(lax.axis_size(job[0]) for job in jobs)
    count = len(arrays)
    return pl.pallas_call(
        functools.partial(exchange_kernel, axes=axes, jobs=tuple(jobs)),
        out_shape=tuple(out_shapes),
        in_specs=[pl.BlockSpec(memory_space=pl.ANY)] * count,
        out_specs=tuple(pl.BlockSpec(memory_space=pl.ANY) for _ in range(count)),
        scratch_shapes=[
            pltpu.SemaphoreType.DMA((count, widest)),
            pltpu.SemaphoreType.DMA((count, widest)),
        ],
        compiler_params=pltpu.CompilerParams(collective_id=collective_id, has_side_effects=True),
    )(*arrays)


def pick_rows(table, pick):
    count = table.shape[0]
    flat = table.reshape(count, -1)
    chosen = (pick[:, None] == jnp.arange(count, dtype=pick.dtype)[None, :]).astype(table.dtype)
    out = jnp.dot(chosen, flat, preferred_element_type=jnp.float32).astype(table.dtype)
    return out.reshape((pick.shape[0],) + table.shape[1:])


def route_tables(picks, local_blocks, ctx_count):
    slots = local_blocks * RSEL
    owners = (picks // local_blocks).reshape(ctx_count, slots)
    within = (picks % local_blocks).reshape(ctx_count, slots)
    owner_ids = jnp.arange(ctx_count, dtype=jnp.int32)
    one_hot = (owners[:, :, None] == owner_ids[None, None, :]).astype(jnp.int32)
    running = jnp.cumsum(one_hot, axis=1)
    position = jnp.sum(one_hot * running, axis=-1) - 1
    return (owners, within, position)


def slot_attention(q, k, v, scale):
    scores = lax.dot_general(
        q, k, (((1,), (1,)), ((), ())), preferred_element_type=jnp.float32
    ) * scale
    row_max = jnp.max(scores, axis=1, keepdims=True)
    exponent = jnp.exp(scores - row_max)
    row_sum = jnp.sum(exponent, axis=1, keepdims=True)
    partial = jnp.dot(
        exponent.astype(jnp.bfloat16), v, preferred_element_type=jnp.float32
    )
    return row_max, row_sum, partial


def finish_kernel(
    idx_ref, q_hbm, ka_hbm, kb_hbm, v_hbm, fka_hbm, fkb_hbm, sv_hbm, y_ref,
    qv, kv, vv, fkv, fvv, wts, base, fac, stage,
    load_sems, ctx_send, ctx_recv, out_send, out_recv, q_send, q_recv,
    *, axes, heads_here, scale, capacity,
):
    n = lax.axis_size("head")
    me = lax.axis_index("head")
    m_ctx = lax.axis_size("ctx")
    c_me = lax.axis_index("ctx")
    local_blocks = qv.shape[0]
    rows = y_ref.shape[0]
    width = heads_here * HD
    per_block = BLOCK // rows
    turn = me // per_block

    def device(axis, peer):
        return tuple(peer if name == axis else lax.axis_index(name) for name in axes)

    barrier = pltpu.get_barrier_semaphore()
    for k in range(1, m_ctx):
        pl.semaphore_signal(
            barrier, inc=1, device_id=device("ctx", (c_me + k) % m_ctx), device_id_type=MESH
        )
    for k in range(1, n):
        pl.semaphore_signal(
            barrier, inc=1, device_id=device("head", (me + k) % n), device_id_type=MESH
        )
    pl.semaphore_wait(barrier, m_ctx - 1 + n - 1)

    def rows_of(ref, index):
        return ref.at[pl.ds(index * capacity, capacity)]

    v_copies = [pltpu.make_async_copy(rows_of(sv_hbm, c_me), rows_of(fvv, c_me), ctx_send.at[0])]
    v_copies[0].start()
    for k in range(1, m_ctx):
        peer = (c_me + k) % m_ctx
        copy = pltpu.make_async_remote_copy(
            src_ref=rows_of(sv_hbm, peer), dst_ref=rows_of(fvv, c_me),
            send_sem=ctx_send.at[k], recv_sem=ctx_recv.at[k],
            device_id=device("ctx", peer), device_id_type=MESH,
        )
        copy.start()
        v_copies.append(copy)

    def q_rows(owner):
        return qv.at[owner // per_block, pl.ds((owner % per_block) * rows, rows), :]

    def q_cols(peer):
        return q_hbm.at[:, pl.ds(peer * width, width)]

    loads = [pltpu.make_async_copy(q_cols(me), q_rows(me), q_send.at[0])]
    loads[0].start()
    for k in range(1, n):
        peer = (me + k) % n
        copy = pltpu.make_async_remote_copy(
            src_ref=q_cols(peer), dst_ref=q_rows(me),
            send_sem=q_send.at[k], recv_sem=q_recv.at[k],
            device_id=device("head", peer), device_id_type=MESH,
        )
        copy.start()
        loads.append(copy)
    top_rows = pl.ds(0, BLOCK // 2)
    low_rows = pl.ds(BLOCK // 2, BLOCK // 2)
    pairs = (
        (ka_hbm, kv.at[:, top_rows, :]), (kb_hbm, kv.at[:, low_rows, :]), (v_hbm, vv),
        (fka_hbm, fkv.at[:, top_rows, :]), (fkb_hbm, fkv.at[:, low_rows, :]),
    )
    for a, (src, dst) in enumerate(pairs):
        load = pltpu.make_async_copy(src, dst, load_sems.at[a])
        load.start()
        loads.append(load)
    for load in loads:
        load.wait()

    def prepare(i, carry):
        j0 = idx_ref[i * RSEL]
        j1 = idx_ref[i * RSEL + 1]
        for h in range(heads_here):
            cols = pl.ds(h * HD, HD)
            q = qv[i, :, cols]
            m0, l0, acc0 = slot_attention(q, kv[i, :, cols], vv[i, :, cols], scale)
            stats = []
            for slot, j in enumerate((j0, j1)):
                scores = lax.dot_general(
                    q, fkv[j, :, cols], (((1,), (1,)), ((), ())),
                    preferred_element_type=jnp.float32,
                ) * scale
                row_max = jnp.max(scores, axis=1, keepdims=True)
                exponent = jnp.exp(scores - row_max)
                stats.append((row_max, jnp.sum(exponent, axis=1, keepdims=True)))
                wts[i, h * RSEL + slot] = exponent.astype(jnp.bfloat16)
            top = jnp.maximum(jnp.maximum(m0, stats[0][0]), stats[1][0])
            f0 = jnp.exp(m0 - top)
            f1 = jnp.exp(stats[0][0] - top)
            f2 = jnp.exp(stats[1][0] - top)
            base[i, :, cols] = acc0 * f0
            fac[i, h * 3] = f1
            fac[i, h * 3 + 1] = f2
            fac[i, h * 3 + 2] = l0 * f0 + stats[0][1] * f1 + stats[1][1] * f2
        return carry

    lax.fori_loop(0, local_blocks, prepare, 0)
    for copy in v_copies:
        copy.wait()

    mine = y_ref.at[:, pl.ds(me * width, width)]

    def piece(b, r):
        return stage.at[b, pl.ds(r * rows, rows), :]

    def remote(b, r, dest):
        return pltpu.make_async_remote_copy(
            src_ref=piece(b, r), dst_ref=mine,
            send_sem=out_send.at[b * per_block + r], recv_sem=out_recv.at[me],
            device_id=device("head", dest), device_id_type=MESH,
        )

    def own(b, r):
        return pltpu.make_async_copy(piece(b, r), mine, out_send.at[b * per_block + r])

    def send(b):
        for r in range(per_block):
            dest = b * per_block + r

            @pl.when(dest == me)
            def _():
                own(b, r).start()

            @pl.when(dest != me)
            def _():
                remote(b, r, dest).start()

    def finish(b):
        for r in range(per_block):
            dest = b * per_block + r

            @pl.when(dest == me)
            def _():
                own(b, r).wait()

            @pl.when(dest != me)
            def _():
                remote(b, r, dest).wait_send()

    def complete(t, carry):
        i = (t + turn) % local_blocks
        j0 = idx_ref[i * RSEL]
        j1 = idx_ref[i * RSEL + 1]
        for h in range(heads_here):
            cols = pl.ds(h * HD, HD)
            p1 = jnp.dot(wts[i, h * RSEL], fvv[j0, :, cols], preferred_element_type=jnp.float32)
            p2 = jnp.dot(
                wts[i, h * RSEL + 1], fvv[j1, :, cols], preferred_element_type=jnp.float32
            )
            numer = base[i, :, cols] + p1 * fac[i, h * 3] + p2 * fac[i, h * 3 + 1]
            stage[i, :, cols] = (numer / fac[i, h * 3 + 2]).astype(stage.dtype)

        @pl.when(t >= 1)
        def _():
            send((t - 1 + turn) % local_blocks)

        return carry

    lax.fori_loop(0, local_blocks, complete, 0)

    def settle(t, carry):
        finish((t + turn) % local_blocks)
        return carry

    lax.fori_loop(0, local_blocks - 1, settle, 0)
    last = (local_blocks - 1 + turn) % local_blocks
    send(last)
    finish(last)
    for sender in range(n):

        @pl.when(sender != me)
        def _():
            pltpu.make_async_remote_copy(
                src_ref=piece(0, 0), dst_ref=mine,
                send_sem=out_send.at[0], recv_sem=out_recv.at[sender],
                device_id=device("head", sender), device_id_type=MESH,
            ).wait_recv()


def finish_attention(
    far_index, queries, k_parts, v_blocks, far_parts, send_v, scale, axes, tok_rows, capacity
):
    local_blocks, _, width = v_blocks.shape
    heads_here = width // HD
    n = HEADS // heads_here
    m_ctx = send_v.shape[0] // capacity
    kernel = functools.partial(
        finish_kernel, axes=axes, heads_here=heads_here, scale=scale, capacity=capacity
    )
    anywhere = pl.BlockSpec(memory_space=pl.ANY)
    flops = local_blocks * heads_here * 3 * 4 * BLOCK * BLOCK * HD
    return pl.pallas_call(
        kernel,
        out_shape=jax.ShapeDtypeStruct((tok_rows, n * width), jnp.bfloat16),
        in_specs=[pl.BlockSpec(memory_space=pltpu.SMEM)] + [anywhere] * 7,
        out_specs=anywhere,
        scratch_shapes=[
            pltpu.VMEM(v_blocks.shape, jnp.bfloat16),
            pltpu.VMEM(v_blocks.shape, jnp.bfloat16),
            pltpu.VMEM(v_blocks.shape, jnp.bfloat16),
            pltpu.VMEM(send_v.shape, jnp.bfloat16),
            pltpu.VMEM(send_v.shape, jnp.bfloat16),
            pltpu.VMEM((local_blocks, heads_here * RSEL, BLOCK, BLOCK), jnp.bfloat16),
            pltpu.VMEM((local_blocks, BLOCK, width), jnp.float32),
            pltpu.VMEM((local_blocks, heads_here * 3, BLOCK, 1), jnp.float32),
            pltpu.VMEM((local_blocks, BLOCK, width), jnp.bfloat16),
            pltpu.SemaphoreType.DMA((6,)),
            pltpu.SemaphoreType.DMA((m_ctx,)),
            pltpu.SemaphoreType.DMA((m_ctx,)),
            pltpu.SemaphoreType.DMA((local_blocks * (BLOCK // tok_rows),)),
            pltpu.SemaphoreType.DMA((n,)),
            pltpu.SemaphoreType.DMA((n,)),
            pltpu.SemaphoreType.DMA((n,)),
        ],
        compiler_params=pltpu.CompilerParams(
            collective_id=2, has_side_effects=True, vmem_limit_bytes=60 * 1024 * 1024
        ),
        cost_estimate=pl.CostEstimate(
            flops=flops,
            transcendentals=local_blocks * heads_here * 3 * BLOCK * BLOCK,
            bytes_accessed=local_blocks * BLOCK * width * 2 * 8,
        ),
    )(far_index, queries, *k_parts, v_blocks, *far_parts, send_v)


def local(queries, keys, values, picks, axes):
    head_count = lax.axis_size("head")
    ctx_count = lax.axis_size("ctx")
    my_index = lax.axis_index("ctx")
    heads_here = HEADS // head_count
    width = heads_here * HD
    tok_rows = queries.shape[0]
    score_scale = 1.0 / math.sqrt(HD)
    head_in = ("head", 1, 0, None)
    ctx_move = ("ctx", 0, 0, None)
    (k_even,) = exchange((keys,), (("head", 1, 0, 0),), axes, collective_id=0)
    local_blocks = k_even.shape[0] * 2 // BLOCK
    half_rows = BLOCK // 2
    k_even = k_even.reshape(local_blocks, half_rows, width)

    capacity = (local_blocks * RSEL + ctx_count - 1) // ctx_count + 1
    owners, within, position = route_tables(picks, local_blocks, ctx_count)
    mine_owner = lax.dynamic_index_in_dim(owners, my_index, 0, keepdims=False)
    mine_pos = lax.dynamic_index_in_dim(position, my_index, 0, keepdims=False)
    slot_ids = jnp.arange(capacity, dtype=jnp.int32)
    asked = (owners == my_index)[:, :, None] & (position[:, :, None] == slot_ids[None, None, :])
    wanted = jnp.sum(asked.astype(jnp.int32) * within[:, :, None], axis=1)
    far_index = (mine_owner * capacity + mine_pos).astype(jnp.int32)

    pick = wanted.reshape(-1)
    far_even, k_odd, v_heads = exchange(
        (pick_rows(k_even, pick), keys, values), (ctx_move, ("head", 1, 0, 1), head_in), axes,
        collective_id=1,
    )
    k_odd = k_odd.reshape(local_blocks, half_rows, width)
    (far_odd,) = exchange((pick_rows(k_odd, pick),), (ctx_move,), axes, collective_id=3)
    v_blocks = v_heads.reshape(local_blocks, BLOCK, width)
    send_v = pick_rows(v_blocks, pick)
    return finish_attention(
        far_index, queries, (k_even, k_odd), v_blocks, (far_even, far_odd), send_v, score_scale,
        axes, tok_rows,
        capacity,
    )


def solution(mesh):
    placed = (P(("ctx", "head"), None), P(("ctx", "head"), None), P(("ctx", "head"), None), P())
    return jax.shard_map(
        functools.partial(local, axes=tuple(mesh.axis_names)), mesh=mesh, in_specs=placed, out_specs=P(("ctx", "head"), None), check_vma=False
    )
```

```python
import functools
import math

import jax
import jax.numpy as jnp
from jax import lax
from jax.experimental import pallas as pl
from jax.experimental.pallas import tpu as pltpu
from jax.sharding import PartitionSpec as P

MESH = pl.DeviceIdType.MESH

HEADS = 16
HD = 128
BLOCK = 512
RSEL = 2


def exchange_kernel(*refs, axes, jobs):
    count = len(jobs)
    srcs, dsts = refs[:count], refs[count:2 * count]
    send_sems, recv_sems = refs[2 * count], refs[2 * count + 1]

    def device(axis, peer):
        return tuple(peer if name == axis else lax.axis_index(name) for name in axes)

    barrier = pltpu.get_barrier_semaphore()
    peers = 0
    for axis in sorted({job[0] for job in jobs}):
        n = lax.axis_size(axis)
        me = lax.axis_index(axis)
        for k in range(1, n):
            pl.semaphore_signal(
                barrier, inc=1, device_id=device(axis, (me + k) % n), device_id_type=MESH
            )
        peers += n - 1
    pl.semaphore_wait(barrier, peers)

    def view(ref, dim, index, n):
        size = ref.shape[dim] // n
        where = [slice(None)] * len(ref.shape)
        where[dim] = pl.ds(index * size, size)
        return ref.at[tuple(where)]

    copies = []
    for a, (axis, split_axis, concat_axis) in enumerate(jobs):
        n = lax.axis_size(axis)
        me = lax.axis_index(axis)
        own = pltpu.make_async_copy(
            view(srcs[a], split_axis, me, n), view(dsts[a], concat_axis, me, n),
            send_sems.at[a, 0],
        )
        own.start()
        copies.append(own)
        for k in range(1, n):
            peer = (me + k) % n
            copy = pltpu.make_async_remote_copy(
                src_ref=view(srcs[a], split_axis, peer, n),
                dst_ref=view(dsts[a], concat_axis, me, n),
                send_sem=send_sems.at[a, k],
                recv_sem=recv_sems.at[a, k],
                device_id=device(axis, peer),
                device_id_type=MESH,
            )
            copy.start()
            copies.append(copy)
    for copy in copies:
        copy.wait()


def exchange(arrays, jobs, axes, collective_id):
    out_shapes = []
    for x, (axis, split_axis, concat_axis) in zip(arrays, jobs):
        n = lax.axis_size(axis)
        shape = list(x.shape)
        shape[split_axis] //= n
        shape[concat_axis] *= n
        out_shapes.append(jax.ShapeDtypeStruct(tuple(shape), x.dtype))
    widest = max(lax.axis_size(job[0]) for job in jobs)
    count = len(arrays)
    return pl.pallas_call(
        functools.partial(exchange_kernel, axes=axes, jobs=tuple(jobs)),
        out_shape=tuple(out_shapes),
        in_specs=[pl.BlockSpec(memory_space=pl.ANY)] * count,
        out_specs=tuple(pl.BlockSpec(memory_space=pl.ANY) for _ in range(count)),
        scratch_shapes=[
            pltpu.SemaphoreType.DMA((count, widest)),
            pltpu.SemaphoreType.DMA((count, widest)),
        ],
        compiler_params=pltpu.CompilerParams(collective_id=collective_id, has_side_effects=True),
    )(*arrays)


def route_tables(picks, local_blocks, ctx_count):
    slots = local_blocks * RSEL
    owners = (picks // local_blocks).reshape(ctx_count, slots)
    within = (picks % local_blocks).reshape(ctx_count, slots)
    owner_ids = jnp.arange(ctx_count, dtype=jnp.int32)
    one_hot = (owners[:, :, None] == owner_ids[None, None, :]).astype(jnp.int32)
    running = jnp.cumsum(one_hot, axis=1)
    position = jnp.sum(one_hot * running, axis=-1) - 1
    return (owners, within, position)


def slot_attention(q, k, v, scale):
    scores = lax.dot_general(
        q, k, (((1,), (1,)), ((), ())), preferred_element_type=jnp.float32
    ) * scale
    row_max = jnp.max(scores, axis=1, keepdims=True)
    exponent = jnp.exp(scores - row_max)
    row_sum = jnp.sum(exponent, axis=1, keepdims=True)
    partial = jnp.dot(
        exponent.astype(jnp.bfloat16), v, preferred_element_type=jnp.float32
    )
    return row_max, row_sum, partial


def finish_kernel(
    idx_ref, q_hbm, k_hbm, v_hbm, fk_hbm, sv_hbm, y_ref,
    qv, kv, vv, fkv, fvv, wts, base, fac, stage,
    load_sems, ctx_send, ctx_recv, out_send, out_recv, q_send, q_recv,
    *, axes, heads_here, scale, capacity,
):
    n = lax.axis_size("head")
    me = lax.axis_index("head")
    m_ctx = lax.axis_size("ctx")
    c_me = lax.axis_index("ctx")
    local_blocks = qv.shape[0]
    rows = y_ref.shape[0]
    width = heads_here * HD
    per_block = BLOCK // rows
    turn = me // per_block

    def device(axis, peer):
        return tuple(peer if name == axis else lax.axis_index(name) for name in axes)

    barrier = pltpu.get_barrier_semaphore()
    for k in range(1, m_ctx):
        pl.semaphore_signal(
            barrier, inc=1, device_id=device("ctx", (c_me + k) % m_ctx), device_id_type=MESH
        )
    for k in range(1, n):
        pl.semaphore_signal(
            barrier, inc=1, device_id=device("head", (me + k) % n), device_id_type=MESH
        )
    pl.semaphore_wait(barrier, m_ctx - 1 + n - 1)

    def rows_of(ref, index):
        return ref.at[pl.ds(index * capacity, capacity)]

    v_copies = [pltpu.make_async_copy(rows_of(sv_hbm, c_me), rows_of(fvv, c_me), ctx_send.at[0])]
    v_copies[0].start()
    for k in range(1, m_ctx):
        peer = (c_me + k) % m_ctx
        copy = pltpu.make_async_remote_copy(
            src_ref=rows_of(sv_hbm, peer), dst_ref=rows_of(fvv, c_me),
            send_sem=ctx_send.at[k], recv_sem=ctx_recv.at[k],
            device_id=device("ctx", peer), device_id_type=MESH,
        )
        copy.start()
        v_copies.append(copy)

    def q_rows(owner):
        return qv.at[owner // per_block, pl.ds((owner % per_block) * rows, rows), :]

    def q_cols(peer):
        return q_hbm.at[:, pl.ds(peer * width, width)]

    loads = [pltpu.make_async_copy(q_cols(me), q_rows(me), q_send.at[0])]
    loads[0].start()
    for k in range(1, n):
        peer = (me + k) % n
        copy = pltpu.make_async_remote_copy(
            src_ref=q_cols(peer), dst_ref=q_rows(me),
            send_sem=q_send.at[k], recv_sem=q_recv.at[k],
            device_id=device("head", peer), device_id_type=MESH,
        )
        copy.start()
        loads.append(copy)
    for a, (src, dst) in enumerate(((k_hbm, kv), (v_hbm, vv), (fk_hbm, fkv))):
        load = pltpu.make_async_copy(src, dst, load_sems.at[a])
        load.start()
        loads.append(load)
    for load in loads:
        load.wait()

    def prepare(i, carry):
        j0 = idx_ref[i * RSEL]
        j1 = idx_ref[i * RSEL + 1]
        for h in range(heads_here):
            cols = pl.ds(h * HD, HD)
            q = qv[i, :, cols]
            m0, l0, acc0 = slot_attention(q, kv[i, :, cols], vv[i, :, cols], scale)
            stats = []
            for slot, j in enumerate((j0, j1)):
                scores = lax.dot_general(
                    q, fkv[j, :, cols], (((1,), (1,)), ((), ())),
                    preferred_element_type=jnp.float32,
                ) * scale
                row_max = jnp.max(scores, axis=1, keepdims=True)
                exponent = jnp.exp(scores - row_max)
                stats.append((row_max, jnp.sum(exponent, axis=1, keepdims=True)))
                wts[i, h * RSEL + slot] = exponent.astype(jnp.bfloat16)
            top = jnp.maximum(jnp.maximum(m0, stats[0][0]), stats[1][0])
            f0 = jnp.exp(m0 - top)
            f1 = jnp.exp(stats[0][0] - top)
            f2 = jnp.exp(stats[1][0] - top)
            base[i, :, cols] = acc0 * f0
            fac[i, h * 3] = f1
            fac[i, h * 3 + 1] = f2
            fac[i, h * 3 + 2] = l0 * f0 + stats[0][1] * f1 + stats[1][1] * f2
        return carry

    lax.fori_loop(0, local_blocks, prepare, 0)
    for copy in v_copies:
        copy.wait()

    mine = y_ref.at[:, pl.ds(me * width, width)]

    def piece(b, r):
        return stage.at[b, pl.ds(r * rows, rows), :]

    def remote(b, r, dest):
        return pltpu.make_async_remote_copy(
            src_ref=piece(b, r), dst_ref=mine,
            send_sem=out_send.at[b * per_block + r], recv_sem=out_recv.at[me],
            device_id=device("head", dest), device_id_type=MESH,
        )

    def own(b, r):
        return pltpu.make_async_copy(piece(b, r), mine, out_send.at[b * per_block + r])

    def send(b):
        for r in range(per_block):
            dest = b * per_block + r

            @pl.when(dest == me)
            def _():
                own(b, r).start()

            @pl.when(dest != me)
            def _():
                remote(b, r, dest).start()

    def finish(b):
        for r in range(per_block):
            dest = b * per_block + r

            @pl.when(dest == me)
            def _():
                own(b, r).wait()

            @pl.when(dest != me)
            def _():
                remote(b, r, dest).wait_send()

    def complete(t, carry):
        i = (t + turn) % local_blocks
        j0 = idx_ref[i * RSEL]
        j1 = idx_ref[i * RSEL + 1]
        for h in range(heads_here):
            cols = pl.ds(h * HD, HD)
            p1 = jnp.dot(wts[i, h * RSEL], fvv[j0, :, cols], preferred_element_type=jnp.float32)
            p2 = jnp.dot(
                wts[i, h * RSEL + 1], fvv[j1, :, cols], preferred_element_type=jnp.float32
            )
            numer = base[i, :, cols] + p1 * fac[i, h * 3] + p2 * fac[i, h * 3 + 1]
            stage[i, :, cols] = (numer / fac[i, h * 3 + 2]).astype(stage.dtype)

        @pl.when(t >= 1)
        def _():
            send((t - 1 + turn) % local_blocks)

        return carry

    lax.fori_loop(0, local_blocks, complete, 0)

    def settle(t, carry):
        finish((t + turn) % local_blocks)
        return carry

    lax.fori_loop(0, local_blocks - 2, settle, 0)
    last = (local_blocks - 1 + turn) % local_blocks
    send(last)
    finish((local_blocks - 2 + turn) % local_blocks)
    finish(last)
    for sender in range(n):

        @pl.when(sender != me)
        def _():
            pltpu.make_async_remote_copy(
                src_ref=piece(0, 0), dst_ref=mine,
                send_sem=out_send.at[0], recv_sem=out_recv.at[sender],
                device_id=device("head", sender), device_id_type=MESH,
            ).wait_recv()


def finish_attention(
    far_index, queries, k_blocks, v_blocks, far_k, send_v, scale, axes, tok_rows, capacity
):
    local_blocks, _, width = k_blocks.shape
    heads_here = width // HD
    n = HEADS // heads_here
    m_ctx = send_v.shape[0] // capacity
    kernel = functools.partial(
        finish_kernel, axes=axes, heads_here=heads_here, scale=scale, capacity=capacity
    )
    anywhere = pl.BlockSpec(memory_space=pl.ANY)
    flops = local_blocks * heads_here * 3 * 4 * BLOCK * BLOCK * HD
    return pl.pallas_call(
        kernel,
        out_shape=jax.ShapeDtypeStruct((tok_rows, n * width), jnp.bfloat16),
        in_specs=[pl.BlockSpec(memory_space=pltpu.SMEM)] + [anywhere] * 5,
        out_specs=anywhere,
        scratch_shapes=[
            pltpu.VMEM(k_blocks.shape, jnp.bfloat16),
            pltpu.VMEM(k_blocks.shape, jnp.bfloat16),
            pltpu.VMEM(v_blocks.shape, jnp.bfloat16),
            pltpu.VMEM(far_k.shape, jnp.bfloat16),
            pltpu.VMEM(send_v.shape, jnp.bfloat16),
            pltpu.VMEM((local_blocks, heads_here * RSEL, BLOCK, BLOCK), jnp.bfloat16),
            pltpu.VMEM((local_blocks, BLOCK, width), jnp.float32),
            pltpu.VMEM((local_blocks, heads_here * 3, BLOCK, 1), jnp.float32),
            pltpu.VMEM((local_blocks, BLOCK, width), jnp.bfloat16),
            pltpu.SemaphoreType.DMA((4,)),
            pltpu.SemaphoreType.DMA((m_ctx,)),
            pltpu.SemaphoreType.DMA((m_ctx,)),
            pltpu.SemaphoreType.DMA((local_blocks * (BLOCK // tok_rows),)),
            pltpu.SemaphoreType.DMA((n,)),
            pltpu.SemaphoreType.DMA((n,)),
            pltpu.SemaphoreType.DMA((n,)),
        ],
        compiler_params=pltpu.CompilerParams(
            collective_id=2, has_side_effects=True, vmem_limit_bytes=60 * 1024 * 1024
        ),
        cost_estimate=pl.CostEstimate(
            flops=flops,
            transcendentals=local_blocks * heads_here * 3 * BLOCK * BLOCK,
            bytes_accessed=local_blocks * BLOCK * width * 2 * 8,
        ),
    )(far_index, queries, k_blocks, v_blocks, far_k, send_v)


def local(queries, keys, values, picks, axes):
    head_count = lax.axis_size("head")
    ctx_count = lax.axis_size("ctx")
    my_index = lax.axis_index("ctx")
    heads_here = HEADS // head_count
    width = heads_here * HD
    tok_rows = queries.shape[0]
    score_scale = 1.0 / math.sqrt(HD)
    head_in = ("head", 1, 0)
    ctx_move = ("ctx", 0, 0)
    (k_heads,) = exchange((keys,), (head_in,), axes, collective_id=0)
    local_blocks = k_heads.shape[0] // BLOCK
    k_blocks = k_heads.reshape(local_blocks, BLOCK, width)

    capacity = (local_blocks * RSEL + ctx_count - 1) // ctx_count + 1
    owners, within, position = route_tables(picks, local_blocks, ctx_count)
    mine_owner = lax.dynamic_index_in_dim(owners, my_index, 0, keepdims=False)
    mine_pos = lax.dynamic_index_in_dim(position, my_index, 0, keepdims=False)
    slot_ids = jnp.arange(capacity, dtype=jnp.int32)
    asked = (owners == my_index)[:, :, None] & (position[:, :, None] == slot_ids[None, None, :])
    wanted = jnp.sum(asked.astype(jnp.int32) * within[:, :, None], axis=1)
    far_index = (mine_owner * capacity + mine_pos).astype(jnp.int32)

    send_k = k_blocks[wanted.reshape(-1)]
    far_k, v_heads = exchange((send_k, values), (ctx_move, head_in), axes, collective_id=1)
    v_blocks = v_heads.reshape(local_blocks, BLOCK, width)
    send_v = v_blocks[wanted.reshape(-1)]
    return finish_attention(
        far_index, queries, k_blocks, v_blocks, far_k, send_v, score_scale, axes, tok_rows,
        capacity,
    )


def solution(mesh):
    placed = (P(("ctx", "head"), None), P(("ctx", "head"), None), P(("ctx", "head"), None), P())
    return jax.shard_map(
        functools.partial(local, axes=tuple(mesh.axis_names)), mesh=mesh, in_specs=placed, out_specs=P(("ctx", "head"), None), check_vma=False
    )
```

```python
import functools
import math

import jax
import jax.numpy as jnp
from jax import lax
from jax.experimental import pallas as pl
from jax.experimental.pallas import tpu as pltpu
from jax.sharding import PartitionSpec as P

MESH = pl.DeviceIdType.MESH

HEADS = 16
HD = 128
BLOCK = 512
RSEL = 2


def exchange_kernel(*refs, axes, jobs):
    count = len(jobs)
    srcs, dsts = refs[:count], refs[count:2 * count]
    send_sems, recv_sems = refs[2 * count], refs[2 * count + 1]

    def device(axis, peer):
        return tuple(peer if name == axis else lax.axis_index(name) for name in axes)

    barrier = pltpu.get_barrier_semaphore()
    peers = 0
    for axis in sorted({job[0] for job in jobs}):
        n = lax.axis_size(axis)
        me = lax.axis_index(axis)
        for k in range(1, n):
            pl.semaphore_signal(
                barrier, inc=1, device_id=device(axis, (me + k) % n), device_id_type=MESH
            )
        peers += n - 1
    pl.semaphore_wait(barrier, peers)

    def view(ref, dim, index, n):
        size = ref.shape[dim] // n
        where = [slice(None)] * len(ref.shape)
        where[dim] = pl.ds(index * size, size)
        return ref.at[tuple(where)]

    copies = []
    for a, (axis, split_axis, concat_axis) in enumerate(jobs):
        n = lax.axis_size(axis)
        me = lax.axis_index(axis)
        own = pltpu.make_async_copy(
            view(srcs[a], split_axis, me, n), view(dsts[a], concat_axis, me, n),
            send_sems.at[a, 0],
        )
        own.start()
        copies.append(own)
        for k in range(1, n):
            peer = (me + k) % n
            copy = pltpu.make_async_remote_copy(
                src_ref=view(srcs[a], split_axis, peer, n),
                dst_ref=view(dsts[a], concat_axis, me, n),
                send_sem=send_sems.at[a, k],
                recv_sem=recv_sems.at[a, k],
                device_id=device(axis, peer),
                device_id_type=MESH,
            )
            copy.start()
            copies.append(copy)
    for copy in copies:
        copy.wait()


def exchange(arrays, jobs, axes, collective_id):
    out_shapes = []
    for x, (axis, split_axis, concat_axis) in zip(arrays, jobs):
        n = lax.axis_size(axis)
        shape = list(x.shape)
        shape[split_axis] //= n
        shape[concat_axis] *= n
        out_shapes.append(jax.ShapeDtypeStruct(tuple(shape), x.dtype))
    widest = max(lax.axis_size(job[0]) for job in jobs)
    count = len(arrays)
    return pl.pallas_call(
        functools.partial(exchange_kernel, axes=axes, jobs=tuple(jobs)),
        out_shape=tuple(out_shapes),
        in_specs=[pl.BlockSpec(memory_space=pl.ANY)] * count,
        out_specs=tuple(pl.BlockSpec(memory_space=pl.ANY) for _ in range(count)),
        scratch_shapes=[
            pltpu.SemaphoreType.DMA((count, widest)),
            pltpu.SemaphoreType.DMA((count, widest)),
        ],
        compiler_params=pltpu.CompilerParams(collective_id=collective_id, has_side_effects=True),
    )(*arrays)


def route_tables(picks, local_blocks, ctx_count):
    slots = local_blocks * RSEL
    owners = (picks // local_blocks).reshape(ctx_count, slots)
    within = (picks % local_blocks).reshape(ctx_count, slots)
    owner_ids = jnp.arange(ctx_count, dtype=jnp.int32)
    one_hot = (owners[:, :, None] == owner_ids[None, None, :]).astype(jnp.int32)
    running = jnp.cumsum(one_hot, axis=1)
    position = jnp.sum(one_hot * running, axis=-1) - 1
    return (owners, within, position)


def slot_attention(q, k, v, scale):
    scores = lax.dot_general(
        q, k, (((1,), (1,)), ((), ())), preferred_element_type=jnp.float32
    ) * scale
    row_max = jnp.max(scores, axis=1, keepdims=True)
    exponent = jnp.exp(scores - row_max)
    row_sum = jnp.sum(exponent, axis=1, keepdims=True)
    partial = jnp.dot(
        exponent.astype(jnp.bfloat16), v, preferred_element_type=jnp.float32
    )
    return row_max, row_sum, partial


def finish_kernel(
    idx_ref, q_hbm, k_hbm, v_hbm, fk_hbm, sv_hbm, y_ref,
    qv, kv, vv, fkv, fvv, wts, base, fac, stage,
    load_sems, ctx_send, ctx_recv, out_send, out_recv, q_send, q_recv,
    *, axes, heads_here, scale, capacity,
):
    n = lax.axis_size("head")
    me = lax.axis_index("head")
    m_ctx = lax.axis_size("ctx")
    c_me = lax.axis_index("ctx")
    local_blocks = qv.shape[0]
    rows = y_ref.shape[0]
    width = heads_here * HD
    per_block = BLOCK // rows
    turn = me % local_blocks

    def device(axis, peer):
        return tuple(peer if name == axis else lax.axis_index(name) for name in axes)

    barrier = pltpu.get_barrier_semaphore()
    for k in range(1, m_ctx):
        pl.semaphore_signal(
            barrier, inc=1, device_id=device("ctx", (c_me + k) % m_ctx), device_id_type=MESH
        )
    for k in range(1, n):
        pl.semaphore_signal(
            barrier, inc=1, device_id=device("head", (me + k) % n), device_id_type=MESH
        )
    pl.semaphore_wait(barrier, m_ctx - 1 + n - 1)

    def rows_of(ref, index):
        return ref.at[pl.ds(index * capacity, capacity)]

    v_copies = [pltpu.make_async_copy(rows_of(sv_hbm, c_me), rows_of(fvv, c_me), ctx_send.at[0])]
    v_copies[0].start()
    for k in range(1, m_ctx):
        peer = (c_me + k) % m_ctx
        copy = pltpu.make_async_remote_copy(
            src_ref=rows_of(sv_hbm, peer), dst_ref=rows_of(fvv, c_me),
            send_sem=ctx_send.at[k], recv_sem=ctx_recv.at[k],
            device_id=device("ctx", peer), device_id_type=MESH,
        )
        copy.start()
        v_copies.append(copy)

    def q_rows(owner):
        return qv.at[owner // per_block, pl.ds((owner % per_block) * rows, rows), :]

    def q_cols(peer):
        return q_hbm.at[:, pl.ds(peer * width, width)]

    loads = [pltpu.make_async_copy(q_cols(me), q_rows(me), q_send.at[0])]
    loads[0].start()
    for k in range(1, n):
        peer = (me + k) % n
        copy = pltpu.make_async_remote_copy(
            src_ref=q_cols(peer), dst_ref=q_rows(me),
            send_sem=q_send.at[k], recv_sem=q_recv.at[k],
            device_id=device("head", peer), device_id_type=MESH,
        )
        copy.start()
        loads.append(copy)
    for a, (src, dst) in enumerate(((k_hbm, kv), (v_hbm, vv), (fk_hbm, fkv))):
        load = pltpu.make_async_copy(src, dst, load_sems.at[a])
        load.start()
        loads.append(load)
    for load in loads:
        load.wait()

    def prepare(i, carry):
        j0 = idx_ref[i * RSEL]
        j1 = idx_ref[i * RSEL + 1]
        for h in range(heads_here):
            cols = pl.ds(h * HD, HD)
            q = qv[i, :, cols]
            m0, l0, acc0 = slot_attention(q, kv[i, :, cols], vv[i, :, cols], scale)
            stats = []
            for slot, j in enumerate((j0, j1)):
                scores = lax.dot_general(
                    q, fkv[j, :, cols], (((1,), (1,)), ((), ())),
                    preferred_element_type=jnp.float32,
                ) * scale
                row_max = jnp.max(scores, axis=1, keepdims=True)
                exponent = jnp.exp(scores - row_max)
                stats.append((row_max, jnp.sum(exponent, axis=1, keepdims=True)))
                wts[i, h * RSEL + slot] = exponent.astype(jnp.bfloat16)
            top = jnp.maximum(jnp.maximum(m0, stats[0][0]), stats[1][0])
            f0 = jnp.exp(m0 - top)
            f1 = jnp.exp(stats[0][0] - top)
            f2 = jnp.exp(stats[1][0] - top)
            base[i, :, cols] = acc0 * f0
            fac[i, h * 3] = f1
            fac[i, h * 3 + 1] = f2
            fac[i, h * 3 + 2] = l0 * f0 + stats[0][1] * f1 + stats[1][1] * f2
        return carry

    lax.fori_loop(0, local_blocks, prepare, 0)
    for copy in v_copies:
        copy.wait()

    mine = y_ref.at[:, pl.ds(me * width, width)]

    def piece(b, r):
        return stage.at[b, pl.ds(r * rows, rows), :]

    def remote(b, r, dest):
        return pltpu.make_async_remote_copy(
            src_ref=piece(b, r), dst_ref=mine,
            send_sem=out_send.at[b * per_block + r], recv_sem=out_recv.at[me],
            device_id=device("head", dest), device_id_type=MESH,
        )

    def own(b, r):
        return pltpu.make_async_copy(piece(b, r), mine, out_send.at[b * per_block + r])

    def send(b):
        for r in range(per_block):
            dest = b * per_block + r

            @pl.when(dest == me)
            def _():
                own(b, r).start()

            @pl.when(dest != me)
            def _():
                remote(b, r, dest).start()

    def finish(b):
        for r in range(per_block):
            dest = b * per_block + r

            @pl.when(dest == me)
            def _():
                own(b, r).wait()

            @pl.when(dest != me)
            def _():
                remote(b, r, dest).wait_send()

    def complete(t, carry):
        i = (t + turn) % local_blocks
        j0 = idx_ref[i * RSEL]
        j1 = idx_ref[i * RSEL + 1]
        for h in range(heads_here):
            cols = pl.ds(h * HD, HD)
            p1 = jnp.dot(wts[i, h * RSEL], fvv[j0, :, cols], preferred_element_type=jnp.float32)
            p2 = jnp.dot(
                wts[i, h * RSEL + 1], fvv[j1, :, cols], preferred_element_type=jnp.float32
            )
            numer = base[i, :, cols] + p1 * fac[i, h * 3] + p2 * fac[i, h * 3 + 1]
            stage[i, :, cols] = (numer / fac[i, h * 3 + 2]).astype(stage.dtype)

        @pl.when(t >= 1)
        def _():
            send((t - 1 + turn) % local_blocks)

        return carry

    lax.fori_loop(0, local_blocks, complete, 0)

    def settle(t, carry):
        finish((t + turn) % local_blocks)
        return carry

    lax.fori_loop(0, local_blocks - 1, settle, 0)
    last = (local_blocks - 1 + turn) % local_blocks
    send(last)
    finish(last)
    for sender in range(n):

        @pl.when(sender != me)
        def _():
            pltpu.make_async_remote_copy(
                src_ref=piece(0, 0), dst_ref=mine,
                send_sem=out_send.at[0], recv_sem=out_recv.at[sender],
                device_id=device("head", sender), device_id_type=MESH,
            ).wait_recv()


def finish_attention(
    far_index, queries, k_blocks, v_blocks, far_k, send_v, scale, axes, tok_rows, capacity
):
    local_blocks, _, width = k_blocks.shape
    heads_here = width // HD
    n = HEADS // heads_here
    m_ctx = send_v.shape[0] // capacity
    kernel = functools.partial(
        finish_kernel, axes=axes, heads_here=heads_here, scale=scale, capacity=capacity
    )
    anywhere = pl.BlockSpec(memory_space=pl.ANY)
    flops = local_blocks * heads_here * 3 * 4 * BLOCK * BLOCK * HD
    return pl.pallas_call(
        kernel,
        out_shape=jax.ShapeDtypeStruct((tok_rows, n * width), jnp.bfloat16),
        in_specs=[pl.BlockSpec(memory_space=pltpu.SMEM)] + [anywhere] * 5,
        out_specs=anywhere,
        scratch_shapes=[
            pltpu.VMEM(k_blocks.shape, jnp.bfloat16),
            pltpu.VMEM(k_blocks.shape, jnp.bfloat16),
            pltpu.VMEM(v_blocks.shape, jnp.bfloat16),
            pltpu.VMEM(far_k.shape, jnp.bfloat16),
            pltpu.VMEM(send_v.shape, jnp.bfloat16),
            pltpu.VMEM((local_blocks, heads_here * RSEL, BLOCK, BLOCK), jnp.bfloat16),
            pltpu.VMEM((local_blocks, BLOCK, width), jnp.float32),
            pltpu.VMEM((local_blocks, heads_here * 3, BLOCK, 1), jnp.float32),
            pltpu.VMEM((local_blocks, BLOCK, width), jnp.bfloat16),
            pltpu.SemaphoreType.DMA((4,)),
            pltpu.SemaphoreType.DMA((m_ctx,)),
            pltpu.SemaphoreType.DMA((m_ctx,)),
            pltpu.SemaphoreType.DMA((local_blocks * (BLOCK // tok_rows),)),
            pltpu.SemaphoreType.DMA((n,)),
            pltpu.SemaphoreType.DMA((n,)),
            pltpu.SemaphoreType.DMA((n,)),
        ],
        compiler_params=pltpu.CompilerParams(
            collective_id=2, has_side_effects=True, vmem_limit_bytes=60 * 1024 * 1024
        ),
        cost_estimate=pl.CostEstimate(
            flops=flops,
            transcendentals=local_blocks * heads_here * 3 * BLOCK * BLOCK,
            bytes_accessed=local_blocks * BLOCK * width * 2 * 8,
        ),
    )(far_index, queries, k_blocks, v_blocks, far_k, send_v)


def local(queries, keys, values, picks, axes):
    head_count = lax.axis_size("head")
    ctx_count = lax.axis_size("ctx")
    my_index = lax.axis_index("ctx")
    heads_here = HEADS // head_count
    width = heads_here * HD
    tok_rows = queries.shape[0]
    score_scale = 1.0 / math.sqrt(HD)
    head_in = ("head", 1, 0)
    ctx_move = ("ctx", 0, 0)
    (k_heads,) = exchange((keys,), (head_in,), axes, collective_id=0)
    local_blocks = k_heads.shape[0] // BLOCK
    k_blocks = k_heads.reshape(local_blocks, BLOCK, width)

    capacity = (local_blocks * RSEL + ctx_count - 1) // ctx_count + 1
    owners, within, position = route_tables(picks, local_blocks, ctx_count)
    mine_owner = lax.dynamic_index_in_dim(owners, my_index, 0, keepdims=False)
    mine_pos = lax.dynamic_index_in_dim(position, my_index, 0, keepdims=False)
    slot_ids = jnp.arange(capacity, dtype=jnp.int32)
    asked = (owners == my_index)[:, :, None] & (position[:, :, None] == slot_ids[None, None, :])
    wanted = jnp.sum(asked.astype(jnp.int32) * within[:, :, None], axis=1)
    far_index = (mine_owner * capacity + mine_pos).astype(jnp.int32)

    send_k = k_blocks[wanted.reshape(-1)]
    far_k, v_heads = exchange((send_k, values), (ctx_move, head_in), axes, collective_id=1)
    v_blocks = v_heads.reshape(local_blocks, BLOCK, width)
    send_v = v_blocks[wanted.reshape(-1)]
    return finish_attention(
        far_index, queries, k_blocks, v_blocks, far_k, send_v, score_scale, axes, tok_rows,
        capacity,
    )


def solution(mesh):
    placed = (P(("ctx", "head"), None), P(("ctx", "head"), None), P(("ctx", "head"), None), P())
    return jax.shard_map(
        functools.partial(local, axes=tuple(mesh.axis_names)), mesh=mesh, in_specs=placed, out_specs=P(("ctx", "head"), None), check_vma=False
    )
```

```python
import functools
import math

import jax
import jax.numpy as jnp
from jax import lax
from jax.experimental import pallas as pl
from jax.experimental.pallas import tpu as pltpu
from jax.sharding import PartitionSpec as P

MESH = pl.DeviceIdType.MESH

HEADS = 16
HD = 128
BLOCK = 512
RSEL = 2


def exchange_kernel(*refs, axes, jobs):
    count = len(jobs)
    srcs, dsts = refs[:count], refs[count:2 * count]
    send_sems, recv_sems = refs[2 * count], refs[2 * count + 1]

    def device(axis, peer):
        return tuple(peer if name == axis else lax.axis_index(name) for name in axes)

    barrier = pltpu.get_barrier_semaphore()
    peers = 0
    for axis in sorted({job[0] for job in jobs}):
        n = lax.axis_size(axis)
        me = lax.axis_index(axis)
        for k in range(1, n):
            pl.semaphore_signal(
                barrier, inc=1, device_id=device(axis, (me + k) % n), device_id_type=MESH
            )
        peers += n - 1
    pl.semaphore_wait(barrier, peers)

    def view(ref, dim, index, n):
        size = ref.shape[dim] // n
        where = [slice(None)] * len(ref.shape)
        where[dim] = pl.ds(index * size, size)
        return ref.at[tuple(where)]

    copies = []
    halves = []
    for a, (axis, split_axis, concat_axis, parity) in enumerate(jobs):
        n = lax.axis_size(axis)
        me = lax.axis_index(axis)
        if parity is None:
            own = pltpu.make_async_copy(
                view(srcs[a], split_axis, me, n), view(dsts[a], concat_axis, me, n),
                send_sems.at[a, 0],
            )
            own.start()
            copies.append(own)
            for k in range(1, n):
                peer = (me + k) % n
                copy = pltpu.make_async_remote_copy(
                    src_ref=view(srcs[a], split_axis, peer, n),
                    dst_ref=view(dsts[a], concat_axis, me, n),
                    send_sem=send_sems.at[a, k],
                    recv_sem=recv_sems.at[a, k],
                    device_id=device(axis, peer),
                    device_id_type=MESH,
                )
                copy.start()
                copies.append(copy)
            continue
        half = n // 2
        slot = me // 2

        def own_half(a=a, n=n, me=me, slot=slot, half=half, split_axis=split_axis,
                     concat_axis=concat_axis):
            return pltpu.make_async_copy(
                view(srcs[a], split_axis, me, n), view(dsts[a], concat_axis, slot, half),
                send_sems.at[a, 0],
            )

        def out_half(k, a=a, n=n, me=me, slot=slot, half=half, axis=axis,
                     split_axis=split_axis, concat_axis=concat_axis):
            peer = (me + k) % n
            return pltpu.make_async_remote_copy(
                src_ref=view(srcs[a], split_axis, peer, n),
                dst_ref=view(dsts[a], concat_axis, slot, half),
                send_sem=send_sems.at[a, k],
                recv_sem=recv_sems.at[a, slot],
                device_id=device(axis, peer),
                device_id_type=MESH,
            )

        @pl.when(me % 2 == parity)
        def _():
            own_half().start()
            for k in range(1, n):
                out_half(k).start()

        halves.append((me, n, parity, own_half, out_half, a))
    for copy in copies:
        copy.wait()
    for me, n, parity, own_half, out_half, a in halves:

        @pl.when(me % 2 == parity)
        def _():
            own_half().wait()
            for k in range(1, n):
                out_half(k).wait_send()

        for j in range(n // 2):
            sender = 2 * j + parity

            @pl.when(sender != me)
            def _():
                pltpu.make_async_remote_copy(
                    src_ref=view(srcs[a], jobs[a][1], 0, n),
                    dst_ref=view(dsts[a], jobs[a][2], j, n // 2),
                    send_sem=send_sems.at[a, 0],
                    recv_sem=recv_sems.at[a, j],
                    device_id=device(jobs[a][0], sender),
                    device_id_type=MESH,
                ).wait_recv()


def exchange(arrays, jobs, axes, collective_id):
    out_shapes = []
    for x, (axis, split_axis, concat_axis, parity) in zip(arrays, jobs):
        n = lax.axis_size(axis)
        shape = list(x.shape)
        shape[split_axis] //= n
        shape[concat_axis] *= n if parity is None else n // 2
        out_shapes.append(jax.ShapeDtypeStruct(tuple(shape), x.dtype))
    widest = max(lax.axis_size(job[0]) for job in jobs)
    count = len(arrays)
    return pl.pallas_call(
        functools.partial(exchange_kernel, axes=axes, jobs=tuple(jobs)),
        out_shape=tuple(out_shapes),
        in_specs=[pl.BlockSpec(memory_space=pl.ANY)] * count,
        out_specs=tuple(pl.BlockSpec(memory_space=pl.ANY) for _ in range(count)),
        scratch_shapes=[
            pltpu.SemaphoreType.DMA((count, widest)),
            pltpu.SemaphoreType.DMA((count, widest)),
        ],
        compiler_params=pltpu.CompilerParams(collective_id=collective_id, has_side_effects=True),
    )(*arrays)


def route_tables(picks, local_blocks, ctx_count):
    slots = local_blocks * RSEL
    owners = (picks // local_blocks).reshape(ctx_count, slots)
    within = (picks % local_blocks).reshape(ctx_count, slots)
    owner_ids = jnp.arange(ctx_count, dtype=jnp.int32)
    one_hot = (owners[:, :, None] == owner_ids[None, None, :]).astype(jnp.int32)
    running = jnp.cumsum(one_hot, axis=1)
    position = jnp.sum(one_hot * running, axis=-1) - 1
    return (owners, within, position)


def slot_attention(q, k, v, scale):
    scores = lax.dot_general(
        q, k, (((1,), (1,)), ((), ())), preferred_element_type=jnp.float32
    ) * scale
    row_max = jnp.max(scores, axis=1, keepdims=True)
    exponent = jnp.exp(scores - row_max)
    row_sum = jnp.sum(exponent, axis=1, keepdims=True)
    partial = jnp.dot(
        exponent.astype(jnp.bfloat16), v, preferred_element_type=jnp.float32
    )
    return row_max, row_sum, partial


def finish_kernel(
    idx_ref, q_hbm, ka_hbm, kb_hbm, v_hbm, fka_hbm, fkb_hbm, sv_hbm, y_ref,
    qv, kv, vv, fkv, fvv, wts, base, fac, stage,
    load_sems, ctx_send, ctx_recv, out_send, out_recv, q_send, q_recv,
    *, axes, heads_here, scale, capacity,
):
    n = lax.axis_size("head")
    me = lax.axis_index("head")
    m_ctx = lax.axis_size("ctx")
    c_me = lax.axis_index("ctx")
    local_blocks = qv.shape[0]
    rows = y_ref.shape[0]
    width = heads_here * HD
    per_block = BLOCK // rows
    turn = me % local_blocks

    def device(axis, peer):
        return tuple(peer if name == axis else lax.axis_index(name) for name in axes)

    barrier = pltpu.get_barrier_semaphore()
    for k in range(1, m_ctx):
        pl.semaphore_signal(
            barrier, inc=1, device_id=device("ctx", (c_me + k) % m_ctx), device_id_type=MESH
        )
    for k in range(1, n):
        pl.semaphore_signal(
            barrier, inc=1, device_id=device("head", (me + k) % n), device_id_type=MESH
        )
    pl.semaphore_wait(barrier, m_ctx - 1 + n - 1)

    def rows_of(ref, index):
        return ref.at[pl.ds(index * capacity, capacity)]

    v_copies = [pltpu.make_async_copy(rows_of(sv_hbm, c_me), rows_of(fvv, c_me), ctx_send.at[0])]
    v_copies[0].start()
    for k in range(1, m_ctx):
        peer = (c_me + k) % m_ctx
        copy = pltpu.make_async_remote_copy(
            src_ref=rows_of(sv_hbm, peer), dst_ref=rows_of(fvv, c_me),
            send_sem=ctx_send.at[k], recv_sem=ctx_recv.at[k],
            device_id=device("ctx", peer), device_id_type=MESH,
        )
        copy.start()
        v_copies.append(copy)

    def q_rows(owner):
        return qv.at[owner // per_block, pl.ds((owner % per_block) * rows, rows), :]

    def q_cols(peer):
        return q_hbm.at[:, pl.ds(peer * width, width)]

    loads = [pltpu.make_async_copy(q_cols(me), q_rows(me), q_send.at[0])]
    loads[0].start()
    for k in range(1, n):
        peer = (me + k) % n
        copy = pltpu.make_async_remote_copy(
            src_ref=q_cols(peer), dst_ref=q_rows(me),
            send_sem=q_send.at[k], recv_sem=q_recv.at[k],
            device_id=device("head", peer), device_id_type=MESH,
        )
        copy.start()
        loads.append(copy)
    top_rows = pl.ds(0, BLOCK // 2)
    low_rows = pl.ds(BLOCK // 2, BLOCK // 2)
    pairs = (
        (ka_hbm, kv.at[:, top_rows, :]), (kb_hbm, kv.at[:, low_rows, :]), (v_hbm, vv),
        (fka_hbm, fkv.at[:, top_rows, :]), (fkb_hbm, fkv.at[:, low_rows, :]),
    )
    for a, (src, dst) in enumerate(pairs):
        load = pltpu.make_async_copy(src, dst, load_sems.at[a])
        load.start()
        loads.append(load)
    for load in loads:
        load.wait()

    def prepare(i, carry):
        j0 = idx_ref[i * RSEL]
        j1 = idx_ref[i * RSEL + 1]
        for h in range(heads_here):
            cols = pl.ds(h * HD, HD)
            q = qv[i, :, cols]
            m0, l0, acc0 = slot_attention(q, kv[i, :, cols], vv[i, :, cols], scale)
            stats = []
            for slot, j in enumerate((j0, j1)):
                scores = lax.dot_general(
                    q, fkv[j, :, cols], (((1,), (1,)), ((), ())),
                    preferred_element_type=jnp.float32,
                ) * scale
                row_max = jnp.max(scores, axis=1, keepdims=True)
                exponent = jnp.exp(scores - row_max)
                stats.append((row_max, jnp.sum(exponent, axis=1, keepdims=True)))
                wts[i, h * RSEL + slot] = exponent.astype(jnp.bfloat16)
            top = jnp.maximum(jnp.maximum(m0, stats[0][0]), stats[1][0])
            f0 = jnp.exp(m0 - top)
            f1 = jnp.exp(stats[0][0] - top)
            f2 = jnp.exp(stats[1][0] - top)
            base[i, :, cols] = acc0 * f0
            fac[i, h * 3] = f1
            fac[i, h * 3 + 1] = f2
            fac[i, h * 3 + 2] = l0 * f0 + stats[0][1] * f1 + stats[1][1] * f2
        return carry

    lax.fori_loop(0, local_blocks, prepare, 0)
    for copy in v_copies:
        copy.wait()

    mine = y_ref.at[:, pl.ds(me * width, width)]

    def piece(b, r):
        return stage.at[b, pl.ds(r * rows, rows), :]

    def remote(b, r, dest):
        return pltpu.make_async_remote_copy(
            src_ref=piece(b, r), dst_ref=mine,
            send_sem=out_send.at[b * per_block + r], recv_sem=out_recv.at[me],
            device_id=device("head", dest), device_id_type=MESH,
        )

    def own(b, r):
        return pltpu.make_async_copy(piece(b, r), mine, out_send.at[b * per_block + r])

    def send(b):
        for r in range(per_block):
            dest = b * per_block + r

            @pl.when(dest == me)
            def _():
                own(b, r).start()

            @pl.when(dest != me)
            def _():
                remote(b, r, dest).start()

    def finish(b):
        for r in range(per_block):
            dest = b * per_block + r

            @pl.when(dest == me)
            def _():
                own(b, r).wait()

            @pl.when(dest != me)
            def _():
                remote(b, r, dest).wait_send()

    def complete(t, carry):
        i = (t + turn) % local_blocks
        j0 = idx_ref[i * RSEL]
        j1 = idx_ref[i * RSEL + 1]
        for h in range(heads_here):
            cols = pl.ds(h * HD, HD)
            p1 = jnp.dot(wts[i, h * RSEL], fvv[j0, :, cols], preferred_element_type=jnp.float32)
            p2 = jnp.dot(
                wts[i, h * RSEL + 1], fvv[j1, :, cols], preferred_element_type=jnp.float32
            )
            numer = base[i, :, cols] + p1 * fac[i, h * 3] + p2 * fac[i, h * 3 + 1]
            stage[i, :, cols] = (numer / fac[i, h * 3 + 2]).astype(stage.dtype)

        @pl.when(t >= 1)
        def _():
            send((t - 1 + turn) % local_blocks)

        return carry

    lax.fori_loop(0, local_blocks, complete, 0)

    def settle(t, carry):
        finish((t + turn) % local_blocks)
        return carry

    lax.fori_loop(0, local_blocks - 2, settle, 0)
    last = (local_blocks - 1 + turn) % local_blocks
    send(last)
    finish((local_blocks - 2 + turn) % local_blocks)
    finish(last)
    for sender in range(n):

        @pl.when(sender != me)
        def _():
            pltpu.make_async_remote_copy(
                src_ref=piece(0, 0), dst_ref=mine,
                send_sem=out_send.at[0], recv_sem=out_recv.at[sender],
                device_id=device("head", sender), device_id_type=MESH,
            ).wait_recv()


def finish_attention(
    far_index, queries, k_parts, v_blocks, far_parts, send_v, scale, axes, tok_rows, capacity
):
    local_blocks, _, width = v_blocks.shape
    heads_here = width // HD
    n = HEADS // heads_here
    m_ctx = send_v.shape[0] // capacity
    kernel = functools.partial(
        finish_kernel, axes=axes, heads_here=heads_here, scale=scale, capacity=capacity
    )
    anywhere = pl.BlockSpec(memory_space=pl.ANY)
    flops = local_blocks * heads_here * 3 * 4 * BLOCK * BLOCK * HD
    return pl.pallas_call(
        kernel,
        out_shape=jax.ShapeDtypeStruct((tok_rows, n * width), jnp.bfloat16),
        in_specs=[pl.BlockSpec(memory_space=pltpu.SMEM)] + [anywhere] * 7,
        out_specs=anywhere,
        scratch_shapes=[
            pltpu.VMEM(v_blocks.shape, jnp.bfloat16),
            pltpu.VMEM(v_blocks.shape, jnp.bfloat16),
            pltpu.VMEM(v_blocks.shape, jnp.bfloat16),
            pltpu.VMEM(send_v.shape, jnp.bfloat16),
            pltpu.VMEM(send_v.shape, jnp.bfloat16),
            pltpu.VMEM((local_blocks, heads_here * RSEL, BLOCK, BLOCK), jnp.bfloat16),
            pltpu.VMEM((local_blocks, BLOCK, width), jnp.float32),
            pltpu.VMEM((local_blocks, heads_here * 3, BLOCK, 1), jnp.float32),
            pltpu.VMEM((local_blocks, BLOCK, width), jnp.bfloat16),
            pltpu.SemaphoreType.DMA((6,)),
            pltpu.SemaphoreType.DMA((m_ctx,)),
            pltpu.SemaphoreType.DMA((m_ctx,)),
            pltpu.SemaphoreType.DMA((local_blocks * (BLOCK // tok_rows),)),
            pltpu.SemaphoreType.DMA((n,)),
            pltpu.SemaphoreType.DMA((n,)),
            pltpu.SemaphoreType.DMA((n,)),
        ],
        compiler_params=pltpu.CompilerParams(
            collective_id=2, has_side_effects=True, vmem_limit_bytes=60 * 1024 * 1024
        ),
        cost_estimate=pl.CostEstimate(
            flops=flops,
            transcendentals=local_blocks * heads_here * 3 * BLOCK * BLOCK,
            bytes_accessed=local_blocks * BLOCK * width * 2 * 8,
        ),
    )(far_index, queries, *k_parts, v_blocks, *far_parts, send_v)


def local(queries, keys, values, picks, axes):
    head_count = lax.axis_size("head")
    ctx_count = lax.axis_size("ctx")
    my_index = lax.axis_index("ctx")
    heads_here = HEADS // head_count
    width = heads_here * HD
    tok_rows = queries.shape[0]
    score_scale = 1.0 / math.sqrt(HD)
    head_in = ("head", 1, 0, None)
    ctx_move = ("ctx", 0, 0, None)
    (k_even,) = exchange((keys,), (("head", 1, 0, 0),), axes, collective_id=0)
    local_blocks = k_even.shape[0] * 2 // BLOCK
    half_rows = BLOCK // 2
    k_even = k_even.reshape(local_blocks, half_rows, width)

    capacity = (local_blocks * RSEL + ctx_count - 1) // ctx_count + 1
    owners, within, position = route_tables(picks, local_blocks, ctx_count)
    mine_owner = lax.dynamic_index_in_dim(owners, my_index, 0, keepdims=False)
    mine_pos = lax.dynamic_index_in_dim(position, my_index, 0, keepdims=False)
    slot_ids = jnp.arange(capacity, dtype=jnp.int32)
    asked = (owners == my_index)[:, :, None] & (position[:, :, None] == slot_ids[None, None, :])
    wanted = jnp.sum(asked.astype(jnp.int32) * within[:, :, None], axis=1)
    far_index = (mine_owner * capacity + mine_pos).astype(jnp.int32)

    pick = wanted.reshape(-1)
    far_even, k_odd, v_heads = exchange(
        (k_even[pick], keys, values), (ctx_move, ("head", 1, 0, 1), head_in), axes,
        collective_id=1,
    )
    k_odd = k_odd.reshape(local_blocks, half_rows, width)
    (far_odd,) = exchange((k_odd[pick],), (ctx_move,), axes, collective_id=3)
    v_blocks = v_heads.reshape(local_blocks, BLOCK, width)
    send_v = v_blocks[pick]
    return finish_attention(
        far_index, queries, (k_even, k_odd), v_blocks, (far_even, far_odd), send_v, score_scale,
        axes, tok_rows,
        capacity,
    )


def solution(mesh):
    placed = (P(("ctx", "head"), None), P(("ctx", "head"), None), P(("ctx", "head"), None), P())
    return jax.shard_map(
        functools.partial(local, axes=tuple(mesh.axis_names)), mesh=mesh, in_specs=placed, out_specs=P(("ctx", "head"), None), check_vma=False
    )
```

```python
import functools
import math

import jax
import jax.numpy as jnp
from jax import lax
from jax.experimental import pallas as pl
from jax.experimental.pallas import tpu as pltpu
from jax.sharding import PartitionSpec as P

MESH = pl.DeviceIdType.MESH

HEADS = 16
HD = 128
BLOCK = 512
RSEL = 2


def exchange_kernel(*refs, axes, jobs):
    count = len(jobs)
    srcs, dsts = refs[:count], refs[count:2 * count]
    send_sems, recv_sems = refs[2 * count], refs[2 * count + 1]

    def device(axis, peer):
        return tuple(peer if name == axis else lax.axis_index(name) for name in axes)

    barrier = pltpu.get_barrier_semaphore()
    peers = 0
    for axis in sorted({job[0] for job in jobs}):
        n = lax.axis_size(axis)
        me = lax.axis_index(axis)
        for k in range(1, n):
            pl.semaphore_signal(
                barrier, inc=1, device_id=device(axis, (me + k) % n), device_id_type=MESH
            )
        peers += n - 1
    pl.semaphore_wait(barrier, peers)

    def view(ref, dim, index, n):
        size = ref.shape[dim] // n
        where = [slice(None)] * len(ref.shape)
        where[dim] = pl.ds(index * size, size)
        return ref.at[tuple(where)]

    copies = []
    halves = []
    for a, (axis, split_axis, concat_axis, parity) in enumerate(jobs):
        n = lax.axis_size(axis)
        me = lax.axis_index(axis)
        if parity is None:
            own = pltpu.make_async_copy(
                view(srcs[a], split_axis, me, n), view(dsts[a], concat_axis, me, n),
                send_sems.at[a, 0],
            )
            own.start()
            copies.append(own)
            for k in range(1, n):
                peer = (me + k) % n
                copy = pltpu.make_async_remote_copy(
                    src_ref=view(srcs[a], split_axis, peer, n),
                    dst_ref=view(dsts[a], concat_axis, me, n),
                    send_sem=send_sems.at[a, k],
                    recv_sem=recv_sems.at[a, k],
                    device_id=device(axis, peer),
                    device_id_type=MESH,
                )
                copy.start()
                copies.append(copy)
            continue
        half = n // 2
        slot = me // 2

        def own_half(a=a, n=n, me=me, slot=slot, half=half, split_axis=split_axis,
                     concat_axis=concat_axis):
            return pltpu.make_async_copy(
                view(srcs[a], split_axis, me, n), view(dsts[a], concat_axis, slot, half),
                send_sems.at[a, 0],
            )

        def out_half(k, a=a, n=n, me=me, slot=slot, half=half, axis=axis,
                     split_axis=split_axis, concat_axis=concat_axis):
            peer = (me + k) % n
            return pltpu.make_async_remote_copy(
                src_ref=view(srcs[a], split_axis, peer, n),
                dst_ref=view(dsts[a], concat_axis, slot, half),
                send_sem=send_sems.at[a, k],
                recv_sem=recv_sems.at[a, slot],
                device_id=device(axis, peer),
                device_id_type=MESH,
            )

        @pl.when(me % 2 == parity)
        def _():
            own_half().start()
            for k in range(1, n):
                out_half(k).start()

        halves.append((me, n, parity, own_half, out_half, a))
    for copy in copies:
        copy.wait()
    for me, n, parity, own_half, out_half, a in halves:

        @pl.when(me % 2 == parity)
        def _():
            own_half().wait()
            for k in range(1, n):
                out_half(k).wait_send()

        for j in range(n // 2):
            sender = 2 * j + parity

            @pl.when(sender != me)
            def _():
                pltpu.make_async_remote_copy(
                    src_ref=view(srcs[a], jobs[a][1], 0, n),
                    dst_ref=view(dsts[a], jobs[a][2], j, n // 2),
                    send_sem=send_sems.at[a, 0],
                    recv_sem=recv_sems.at[a, j],
                    device_id=device(jobs[a][0], sender),
                    device_id_type=MESH,
                ).wait_recv()


def exchange(arrays, jobs, axes, collective_id):
    out_shapes = []
    for x, (axis, split_axis, concat_axis, parity) in zip(arrays, jobs):
        n = lax.axis_size(axis)
        shape = list(x.shape)
        shape[split_axis] //= n
        shape[concat_axis] *= n if parity is None else n // 2
        out_shapes.append(jax.ShapeDtypeStruct(tuple(shape), x.dtype))
    widest = max(lax.axis_size(job[0]) for job in jobs)
    count = len(arrays)
    return pl.pallas_call(
        functools.partial(exchange_kernel, axes=axes, jobs=tuple(jobs)),
        out_shape=tuple(out_shapes),
        in_specs=[pl.BlockSpec(memory_space=pl.ANY)] * count,
        out_specs=tuple(pl.BlockSpec(memory_space=pl.ANY) for _ in range(count)),
        scratch_shapes=[
            pltpu.SemaphoreType.DMA((count, widest)),
            pltpu.SemaphoreType.DMA((count, widest)),
        ],
        compiler_params=pltpu.CompilerParams(collective_id=collective_id, has_side_effects=True),
    )(*arrays)


def route_tables(picks, local_blocks, ctx_count):
    slots = local_blocks * RSEL
    owners = (picks // local_blocks).reshape(ctx_count, slots)
    within = (picks % local_blocks).reshape(ctx_count, slots)
    owner_ids = jnp.arange(ctx_count, dtype=jnp.int32)
    one_hot = (owners[:, :, None] == owner_ids[None, None, :]).astype(jnp.int32)
    running = jnp.cumsum(one_hot, axis=1)
    position = jnp.sum(one_hot * running, axis=-1) - 1
    return (owners, within, position)


def slot_attention(q, k, v, scale):
    scores = lax.dot_general(
        q, k, (((1,), (1,)), ((), ())), preferred_element_type=jnp.float32
    ) * scale
    row_max = jnp.max(scores, axis=1, keepdims=True)
    exponent = jnp.exp(scores - row_max)
    row_sum = jnp.sum(exponent, axis=1, keepdims=True)
    partial = jnp.dot(
        exponent.astype(jnp.bfloat16), v, preferred_element_type=jnp.float32
    )
    return row_max, row_sum, partial


def finish_kernel(
    idx_ref, q_hbm, ka_hbm, kb_hbm, v_hbm, fka_hbm, fkb_hbm, sv_hbm, y_ref,
    qv, kv, vv, fkv, fvv, wts, base, fac, stage,
    load_sems, ctx_send, ctx_recv, out_send, out_recv, q_send, q_recv,
    *, axes, heads_here, scale, capacity,
):
    n = lax.axis_size("head")
    me = lax.axis_index("head")
    m_ctx = lax.axis_size("ctx")
    c_me = lax.axis_index("ctx")
    local_blocks = qv.shape[0]
    rows = y_ref.shape[0]
    width = heads_here * HD
    per_block = BLOCK // rows
    turn = me % local_blocks

    def device(axis, peer):
        return tuple(peer if name == axis else lax.axis_index(name) for name in axes)

    barrier = pltpu.get_barrier_semaphore()
    for k in range(1, m_ctx):
        pl.semaphore_signal(
            barrier, inc=1, device_id=device("ctx", (c_me + k) % m_ctx), device_id_type=MESH
        )
    for k in range(1, n):
        pl.semaphore_signal(
            barrier, inc=1, device_id=device("head", (me + k) % n), device_id_type=MESH
        )
    pl.semaphore_wait(barrier, m_ctx - 1 + n - 1)

    def rows_of(ref, index):
        return ref.at[pl.ds(index * capacity, capacity)]

    v_copies = [pltpu.make_async_copy(rows_of(sv_hbm, c_me), rows_of(fvv, c_me), ctx_send.at[0])]
    v_copies[0].start()
    for k in range(1, m_ctx):
        peer = (c_me + k) % m_ctx
        copy = pltpu.make_async_remote_copy(
            src_ref=rows_of(sv_hbm, peer), dst_ref=rows_of(fvv, c_me),
            send_sem=ctx_send.at[k], recv_sem=ctx_recv.at[k],
            device_id=device("ctx", peer), device_id_type=MESH,
        )
        copy.start()
        v_copies.append(copy)

    def q_rows(owner):
        return qv.at[owner // per_block, pl.ds((owner % per_block) * rows, rows), :]

    def q_cols(peer):
        return q_hbm.at[:, pl.ds(peer * width, width)]

    loads = [pltpu.make_async_copy(q_hbm, qv, q_send.at[0])]
    loads[0].start()
    top_rows = pl.ds(0, BLOCK // 2)
    low_rows = pl.ds(BLOCK // 2, BLOCK // 2)
    pairs = (
        (ka_hbm, kv.at[:, top_rows, :]), (kb_hbm, kv.at[:, low_rows, :]), (v_hbm, vv),
        (fka_hbm, fkv.at[:, top_rows, :]), (fkb_hbm, fkv.at[:, low_rows, :]),
    )
    for a, (src, dst) in enumerate(pairs):
        load = pltpu.make_async_copy(src, dst, load_sems.at[a])
        load.start()
        loads.append(load)
    for load in loads:
        load.wait()

    def prepare(i, carry):
        j0 = idx_ref[i * RSEL]
        j1 = idx_ref[i * RSEL + 1]
        for h in range(heads_here):
            cols = pl.ds(h * HD, HD)
            q = qv[i, :, cols]
            m0, l0, acc0 = slot_attention(q, kv[i, :, cols], vv[i, :, cols], scale)
            stats = []
            for slot, j in enumerate((j0, j1)):
                scores = lax.dot_general(
                    q, fkv[j, :, cols], (((1,), (1,)), ((), ())),
                    preferred_element_type=jnp.float32,
                ) * scale
                row_max = jnp.max(scores, axis=1, keepdims=True)
                exponent = jnp.exp(scores - row_max)
                stats.append((row_max, jnp.sum(exponent, axis=1, keepdims=True)))
                wts[i, h * RSEL + slot] = exponent.astype(jnp.bfloat16)
            top = jnp.maximum(jnp.maximum(m0, stats[0][0]), stats[1][0])
            f0 = jnp.exp(m0 - top)
            f1 = jnp.exp(stats[0][0] - top)
            f2 = jnp.exp(stats[1][0] - top)
            base[i, :, cols] = acc0 * f0
            fac[i, h * 3] = f1
            fac[i, h * 3 + 1] = f2
            fac[i, h * 3 + 2] = l0 * f0 + stats[0][1] * f1 + stats[1][1] * f2
        return carry

    lax.fori_loop(0, local_blocks, prepare, 0)
    for copy in v_copies:
        copy.wait()

    mine = y_ref.at[:, pl.ds(me * width, width)]

    def piece(b, r):
        return stage.at[b, pl.ds(r * rows, rows), :]

    def remote(b, r, dest):
        return pltpu.make_async_remote_copy(
            src_ref=piece(b, r), dst_ref=mine,
            send_sem=out_send.at[b * per_block + r], recv_sem=out_recv.at[me],
            device_id=device("head", dest), device_id_type=MESH,
        )

    def own(b, r):
        return pltpu.make_async_copy(piece(b, r), mine, out_send.at[b * per_block + r])

    def send(b):
        for r in range(per_block):
            dest = b * per_block + r

            @pl.when(dest == me)
            def _():
                own(b, r).start()

            @pl.when(dest != me)
            def _():
                remote(b, r, dest).start()

    def finish(b):
        for r in range(per_block):
            dest = b * per_block + r

            @pl.when(dest == me)
            def _():
                own(b, r).wait()

            @pl.when(dest != me)
            def _():
                remote(b, r, dest).wait_send()

    def complete(t, carry):
        i = (t + turn) % local_blocks
        j0 = idx_ref[i * RSEL]
        j1 = idx_ref[i * RSEL + 1]
        for h in range(heads_here):
            cols = pl.ds(h * HD, HD)
            p1 = jnp.dot(wts[i, h * RSEL], fvv[j0, :, cols], preferred_element_type=jnp.float32)
            p2 = jnp.dot(
                wts[i, h * RSEL + 1], fvv[j1, :, cols], preferred_element_type=jnp.float32
            )
            numer = base[i, :, cols] + p1 * fac[i, h * 3] + p2 * fac[i, h * 3 + 1]
            stage[i, :, cols] = (numer / fac[i, h * 3 + 2]).astype(stage.dtype)

        @pl.when(t >= 1)
        def _():
            send((t - 1 + turn) % local_blocks)

        return carry

    lax.fori_loop(0, local_blocks, complete, 0)

    def settle(t, carry):
        finish((t + turn) % local_blocks)
        return carry

    lax.fori_loop(0, local_blocks - 2, settle, 0)
    last = (local_blocks - 1 + turn) % local_blocks
    send(last)
    finish((local_blocks - 2 + turn) % local_blocks)
    finish(last)
    for sender in range(n):

        @pl.when(sender != me)
        def _():
            pltpu.make_async_remote_copy(
                src_ref=piece(0, 0), dst_ref=mine,
                send_sem=out_send.at[0], recv_sem=out_recv.at[sender],
                device_id=device("head", sender), device_id_type=MESH,
            ).wait_recv()


def finish_attention(
    far_index, queries, k_parts, v_blocks, far_parts, send_v, scale, axes, tok_rows, capacity
):
    local_blocks, _, width = v_blocks.shape
    heads_here = width // HD
    n = HEADS // heads_here
    m_ctx = send_v.shape[0] // capacity
    kernel = functools.partial(
        finish_kernel, axes=axes, heads_here=heads_here, scale=scale, capacity=capacity
    )
    anywhere = pl.BlockSpec(memory_space=pl.ANY)
    flops = local_blocks * heads_here * 3 * 4 * BLOCK * BLOCK * HD
    return pl.pallas_call(
        kernel,
        out_shape=jax.ShapeDtypeStruct((tok_rows, n * width), jnp.bfloat16),
        in_specs=[pl.BlockSpec(memory_space=pltpu.SMEM)] + [anywhere] * 7,
        out_specs=anywhere,
        scratch_shapes=[
            pltpu.VMEM(v_blocks.shape, jnp.bfloat16),
            pltpu.VMEM(v_blocks.shape, jnp.bfloat16),
            pltpu.VMEM(v_blocks.shape, jnp.bfloat16),
            pltpu.VMEM(send_v.shape, jnp.bfloat16),
            pltpu.VMEM(send_v.shape, jnp.bfloat16),
            pltpu.VMEM((local_blocks, heads_here * RSEL, BLOCK, BLOCK), jnp.bfloat16),
            pltpu.VMEM((local_blocks, BLOCK, width), jnp.float32),
            pltpu.VMEM((local_blocks, heads_here * 3, BLOCK, 1), jnp.float32),
            pltpu.VMEM((local_blocks, BLOCK, width), jnp.bfloat16),
            pltpu.SemaphoreType.DMA((6,)),
            pltpu.SemaphoreType.DMA((m_ctx,)),
            pltpu.SemaphoreType.DMA((m_ctx,)),
            pltpu.SemaphoreType.DMA((local_blocks * (BLOCK // tok_rows),)),
            pltpu.SemaphoreType.DMA((n,)),
            pltpu.SemaphoreType.DMA((n,)),
            pltpu.SemaphoreType.DMA((n,)),
        ],
        compiler_params=pltpu.CompilerParams(
            collective_id=2, has_side_effects=True, vmem_limit_bytes=60 * 1024 * 1024
        ),
        cost_estimate=pl.CostEstimate(
            flops=flops,
            transcendentals=local_blocks * heads_here * 3 * BLOCK * BLOCK,
            bytes_accessed=local_blocks * BLOCK * width * 2 * 8,
        ),
    )(far_index, queries, *k_parts, v_blocks, *far_parts, send_v)


def local(queries, keys, values, picks, axes):
    head_count = lax.axis_size("head")
    ctx_count = lax.axis_size("ctx")
    my_index = lax.axis_index("ctx")
    heads_here = HEADS // head_count
    width = heads_here * HD
    tok_rows = queries.shape[0]
    score_scale = 1.0 / math.sqrt(HD)
    head_in = ("head", 1, 0, None)
    ctx_move = ("ctx", 0, 0, None)
    (k_even,) = exchange((keys,), (("head", 1, 0, 0),), axes, collective_id=0)
    local_blocks = k_even.shape[0] * 2 // BLOCK
    half_rows = BLOCK // 2
    k_even = k_even.reshape(local_blocks, half_rows, width)

    capacity = (local_blocks * RSEL + ctx_count - 1) // ctx_count + 1
    owners, within, position = route_tables(picks, local_blocks, ctx_count)
    mine_owner = lax.dynamic_index_in_dim(owners, my_index, 0, keepdims=False)
    mine_pos = lax.dynamic_index_in_dim(position, my_index, 0, keepdims=False)
    slot_ids = jnp.arange(capacity, dtype=jnp.int32)
    asked = (owners == my_index)[:, :, None] & (position[:, :, None] == slot_ids[None, None, :])
    wanted = jnp.sum(asked.astype(jnp.int32) * within[:, :, None], axis=1)
    far_index = (mine_owner * capacity + mine_pos).astype(jnp.int32)

    pick = wanted.reshape(-1)
    far_even, k_odd, v_heads = exchange(
        (k_even[pick], keys, values), (ctx_move, ("head", 1, 0, 1), head_in), axes,
        collective_id=1,
    )
    k_odd = k_odd.reshape(local_blocks, half_rows, width)
    far_odd, q_heads = exchange(
        (k_odd[pick], queries), (ctx_move, head_in), axes, collective_id=3
    )
    q_blocks = q_heads.reshape(local_blocks, BLOCK, width)
    v_blocks = v_heads.reshape(local_blocks, BLOCK, width)
    send_v = v_blocks[pick]
    return finish_attention(
        far_index, q_blocks, (k_even, k_odd), v_blocks, (far_even, far_odd), send_v, score_scale,
        axes, tok_rows,
        capacity,
    )


def solution(mesh):
    placed = (P(("ctx", "head"), None), P(("ctx", "head"), None), P(("ctx", "head"), None), P())
    return jax.shard_map(
        functools.partial(local, axes=tuple(mesh.axis_names)), mesh=mesh, in_specs=placed, out_specs=P(("ctx", "head"), None), check_vma=False
    )
```

```python
import functools
import math

import jax
import jax.numpy as jnp
from jax import lax
from jax.experimental import pallas as pl
from jax.experimental.pallas import tpu as pltpu
from jax.sharding import PartitionSpec as P

MESH = pl.DeviceIdType.MESH

HEADS = 16
HD = 128
BLOCK = 512
RSEL = 2


def exchange_kernel(*refs, axes, jobs):
    count = len(jobs)
    srcs, dsts = refs[:count], refs[count:2 * count]
    send_sems, recv_sems = refs[2 * count], refs[2 * count + 1]

    def device(axis, peer):
        return tuple(peer if name == axis else lax.axis_index(name) for name in axes)

    barrier = pltpu.get_barrier_semaphore()
    peers = 0
    for axis in sorted({job[0] for job in jobs}):
        n = lax.axis_size(axis)
        me = lax.axis_index(axis)
        for k in range(1, n):
            pl.semaphore_signal(
                barrier, inc=1, device_id=device(axis, (me + k) % n), device_id_type=MESH
            )
        peers += n - 1
    pl.semaphore_wait(barrier, peers)

    def view(ref, dim, index, n):
        size = ref.shape[dim] // n
        where = [slice(None)] * len(ref.shape)
        where[dim] = pl.ds(index * size, size)
        return ref.at[tuple(where)]

    copies = []
    halves = []
    for a, (axis, split_axis, concat_axis, parity) in enumerate(jobs):
        n = lax.axis_size(axis)
        me = lax.axis_index(axis)
        if parity is None:
            own = pltpu.make_async_copy(
                view(srcs[a], split_axis, me, n), view(dsts[a], concat_axis, me, n),
                send_sems.at[a, 0],
            )
            own.start()
            copies.append(own)
            for k in range(1, n):
                peer = (me + k) % n
                copy = pltpu.make_async_remote_copy(
                    src_ref=view(srcs[a], split_axis, peer, n),
                    dst_ref=view(dsts[a], concat_axis, me, n),
                    send_sem=send_sems.at[a, k],
                    recv_sem=recv_sems.at[a, k],
                    device_id=device(axis, peer),
                    device_id_type=MESH,
                )
                copy.start()
                copies.append(copy)
            continue
        half = n // 2
        slot = me // 2

        def own_half(a=a, n=n, me=me, slot=slot, half=half, split_axis=split_axis,
                     concat_axis=concat_axis):
            return pltpu.make_async_copy(
                view(srcs[a], split_axis, me, n), view(dsts[a], concat_axis, slot, half),
                send_sems.at[a, 0],
            )

        def out_half(k, a=a, n=n, me=me, slot=slot, half=half, axis=axis,
                     split_axis=split_axis, concat_axis=concat_axis):
            peer = (me + k) % n
            return pltpu.make_async_remote_copy(
                src_ref=view(srcs[a], split_axis, peer, n),
                dst_ref=view(dsts[a], concat_axis, slot, half),
                send_sem=send_sems.at[a, k],
                recv_sem=recv_sems.at[a, slot],
                device_id=device(axis, peer),
                device_id_type=MESH,
            )

        @pl.when(me % 2 == parity)
        def _():
            own_half().start()
            for k in range(1, n):
                out_half(k).start()

        halves.append((me, n, parity, own_half, out_half, a))
    for copy in copies:
        copy.wait()
    for me, n, parity, own_half, out_half, a in halves:

        @pl.when(me % 2 == parity)
        def _():
            own_half().wait()
            for k in range(1, n):
                out_half(k).wait_send()

        for j in range(n // 2):
            sender = 2 * j + parity

            @pl.when(sender != me)
            def _():
                pltpu.make_async_remote_copy(
                    src_ref=view(srcs[a], jobs[a][1], 0, n),
                    dst_ref=view(dsts[a], jobs[a][2], j, n // 2),
                    send_sem=send_sems.at[a, 0],
                    recv_sem=recv_sems.at[a, j],
                    device_id=device(jobs[a][0], sender),
                    device_id_type=MESH,
                ).wait_recv()


def exchange(arrays, jobs, axes, collective_id):
    out_shapes = []
    for x, (axis, split_axis, concat_axis, parity) in zip(arrays, jobs):
        n = lax.axis_size(axis)
        shape = list(x.shape)
        shape[split_axis] //= n
        shape[concat_axis] *= n if parity is None else n // 2
        out_shapes.append(jax.ShapeDtypeStruct(tuple(shape), x.dtype))
    widest = max(lax.axis_size(job[0]) for job in jobs)
    count = len(arrays)
    return pl.pallas_call(
        functools.partial(exchange_kernel, axes=axes, jobs=tuple(jobs)),
        out_shape=tuple(out_shapes),
        in_specs=[pl.BlockSpec(memory_space=pl.ANY)] * count,
        out_specs=tuple(pl.BlockSpec(memory_space=pl.ANY) for _ in range(count)),
        scratch_shapes=[
            pltpu.SemaphoreType.DMA((count, widest)),
            pltpu.SemaphoreType.DMA((count, widest)),
        ],
        compiler_params=pltpu.CompilerParams(collective_id=collective_id, has_side_effects=True),
    )(*arrays)


def route_tables(picks, local_blocks, ctx_count):
    slots = local_blocks * RSEL
    owners = (picks // local_blocks).reshape(ctx_count, slots)
    within = (picks % local_blocks).reshape(ctx_count, slots)
    owner_ids = jnp.arange(ctx_count, dtype=jnp.int32)
    one_hot = (owners[:, :, None] == owner_ids[None, None, :]).astype(jnp.int32)
    running = jnp.cumsum(one_hot, axis=1)
    position = jnp.sum(one_hot * running, axis=-1) - 1
    return (owners, within, position)


def slot_attention(q, k, v, scale):
    scores = lax.dot_general(
        q, k, (((1,), (1,)), ((), ())), preferred_element_type=jnp.float32
    ) * scale
    row_max = jnp.max(scores, axis=1, keepdims=True)
    exponent = jnp.exp(scores - row_max)
    row_sum = jnp.sum(exponent, axis=1, keepdims=True)
    partial = jnp.dot(
        exponent.astype(jnp.bfloat16), v, preferred_element_type=jnp.float32
    )
    return row_max, row_sum, partial


def finish_kernel(
    idx_ref, q_hbm, ka_hbm, kb_hbm, v_hbm, fka_hbm, fkb_hbm, sv_hbm, y_ref,
    qv, kv, vv, fkv, fvv, wts, base, fac, stage,
    load_sems, ctx_send, ctx_recv, out_send, out_recv, q_send, q_recv,
    *, axes, heads_here, scale, capacity,
):
    n = lax.axis_size("head")
    me = lax.axis_index("head")
    m_ctx = lax.axis_size("ctx")
    c_me = lax.axis_index("ctx")
    local_blocks = qv.shape[0]
    rows = y_ref.shape[0]
    width = heads_here * HD
    per_block = BLOCK // rows
    turn = me % local_blocks

    def device(axis, peer):
        return tuple(peer if name == axis else lax.axis_index(name) for name in axes)

    barrier = pltpu.get_barrier_semaphore()
    for k in range(1, m_ctx):
        pl.semaphore_signal(
            barrier, inc=1, device_id=device("ctx", (c_me + k) % m_ctx), device_id_type=MESH
        )
    for k in range(1, n):
        pl.semaphore_signal(
            barrier, inc=1, device_id=device("head", (me + k) % n), device_id_type=MESH
        )
    pl.semaphore_wait(barrier, m_ctx - 1 + n - 1)

    def rows_of(ref, index):
        return ref.at[pl.ds(index * capacity, capacity)]

    v_copies = [pltpu.make_async_copy(rows_of(sv_hbm, c_me), rows_of(fvv, c_me), ctx_send.at[0])]
    v_copies[0].start()
    for k in range(1, m_ctx):
        peer = (c_me + k) % m_ctx
        copy = pltpu.make_async_remote_copy(
            src_ref=rows_of(sv_hbm, peer), dst_ref=rows_of(fvv, c_me),
            send_sem=ctx_send.at[k], recv_sem=ctx_recv.at[k],
            device_id=device("ctx", peer), device_id_type=MESH,
        )
        copy.start()
        v_copies.append(copy)

    def q_rows(owner):
        return qv.at[owner // per_block, pl.ds((owner % per_block) * rows, rows), :]

    def q_cols(peer):
        return q_hbm.at[:, pl.ds(peer * width, width)]

    loads = [pltpu.make_async_copy(q_cols(me), q_rows(me), q_send.at[0])]
    loads[0].start()
    for k in range(1, n):
        peer = (me + k) % n
        copy = pltpu.make_async_remote_copy(
            src_ref=q_cols(peer), dst_ref=q_rows(me),
            send_sem=q_send.at[k], recv_sem=q_recv.at[k],
            device_id=device("head", peer), device_id_type=MESH,
        )
        copy.start()
        loads.append(copy)
    top_rows = pl.ds(0, BLOCK // 2)
    low_rows = pl.ds(BLOCK // 2, BLOCK // 2)
    pairs = (
        (ka_hbm, kv.at[:, top_rows, :]), (kb_hbm, kv.at[:, low_rows, :]), (v_hbm, vv),
        (fka_hbm, fkv.at[:, top_rows, :]), (fkb_hbm, fkv.at[:, low_rows, :]),
    )
    for a, (src, dst) in enumerate(pairs):
        load = pltpu.make_async_copy(src, dst, load_sems.at[a])
        load.start()
        loads.append(load)
    for load in loads:
        load.wait()

    def prepare(i, carry):
        j0 = idx_ref[i * RSEL]
        j1 = idx_ref[i * RSEL + 1]
        for h in range(heads_here):
            cols = pl.ds(h * HD, HD)
            q = qv[i, :, cols]
            m0, l0, acc0 = slot_attention(q, kv[i, :, cols], vv[i, :, cols], scale)
            stats = []
            for slot, j in enumerate((j0, j1)):
                scores = lax.dot_general(
                    q, fkv[j, :, cols], (((1,), (1,)), ((), ())),
                    preferred_element_type=jnp.float32,
                ) * scale
                row_max = jnp.max(scores, axis=1, keepdims=True)
                exponent = jnp.exp(scores - row_max)
                stats.append((row_max, jnp.sum(exponent, axis=1, keepdims=True)))
                wts[i, h * RSEL + slot] = exponent.astype(jnp.bfloat16)
            top = jnp.maximum(jnp.maximum(m0, stats[0][0]), stats[1][0])
            f0 = jnp.exp(m0 - top)
            f1 = jnp.exp(stats[0][0] - top)
            f2 = jnp.exp(stats[1][0] - top)
            base[i, :, cols] = acc0 * f0
            fac[i, h * 3] = f1
            fac[i, h * 3 + 1] = f2
            fac[i, h * 3 + 2] = l0 * f0 + stats[0][1] * f1 + stats[1][1] * f2
        return carry

    lax.fori_loop(0, local_blocks, prepare, 0)
    for copy in v_copies:
        copy.wait()

    mine = y_ref.at[:, pl.ds(me * width, width)]

    def piece(b, r):
        return stage.at[b, pl.ds(r * rows, rows), :]

    def remote(b, r, dest):
        return pltpu.make_async_remote_copy(
            src_ref=piece(b, r), dst_ref=mine,
            send_sem=out_send.at[b * per_block + r], recv_sem=out_recv.at[me],
            device_id=device("head", dest), device_id_type=MESH,
        )

    def own(b, r):
        return pltpu.make_async_copy(piece(b, r), mine, out_send.at[b * per_block + r])

    def send(b):
        for r in range(per_block):
            dest = b * per_block + r

            @pl.when(dest == me)
            def _():
                own(b, r).start()

            @pl.when(dest != me)
            def _():
                remote(b, r, dest).start()

    def finish(b):
        for r in range(per_block):
            dest = b * per_block + r

            @pl.when(dest == me)
            def _():
                own(b, r).wait()

            @pl.when(dest != me)
            def _():
                remote(b, r, dest).wait_send()

    def complete(t, carry):
        i = (t + turn) % local_blocks
        j0 = idx_ref[i * RSEL]
        j1 = idx_ref[i * RSEL + 1]
        for h in range(heads_here):
            cols = pl.ds(h * HD, HD)
            p1 = jnp.dot(wts[i, h * RSEL], fvv[j0, :, cols], preferred_element_type=jnp.float32)
            p2 = jnp.dot(
                wts[i, h * RSEL + 1], fvv[j1, :, cols], preferred_element_type=jnp.float32
            )
            numer = base[i, :, cols] + p1 * fac[i, h * 3] + p2 * fac[i, h * 3 + 1]
            stage[i, :, cols] = (numer / fac[i, h * 3 + 2]).astype(stage.dtype)

        @pl.when(t >= 1)
        def _():
            send((t - 1 + turn) % local_blocks)

        return carry

    lax.fori_loop(0, local_blocks, complete, 0)

    def settle(t, carry):
        finish((t + turn) % local_blocks)
        return carry

    lax.fori_loop(0, local_blocks - 2, settle, 0)
    last = (local_blocks - 1 + turn) % local_blocks
    send(last)
    finish((local_blocks - 2 + turn) % local_blocks)
    finish(last)
    for sender in range(n):

        @pl.when(sender != me)
        def _():
            pltpu.make_async_remote_copy(
                src_ref=piece(0, 0), dst_ref=mine,
                send_sem=out_send.at[0], recv_sem=out_recv.at[sender],
                device_id=device("head", sender), device_id_type=MESH,
            ).wait_recv()


def finish_attention(
    far_index, queries, k_parts, v_blocks, far_parts, send_v, scale, axes, tok_rows, capacity
):
    local_blocks, _, width = v_blocks.shape
    heads_here = width // HD
    n = HEADS // heads_here
    m_ctx = send_v.shape[0] // capacity
    kernel = functools.partial(
        finish_kernel, axes=axes, heads_here=heads_here, scale=scale, capacity=capacity
    )
    anywhere = pl.BlockSpec(memory_space=pl.ANY)
    flops = local_blocks * heads_here * 3 * 4 * BLOCK * BLOCK * HD
    return pl.pallas_call(
        kernel,
        out_shape=jax.ShapeDtypeStruct((tok_rows, n * width), jnp.bfloat16),
        in_specs=[pl.BlockSpec(memory_space=pltpu.SMEM)] + [anywhere] * 7,
        out_specs=anywhere,
        scratch_shapes=[
            pltpu.VMEM(v_blocks.shape, jnp.bfloat16),
            pltpu.VMEM(v_blocks.shape, jnp.bfloat16),
            pltpu.VMEM(v_blocks.shape, jnp.bfloat16),
            pltpu.VMEM(send_v.shape, jnp.bfloat16),
            pltpu.VMEM(send_v.shape, jnp.bfloat16),
            pltpu.VMEM((local_blocks, heads_here * RSEL, BLOCK, BLOCK), jnp.bfloat16),
            pltpu.VMEM((local_blocks, BLOCK, width), jnp.float32),
            pltpu.VMEM((local_blocks, heads_here * 3, BLOCK, 1), jnp.float32),
            pltpu.VMEM((local_blocks, BLOCK, width), jnp.bfloat16),
            pltpu.SemaphoreType.DMA((6,)),
            pltpu.SemaphoreType.DMA((m_ctx,)),
            pltpu.SemaphoreType.DMA((m_ctx,)),
            pltpu.SemaphoreType.DMA((local_blocks * (BLOCK // tok_rows),)),
            pltpu.SemaphoreType.DMA((n,)),
            pltpu.SemaphoreType.DMA((n,)),
            pltpu.SemaphoreType.DMA((n,)),
        ],
        compiler_params=pltpu.CompilerParams(
            collective_id=2, has_side_effects=True, vmem_limit_bytes=60 * 1024 * 1024
        ),
        cost_estimate=pl.CostEstimate(
            flops=flops,
            transcendentals=local_blocks * heads_here * 3 * BLOCK * BLOCK,
            bytes_accessed=local_blocks * BLOCK * width * 2 * 8,
        ),
    )(far_index, queries, *k_parts, v_blocks, *far_parts, send_v)


def local(queries, keys, values, picks, axes):
    head_count = lax.axis_size("head")
    ctx_count = lax.axis_size("ctx")
    my_index = lax.axis_index("ctx")
    heads_here = HEADS // head_count
    width = heads_here * HD
    tok_rows = queries.shape[0]
    score_scale = 1.0 / math.sqrt(HD)
    head_in = ("head", 1, 0, None)
    ctx_move = ("ctx", 0, 0, None)
    (k_even,) = exchange((keys,), (("head", 1, 0, 0),), axes, collective_id=0)
    local_blocks = k_even.shape[0] * 2 // BLOCK
    half_rows = BLOCK // 2
    k_even = k_even.reshape(local_blocks, half_rows, width)

    capacity = (local_blocks * RSEL + ctx_count - 1) // ctx_count + 1
    owners, within, position = route_tables(picks, local_blocks, ctx_count)
    mine_owner = lax.dynamic_index_in_dim(owners, my_index, 0, keepdims=False)
    mine_pos = lax.dynamic_index_in_dim(position, my_index, 0, keepdims=False)
    slot_ids = jnp.arange(capacity, dtype=jnp.int32)
    asked = (owners == my_index)[:, :, None] & (position[:, :, None] == slot_ids[None, None, :])
    wanted = jnp.sum(asked.astype(jnp.int32) * within[:, :, None], axis=1)
    far_index = (mine_owner * capacity + mine_pos).astype(jnp.int32)

    pick = wanted.reshape(-1)
    far_even, k_odd = exchange(
        (k_even[pick], keys), (ctx_move, ("head", 1, 0, 1)), axes, collective_id=1
    )
    k_odd = k_odd.reshape(local_blocks, half_rows, width)
    far_odd, v_heads = exchange(
        (k_odd[pick], values), (ctx_move, head_in), axes, collective_id=3
    )
    v_blocks = v_heads.reshape(local_blocks, BLOCK, width)
    send_v = v_blocks[pick]
    return finish_attention(
        far_index, queries, (k_even, k_odd), v_blocks, (far_even, far_odd), send_v, score_scale,
        axes, tok_rows,
        capacity,
    )


def solution(mesh):
    placed = (P(("ctx", "head"), None), P(("ctx", "head"), None), P(("ctx", "head"), None), P())
    return jax.shard_map(
        functools.partial(local, axes=tuple(mesh.axis_names)), mesh=mesh, in_specs=placed, out_specs=P(("ctx", "head"), None), check_vma=False
    )
```
